32 devices in a mesh: slab: 2 (over x), tile: 16 (over z, y, core).
Axes of the slice: x: 2, y: 2, z: 4, core: 2. Of those that a mesh axis runs over, the one named last changes fastest.
Arguments:
- mask: float32 [16384, 512], P(('slab', 'tile')), parts along dimension 0, may hold values from -1 to 1
- target: float32 [16384, 512], P(('slab', 'tile')), parts along dimension 0, may hold values from 0 to 1
- partner: int32 [2048], P(('slab', 'tile')), parts along dimension 0, may hold values from 0 to 1023, as said below
- kernels: float32 [1, 6, 2, 32, 32], replicated, may hold values from -6 to 6
- socs_weights: float32 [6], replicated, may hold values from 0.2 to 1
- dose: float32 [1], replicated, may hold values from 0.6 to 1.6
Outputs:
- gradient: float32 [16384, 512], P(('slab', 'tile')), parts along dimension 0
- updated: float32 [16384, 512], P(('slab', 'tile')), parts along dimension 0
The draws below stay inside these ranges and needn't reach their ends.
There are 2 independent parts, one for each index of `slab`. The reference program is written for one: setup_inputs(seed, part) draws one part's arguments, and reference() takes and returns one part's arrays. A program takes and returns all parts, laid end to end along the dimension named above; an argument that names none is the same for every part. Nothing has to cross between parts.
Inputs may be any that keep to these rules, and one draw needn't show every extreme that they name: Every cell has exactly one partner, on another tile, and is its partner's partner. Two tiles share at most 8 pairs, and every tile shares exactly 8 with some tile.
All inputs are finite; a program needn't handle non-finite values.
Results may differ from the reference program's by a relative error of at most 0.0003.
Values sent between devices are 32-bit elements; how exact they have to be, the bound alone decides.
A program may use at most 64 MiB of HBM per device.

```python
import math
import jax
import jax.numpy as jnp
from jax import lax

TILE = 512
CELL = 64
MARGIN = 32
BAND = 32
KERNELS = 6
CONDS = 1
CELLS = 64
DOMAIN = 576
CAP = 8
ROWS = 8192
N_TILE = 16


def draw_partner(key, part):
    tile_count = N_TILE
    half_turn = tile_count // 2
    capacity = CAP
    half_cap = capacity // 2
    key_class, key_place, key_cells = jax.random.split(key, 3)
    picked = jax.random.permutation(key_class, half_turn - 1)
    class_load = jnp.full((half_turn - 1,), half_cap, jnp.int32)
    class_load = class_load.at[picked[0]].add(half_cap).at[picked[1]].add(-half_cap)
    seg_load = jnp.concatenate([jnp.repeat(class_load, 2), jnp.full((1,), capacity, jnp.int32)])
    seg_end = jnp.cumsum(seg_load)
    seg_start = seg_end - seg_load
    slot_ids = jnp.arange(CELLS, dtype=jnp.int32)
    segment = jnp.sum((slot_ids[:, None] >= seg_end[None, :]).astype(jnp.int32), axis=1)
    rank_in = slot_ids - seg_start[segment]
    is_last = segment == 2 * half_turn - 2
    offset = jnp.where(is_last, half_turn, segment // 2 + 1)
    signed = jnp.where(is_last | (segment % 2 == 0), offset, -offset)
    mate_seg = jnp.where(is_last, segment, jnp.bitwise_xor(segment, 1))
    mate_slot = seg_start[mate_seg] + rank_in
    place_order = jax.random.permutation(key_place, tile_count).astype(jnp.int32)
    position = jnp.zeros((tile_count,), jnp.int32).at[place_order].set(jnp.arange(tile_count, dtype=jnp.int32))
    devices = jnp.arange(tile_count, dtype=jnp.int32)
    cell_perm = jax.vmap(lambda device: jax.random.permutation(jax.random.fold_in(key_cells, device), CELLS).astype(jnp.int32))(devices)
    mate_pos = (position[:, None] + signed[None, :]) % tile_count
    mate_dev = place_order[mate_pos]
    mate_cell = cell_perm[mate_dev, jnp.broadcast_to(mate_slot[None, :], mate_dev.shape)]
    flat_index = devices[:, None] * CELLS + cell_perm
    values = mate_dev * CELLS + mate_cell
    return jnp.zeros((tile_count * CELLS,), jnp.int32).at[flat_index.reshape(-1)].set(values.reshape(-1))


def level_of(own_key, dims, pieces, low, largest):
    gain = 1.0
    for dim, shards_of in pieces:
        steps = jax.random.uniform(jax.random.fold_in(jax.random.fold_in(own_key, 6), dim), (shards_of,), jnp.float32, low / len(pieces), largest / len(pieces))
        gain = gain * jnp.repeat(jnp.exp(steps), dims[dim] // shards_of).reshape((-1,) + (1,) * (len(dims) - 1 - dim))
    return gain


def noise(stream_key, dims, width, most, held_as=jnp.bfloat16):
    return jnp.clip(width * jax.random.normal(stream_key, dims, jnp.float32), -most, most).astype(held_as)


def setup_inputs(seed: int = 0, part: int = 0) -> dict:
    streams_of = jax.random.split(jax.random.key(seed), 7)
    part_keys = jax.random.split(jax.random.fold_in(streams_of[6], part), 7)
    return {
        "mask": jnp.clip(jax.random.uniform(part_keys[0], (ROWS, TILE), jnp.float32, -1.0, 1.0) * level_of(part_keys[0], (ROWS, TILE), ((0, 16),), -0.4, 0.0), -1.0, 1.0),
        "target": jnp.clip(1.0 * jax.random.uniform(part_keys[1], (ROWS, TILE), jnp.float32) ** level_of(part_keys[1], (ROWS, TILE), ((0, 16),), -0.2, 0.2), 0.0, 1.0),
        "partner": draw_partner(jax.random.fold_in(jax.random.fold_in(streams_of[6], part), 71), part),
        "kernels": noise(streams_of[3], (CONDS, KERNELS, 2, BAND, BAND), 1.0, 6.0, jnp.float32),
        "socs_weights": jnp.clip(jnp.exp(jax.random.uniform(streams_of[4], (KERNELS,), jnp.float32, math.log(0.2), math.log(1.0))), 0.2, 1.0),
        "dose": jnp.clip(jnp.exp(jax.random.uniform(streams_of[5], (CONDS,), jnp.float32, math.log(0.6), math.log(1.6))), 0.6, 1.6),
    }


HIGHEST = lax.Precision.HIGHEST
steepness = 4.0
step_size = 0.1
blur_taps = (0.0625, 0.25, 0.375, 0.25, 0.0625)

def matmul(first_op, second_op):
    return jnp.dot(first_op, second_op, precision=HIGHEST, preferred_element_type=jnp.float32)

def dft_tables(extent, band_size):
    frequency = jnp.arange(band_size, dtype=jnp.int32) - band_size // 2
    phase_index = frequency[:, None] * jnp.arange(extent, dtype=jnp.int32)[None, :] % extent
    angles = phase_index.astype(jnp.float32) * (2.0 * math.pi / extent)
    return (jnp.cos(angles), jnp.sin(angles))

def resist_blur(field_in):
    extent = field_in.shape[0]
    padded = jnp.pad(field_in, ((2, 2), (0, 0)))
    along_rows = sum((blur_taps[offset] * padded[offset:offset + extent] for offset in range(5)))
    return sum((blur_taps[offset] * jnp.roll(along_rows, offset - 2, axis=1) for offset in range(5)))

def spectrum_part(block, cos_x, sin_x, cos_y, sin_y, norm_factor):
    part_re = matmul(block, cos_y.T)
    part_im = -matmul(block, sin_y.T)
    spec_re = (matmul(cos_x, part_re) + matmul(sin_x, part_im)) * norm_factor
    spec_im = (matmul(cos_x, part_im) - matmul(sin_x, part_re)) * norm_factor
    return (spec_re, spec_im)

def kernel_field(amp_re, amp_im, cos_x, sin_x, cos_y, sin_y):
    band_size = cos_x.shape[0]
    col_count = cos_y.shape[1]
    quad_re = matmul(amp_re, cos_y) - matmul(amp_im, sin_y)
    quad_im = matmul(amp_re, sin_y) + matmul(amp_im, cos_y)
    first_op = jnp.concatenate([cos_x.T, -sin_x.T], axis=1)
    second_op = jnp.concatenate([jnp.concatenate([quad_re, quad_im], 1), jnp.concatenate([quad_im, -quad_re], 1)], 0)
    stacked = matmul(first_op, second_op) / band_size
    return (stacked[:, :col_count], stacked[:, col_count:])

def kernel_adjoint(grad_re, grad_im, cos_x, sin_x, cos_y, sin_y):
    band_size = cos_x.shape[0]
    quad_re = (matmul(cos_x, grad_re) + matmul(sin_x, grad_im)) / band_size
    quad_im = (matmul(cos_x, grad_im) - matmul(sin_x, grad_re)) / band_size
    amp_re = matmul(quad_re, cos_y.T) + matmul(quad_im, sin_y.T)
    amp_im = matmul(quad_im, cos_y.T) - matmul(quad_re, sin_y.T)
    return (amp_re, amp_im)

def pixel_adjoint(acc_re, acc_im, cos_x, sin_x, cos_y, sin_y, norm_factor):
    part_re = (matmul(cos_x.T, acc_re) - matmul(sin_x.T, acc_im)) * norm_factor
    part_im = (matmul(sin_x.T, acc_re) + matmul(cos_x.T, acc_im)) * norm_factor
    return matmul(part_re, cos_y) - matmul(part_im, sin_y)

def window_gradient(spec_re, spec_im, target_tile, kernels, socs_weights, dose, cos_x, sin_x, cos_y, sin_y, norm_factor):
    row_count = cos_x.shape[1]
    col_count = cos_y.shape[1]
    tile_side = target_tile.shape[0]
    margin = (row_count - tile_side) // 2
    acc_re = jnp.zeros_like(spec_re)
    acc_im = jnp.zeros_like(spec_im)
    for cond_id in range(kernels.shape[0]):
        intensity = jnp.zeros((row_count, col_count), jnp.float32)
        stored = []
        for kernel_id in range(kernels.shape[1]):
            kern_re = kernels[cond_id, kernel_id, 0]
            kern_im = kernels[cond_id, kernel_id, 1]
            amp_re = kern_re * spec_re - kern_im * spec_im
            amp_im = kern_re * spec_im + kern_im * spec_re
            field_re, field_im = kernel_field(amp_re, amp_im, cos_x, sin_x, cos_y, sin_y)
            stored.append((field_re, field_im))
            intensity = intensity + socs_weights[kernel_id] * (field_re * field_re + field_im * field_im)
        blurred = resist_blur(intensity)
        resist = jax.nn.sigmoid(steepness * (dose[cond_id] * blurred - 1.0))
        interior = resist[margin:margin + tile_side] - target_tile
        grad_resist = jnp.pad(2.0 * interior, ((margin, margin), (0, 0)))
        grad_image = resist_blur(grad_resist * (steepness * dose[cond_id]) * resist * (1.0 - resist))
        for kernel_id in range(kernels.shape[1]):
            kern_re = kernels[cond_id, kernel_id, 0]
            kern_im = kernels[cond_id, kernel_id, 1]
            field_re, field_im = stored[kernel_id]
            scaled = 2.0 * socs_weights[kernel_id] * grad_image
            grad_ar, grad_ai = kernel_adjoint(scaled * field_re, scaled * field_im, cos_x, sin_x, cos_y, sin_y)
            acc_re = acc_re + kern_re * grad_ar + kern_im * grad_ai
            acc_im = acc_im + kern_re * grad_ai - kern_im * grad_ar
    return pixel_adjoint(acc_re, acc_im, cos_x, sin_x, cos_y, sin_y, norm_factor)

def to_cells(pixels):
    per_side = TILE // CELL
    return pixels.reshape(N_TILE, per_side, CELL, per_side, CELL).transpose(0, 1, 3, 2, 4).reshape(N_TILE * CELLS, CELL * CELL)

def from_cells(cell_rows):
    per_side = TILE // CELL
    return cell_rows.reshape(N_TILE, per_side, per_side, CELL, CELL).transpose(0, 1, 3, 2, 4).reshape(N_TILE * TILE, TILE)

def reference(mask, target, partner, kernels, socs_weights, dose):
    mask_cells = to_cells(mask)
    averaged = from_cells(0.5 * (mask_cells + mask_cells[partner]))
    cos_x, sin_x = dft_tables(DOMAIN, BAND)
    cos_y, sin_y = dft_tables(TILE, BAND)
    norm_factor = 1.0 / math.sqrt(DOMAIN * TILE)
    padded = jnp.pad(averaged, ((MARGIN, MARGIN), (0, 0)))

    def one_window(tile_id):
        start = (tile_id * TILE).astype(jnp.int32)
        window = lax.dynamic_slice_in_dim(padded, start, DOMAIN, 0)
        target_tile = lax.dynamic_slice_in_dim(target, start, TILE, 0)
        spec_re, spec_im = spectrum_part(window, cos_x, sin_x, cos_y, sin_y, norm_factor)
        return window_gradient(spec_re, spec_im, target_tile, kernels, socs_weights, dose, cos_x, sin_x, cos_y, sin_y, norm_factor)
    windows = lax.map(one_window, jnp.arange(N_TILE, dtype=jnp.int32))
    core = windows[:, MARGIN:MARGIN + TILE]
    core = core.at[:-1, TILE - MARGIN:].add(windows[1:, :MARGIN])
    core = core.at[1:, :MARGIN].add(windows[:-1, MARGIN + TILE:])
    summed_cells = to_cells(core.reshape(N_TILE * TILE, TILE))
    gradient = from_cells(0.5 * (summed_cells + summed_cells[partner]))
    updated = averaged - step_size * gradient
    return (gradient, updated)
```

```python
import functools
import math

import numpy as np
import jax
import jax.numpy as jnp
from jax import lax
from jax.experimental import pallas as pl
from jax.experimental.pallas import tpu as pltpu
from jax.sharding import PartitionSpec as P

TILE = 512
CELL = 64
MARGIN = 32
BAND = 32
CELLS = 64
SIDE = 8
DOMAIN = 576
GRID = 64
KERNELS = 6
CUTS = (3, 8, 11, 15)
EXTRA = 16
RELAYS = 4
VMEM_LIMIT = 56 * 1024 * 1024
HIGHEST = lax.Precision.HIGHEST
BLUR = (0.0625, 0.25, 0.375, 0.25, 0.0625)


def tables():
    f = np.arange(BAND) - BAND // 2
    norm = 0.5 / math.sqrt(DOMAIN * TILE)
    ph_x = np.zeros((2, SIDE, BAND, 128))
    for h in range(2):
        ang = 2 * np.pi * np.outer(1 + 2 * np.arange(SIDE) + h, f) / 18.0
        ph_x[0, :, :, 64 * h : 64 * h + 64] = norm * np.cos(ang)[:, :, None]
        ph_x[1, :, :, 64 * h : 64 * h + 64] = norm * np.sin(ang)[:, :, None]
    ang = 2 * np.pi * np.outer(np.arange(SIDE), f) / 8.0
    ph_y = np.stack([np.tile(np.cos(ang), (1, 4)), np.tile(np.sin(ang), (1, 4))])
    ang = 2 * np.pi * f * 16 / 18.0
    one = np.ones((1, 32))
    cos16, sin16 = np.cos(ang)[:, None] * one, np.sin(ang)[:, None] * one
    sh = np.stack(
        [np.concatenate([cos16] * 4, 1), np.concatenate([-sin16, sin16] * 2, 1)]
    )
    q = np.arange(CELL)
    cy = np.cos(2 * np.pi * np.outer(f, q) / TILE)
    sy = np.sin(2 * np.pi * np.outer(f, q) / TILE)
    by = np.zeros((256, 512))
    for i in range(4):
        r, o = 64 * i, 64 * i
        by[r : r + 32, o : o + 64] = cy
        by[r : r + 32, 256 + o : 256 + o + 64] = sy
        by[r + 32 : r + 64, o : o + 64] = -sy
        by[r + 32 : r + 64, 256 + o : 256 + o + 64] = cy
    r32 = np.arange(32)
    cx = np.cos(2 * np.pi * np.outer(r32, f) / DOMAIN)
    sx = np.sin(2 * np.pi * np.outer(r32, f) / DOMAIN)
    lx = np.zeros((256, 512))
    for j in range(8):
        k = 32 * j
        lx[k : k + 32, k : k + 32] = cx
        lx[k : k + 32, 256 + k : 256 + k + 32] = -sx
    m = np.arange(GRID)
    c = np.cos(2 * np.pi * np.outer(f, m) / GRID)
    s = np.sin(2 * np.pi * np.outer(f, m) / GRID)
    yt = np.zeros((128, 128))
    yt[:32, :64], yt[:32, 64:], yt[32:64, :64], yt[32:64, 64:] = c, s, -s, c
    x1 = np.concatenate([c.T, s.T], 1) / BAND
    x2 = np.concatenate([c, s], 1) / BAND
    y2 = np.zeros((128, 128))
    half = np.concatenate([np.concatenate([c.T, -s.T], 1), np.concatenate([s.T, c.T], 1)], 0)
    y2[:, :64], y2[:, 64:] = half, half
    g = np.arange(-31, 32)

    def interp(extent):
        d = np.arange(extent)[:, None] / extent - m[None, :] / GRID
        return np.cos(2 * np.pi * g[:, None, None] * d[None]).sum(0) / GRID

    ux = interp(DOMAIN)
    ux = sum(BLUR[i] * ux[MARGIN - 2 + i : MARGIN - 2 + i + TILE] for i in range(5))
    uy = interp(TILE)
    uy = sum(BLUR[i] * np.roll(uy, i - 2, axis=0) for i in range(5))
    uyt = np.concatenate([uy.T, uy.T], 0)
    uy2 = np.concatenate([uy, uy], 1)
    whole = [ph_x, ph_y, sh, yt, x1, x2, y2, ux, uyt]
    return [np.ascontiguousarray(t, dtype=np.float32) for t in whole] + [
        split(np.ascontiguousarray(t, dtype=np.float32)) for t in (by, 2 * lx, lx.T, ux.T, uy2)
    ]


def split(t):
    hi = t.astype(jnp.bfloat16)
    return np.stack([hi, (t - hi.astype(np.float32)).astype(jnp.bfloat16)])


def dot(x, y):
    return jnp.dot(x, y, precision=HIGHEST, preferred_element_type=jnp.float32)


def halves(x):
    hi = x.astype(jnp.bfloat16)
    return hi, (x - hi.astype(jnp.float32)).astype(jnp.bfloat16)


def dot3(x, y, dims=((1,), (0,))):
    def one(p, q):
        return lax.dot_general(p, q, (dims, ((), ())), preferred_element_type=jnp.float32)

    return one(x[0], y[0]) + (one(x[0], y[1]) + one(x[1], y[0]))


def body(n, cap, n_in, wts, dose, tab, *refs):
    hbm, outs = refs[:n_in], refs[n_in : n_in + 3]
    vm = refs[n_in + 3 : 2 * n_in + 3]
    load_sem = refs[2 * n_in + 3]
    (
        mask, target, kraw, ph_x, ph_y, sh, yt, x1, x2, y2, ux, uyt, by, lx, lxt, uxt, uy2
    ) = vm
    main(n, cap, tab, wts, dose, hbm, vm, load_sem,
         mask, target, kraw, ph_x, ph_y, sh, yt, x1, x2, y2, ux, uyt, by, lx, lxt, uxt, uy2,
         *outs, *refs[2 * n_in + 4 :])


def main(
    n, cap, tab, wts, dose, hbm, vm, load_sem,
    mask, target, kraw, ph_x, ph_y, sh, yt, x1, x2, y2, ux, uyt, by, lx, lxt, uxt, uy2,
    grad_out, upd_out, flag_out, pc, ps,
    out_cells, in_cells, tiles, plane, vv, wide, part, top, bot, spec_in, acc_all, acc2, acc2s, rhs, rhs2, stack,
    kr, ki, ix, tab_sem, out_ov, in_ov, out2, in2, meta_out, meta_in, route_v, route, flag_mine, flag_in,
    ov_send, ov_recv, meta_send, meta_recv, hop_send, hop_recv, flag_send, flag_recv,
    cell_send, cell_recv, spec_send, spec_recv, acc_send, acc_recv,
):
    me = lax.axis_index("tile")
    lane = lax.broadcasted_iota(jnp.int32, (32, 128), 1)
    low = lane < 64
    slabs = lax.axis_size("slab")
    slab = lax.axis_index("slab")
    direct = cap // 2
    first = n // 4
    relay = (me - first) // 2
    is_relay = (me >= first) & (me < first + 2 * RELAYS) & (lax.rem(me, 2) == 0)

    def swap(x):
        return jnp.where(lane % 64 < 32, pltpu.roll(x, 96, 1), pltpu.roll(x, 32, 1))

    def pair(x, y):
        rx, ry = pltpu.roll(x, 64, 1), pltpu.roll(y, 64, 1)
        return jnp.where(low, x, ry), jnp.where(low, rx, y)

    def to_tiles(src):
        @pl.loop(0, SIDE)
        def _(a):
            r = pl.multiple_of(a * 64, 64)
            for b in range(4):
                h0 = src[pl.ds(r, 32), 128 * b : 128 * b + 128]
                h1 = src[pl.ds(r + 32, 32), 128 * b : 128 * b + 128]
                x, y = pair(h0, h1)
                tiles[a * 8 + 2 * b] = x
                tiles[a * 8 + 2 * b + 1] = y

    def compact(x):
        return jnp.where(low[0:16], x[0:16], x[16:32])

    def expand(x):
        r = pltpu.roll(x, 64, 1)
        return jnp.concatenate([jnp.where(low[0:16], x, r), jnp.where(low[0:16], r, x)], axis=0)

    def peer_of(k):
        return jnp.bitwise_xor(me, k)

    barrier = pltpu.get_barrier_semaphore()

    @pl.loop(1, n)
    def _(k):
        pl.semaphore_signal(barrier, inc=1, device_id={"tile": peer_of(k)}, device_id_type=pl.DeviceIdType.MESH)

    for k in range(1, slabs):
        pl.semaphore_signal(
            barrier, inc=1, device_id={"slab": lax.rem(slab + k, slabs)}, device_id_type=pl.DeviceIdType.MESH
        )

    index_load = pltpu.make_async_copy(tab.at[pl.ds(0, 8)], ix, tab_sem.at[0])
    meta_load = pltpu.make_async_copy(tab.at[pl.ds(8, meta_out.shape[0])], meta_out, tab_sem.at[1])
    index_load.start()
    meta_load.start()

    loads = [pltpu.make_async_copy(hbm[i], vm[i], load_sem.at[i]) for i in range(len(hbm))]
    for load in loads:
        load.start()

    loads[0].wait()
    to_tiles(mask)

    in_cells[pl.ds(me * direct, direct)] = jnp.zeros((direct, 32, 128), jnp.float32)
    index_load.wait()
    meta_load.wait()

    @pl.loop(0, EXTRA, unroll=4)
    def _(o):
        x = tiles[ix[3, CELLS + o]]
        for q in range(RELAYS):
            out_ov[q, o] = x[8 * q : 8 * q + 8]

    pl.semaphore_wait(barrier, n + slabs - 2)

    def to_relay(q, source):
        where = {"device_id": {"tile": first + 2 * q}, "device_id_type": pl.DeviceIdType.MESH}
        return (
            pltpu.make_async_remote_copy(
                src_ref=meta_out, dst_ref=meta_in.at[source],
                send_sem=meta_send.at[q], recv_sem=meta_recv.at[source], **where,
            ),
            pltpu.make_async_remote_copy(
                src_ref=out_ov.at[q], dst_ref=in_ov.at[pl.ds(source * EXTRA, EXTRA)],
                send_sem=ov_send.at[q], recv_sem=ov_recv.at[source], **where,
            ),
        )

    for q in range(RELAYS):
        @pl.when(me != first + 2 * q)
        def _():
            for copy in to_relay(q, me):
                copy.start()

    def cell_copy(k):
        to = peer_of(k)
        return pltpu.make_async_remote_copy(
            src_ref=out_cells.at[to], dst_ref=in_cells.at[pl.ds(me * direct, direct)],
            send_sem=cell_send.at[k], recv_sem=cell_recv.at[k],
            device_id={"tile": to}, device_id_type=pl.DeviceIdType.MESH,
        )

    cuts = [(n - 1) * c // 15 for c in (0,) + CUTS + (15,)]

    def offset_of(j):
        return jnp.where(lax.rem(j, 2) == 0, n // 2 + j // 2, n // 2 - 1 - j // 2)

    def pack(k):
        to = peer_of(k)
        for r in range(direct):
            out_cells[to, r] = tiles[ix[0, to * cap + r]]

    def start_cells(stage):
        @pl.loop(cuts[stage], cuts[stage + 1])
        def _(j):
            cell_copy(offset_of(j)).start()

    @pl.loop(cuts[0], cuts[1])
    def _(j):
        pack(offset_of(j))
        cell_copy(offset_of(j)).start()

    @pl.loop(cuts[1], n - 1)
    def _(j):
        pack(offset_of(j))

    for load in loads[1:]:
        load.wait()

    zero = jnp.zeros((32, 128), jnp.float32)
    lane_sign = jnp.where(lane % 64 < 32, -1.0, 1.0)

    @pl.loop(0, SIDE)
    def _(a):
        c, s = ph_x[0, a], ph_x[1, a]
        for b in range(SIDE):
            cb, sb = ph_y[0, b : b + 1, :], ph_y[1, b : b + 1, :]
            pc[a * 8 + b] = c * cb - s * sb
            ps[a * 8 + b] = (s * cb + c * sb) * lane_sign

    pc[CELLS] = zero
    ps[CELLS] = zero

    lxt_pair = lxt[0], lxt[1]
    for g in range(2):
        vv[g] = dot3(lxt_pair, halves(mask[256 * g : 256 * g + 256, :]))
    for g in range(2):
        for c in range(2):
            cols = slice(256 * c, 256 * c + 256)
            left = jnp.concatenate([vv[g, 0:256, cols], vv[g, 256:512, cols]], axis=1)
            plane[256 * g : 256 * g + 256, cols] = dot3(halves(left), (by[0], by[1]), ((1,), (1,)))
    to_tiles(plane)

    top[n] = zero
    bot[0] = zero

    @pl.loop(0, n, unroll=2)
    def _(t):
        sums = [zero] * 6
        for r in range(cap):
            s = t * cap + r
            x = tiles[ix[0, s]]
            p = ix[1, s]
            u, w = x * pc[p], x * ps[p]
            wt = jnp.where(p < 8, 1.0, 0.0)
            wb = jnp.where(p >= 56, 1.0, 0.0)
            sums = [
                sums[0] + u, sums[1] + w, sums[2] + wt * u, sums[3] + wt * w,
                sums[4] + wb * u, sums[5] + wb * w,
            ]
        wide[t] = sums[0] + swap(sums[1])
        top[t] = sums[2] + swap(sums[3])
        bot[t + 1] = sums[4] + swap(sums[5])

    def own_row(a, carry):
        u, w = carry
        for b in range(8):
            x = tiles[a * 8 + b]
            u, w = u + x * pc[a * 8 + b], w + x * ps[a * 8 + b]
        return u, w

    u0, w0 = own_row(0, (zero, zero))
    u7, w7 = own_row(7, (zero, zero))
    u, w = lax.fori_loop(1, 7, own_row, (u0 + u7, w0 + w7))
    wide[me] += u + swap(w)
    top[me] += u0 + swap(w0)
    bot[me + 1] += u7 + swap(w7)

    @pl.loop(0, n, unroll=4)
    def _(t):
        tp = jnp.where(low, top[t + 1], 0.0)
        bt = jnp.where(low, 0.0, bot[t])
        tp = tp + pltpu.roll(tp, 64, 1)
        bt = bt + pltpu.roll(bt, 64, 1)
        x = wide[t]
        x = x + pltpu.roll(x, 64, 1)
        both = (tp + bt) * sh[0] + pltpu.roll((bt - tp), 32, 1) * sh[1]
        part[t] = compact(x + both)

    def spec_copy(k):
        to = peer_of(k)
        return pltpu.make_async_remote_copy(
            src_ref=part.at[to], dst_ref=spec_in.at[me],
            send_sem=spec_send.at[k], recv_sem=spec_recv.at[k],
            device_id={"tile": to}, device_id_type=pl.DeviceIdType.MESH,
        )

    @pl.loop(1, n)
    def _(k):
        spec_copy(k).start()

    start_cells(1)

    def flag_copy(k):
        to = lax.rem(slab + k, slabs)
        return pltpu.make_async_remote_copy(
            src_ref=flag_mine, dst_ref=flag_in.at[k],
            send_sem=flag_send.at[k], recv_sem=flag_recv.at[k],
            device_id={"slab": to}, device_id_type=pl.DeviceIdType.MESH,
        )

    def hop_copy(k, source):
        to = peer_of(k)
        return pltpu.make_async_remote_copy(
            src_ref=out2.at[to], dst_ref=in2.at[source],
            send_sem=hop_send.at[k], recv_sem=hop_recv.at[source],
            device_id={"tile": to}, device_id_type=pl.DeviceIdType.MESH,
        )

    @pl.when(is_relay)
    def _():
        meta_in[me] = meta_out[...]
        in_ov[pl.ds(me * EXTRA, EXTRA)] = out_ov[relay]

        @pl.loop(1, n)
        def _(k):
            for copy in to_relay(0, peer_of(k)):
                copy.wait_recv()

        lines = n // 8
        slot = lax.broadcasted_iota(jnp.int32, (lines, 128), 1) % 16
        start = jnp.zeros((lines, 128), jnp.int32)
        found = jnp.zeros((lines, 128), jnp.int32)
        most = jnp.zeros((lines, 128), jnp.int32)
        for i in range(n):
            count, offset = meta_in[i, 0:lines], meta_in[i, lines : 2 * lines]
            rel = slot - start
            found = jnp.where((rel >= 0) & (rel < count), i * EXTRA + offset + rel, found)
            start = start + count
            most = jnp.maximum(most, count + offset)
        route_v[...] = jnp.zeros((8, 128), jnp.int32)
        route_v[0:lines] = jnp.clip(found, 0, n * EXTRA - 1)
        over = jnp.broadcast_to(jnp.max(jnp.where(most > EXTRA, 1.0, 0.0)), (8, 128))
        route_copy = pltpu.make_async_copy(route_v, route, tab_sem.at[2])
        route_copy.start()
        flag_mine[...] = over

        @pl.when(me == first)
        def _():
            for k in range(1, slabs):
                flag_copy(k).start()

        route_copy.wait()

        @pl.loop(0, n)
        def _(d):
            for m in range(EXTRA):
                out2[d, m] = in_ov[route[d // 8, lax.rem(d, 8) * 16 + m]]

        flag_in[0] = over

        @pl.when(me == first)
        def _():
            for k in range(1, slabs):
                flag_copy(k).wait()
                flag_in[0] = jnp.maximum(flag_in[0], flag_in[k])

        @pl.loop(0, n)
        def _(d):
            out2[d, EXTRA] = flag_in[0]

        @pl.loop(1, n)
        def _(k):
            hop_copy(k, relay).start()

        in2[relay] = out2[me]

    spec_in[me] = part[me]

    for k in range(KERNELS):
        rows = slice(32 * k, 32 * k + 32)
        re, im = kraw[64 * k : 64 * k + 32, :], kraw[64 * k + 32 : 64 * k + 64, :]
        kr[rows, :] = jnp.concatenate([re] * 4, axis=1)
        ki[rows, :] = jnp.concatenate([-im, im] * 2, axis=1)

    @pl.loop(1, n)
    def _(k):
        spec_copy(k).wait_recv()

    start_cells(2)
    spec = expand(lax.fori_loop(0, n, lambda t, s: s + spec_in[t], zero[0:16]))

    spec_s = pltpu.roll(spec, 32, 1)
    for k in range(KERNELS):
        rows = slice(32 * k, 32 * k + 32)
        stack[rows, :] = spec * kr[rows, :] + spec_s * ki[rows, :]
    fields_y = dot(stack[...], yt[...])
    sign = jnp.where(low, -1.0, 1.0)
    for k in range(KERNELS):
        part_k = fields_y[32 * k : 32 * k + 32]
        rhs[0:32, 128 * k : 128 * k + 128] = part_k
        rhs[32:64, 128 * k : 128 * k + 128] = pltpu.roll(part_k, 64, 1) * sign
    fields = dot(x1[...], rhs[...])
    inten = jnp.zeros((64, 128), jnp.float32)
    for k in range(KERNELS):
        e = fields[:, 128 * k : 128 * k + 128]
        inten = inten + wts[k] * (e * e)
    blurred = dot(ux[...], dot(inten, uyt[...]))
    d = dose[0]
    resist = jax.nn.sigmoid(4.0 * (d * blurred - 1.0))
    slope = 2.0 * (resist - target[...]) * (4.0 * d) * resist * (1.0 - resist)
    grad_i = dot3((uxt[0], uxt[1]), halves(dot3(halves(slope), (uy2[0], uy2[1]))))
    lane2 = lax.broadcasted_iota(jnp.int32, (64, 128), 1)
    sign2 = jnp.where(lane2 < 64, 1.0, -1.0)
    for k in range(KERNELS):
        ge = (2.0 * wts[k]) * grad_i * fields[:, 128 * k : 128 * k + 128]
        rhs2[0:64, 128 * k : 128 * k + 128] = ge
        rhs2[64:128, 128 * k : 128 * k + 128] = pltpu.roll(ge, 64, 1) * sign2
    grad_y = dot(x2[...], rhs2[...])
    for k in range(KERNELS):
        stack[32 * k : 32 * k + 32, :] = grad_y[:, 128 * k : 128 * k + 128]
    grad_a = dot(stack[...], y2[...])
    acc = zero
    for k in range(KERNELS):
        rows = slice(32 * k, 32 * k + 32)
        ga = grad_a[rows]
        acc = acc + kr[rows, :] * ga - ki[rows, :] * pltpu.roll(ga, 32, 1)
    acc_all[me] = compact(acc)

    def acc_copy(k):
        return pltpu.make_async_remote_copy(
            src_ref=acc_all.at[me], dst_ref=acc_all.at[me],
            send_sem=acc_send.at[k], recv_sem=acc_recv.at[k],
            device_id={"tile": peer_of(k)}, device_id_type=pl.DeviceIdType.MESH,
        )

    @pl.loop(1, n)
    def _(k):
        acc_copy(k).start()

    start_cells(3)

    @pl.loop(1, n)
    def _(k):
        acc_copy(k).wait_recv()

    start_cells(4)

    @pl.loop(0, n, unroll=4)
    def _(t):
        mid = expand(acc_all[t])
        before = expand(acc_all[jnp.maximum(t - 1, 0)]) * jnp.where(t > 0, 1.0, 0.0)
        after = expand(acc_all[jnp.minimum(t + 1, n - 1)]) * jnp.where(t < n - 1, 1.0, 0.0)
        first = mid + before * sh[0] + pltpu.roll(before, 32, 1) * sh[1]
        last = mid + after * sh[0] - pltpu.roll(after, 32, 1) * sh[1]
        mid_s, first_s, last_s = (pltpu.roll(v, 32, 1) for v in (mid, first, last))
        acc2[t * 3] = jnp.where(low, first, mid)
        acc2[t * 3 + 1] = mid
        acc2[t * 3 + 2] = jnp.where(low, mid, last)
        acc2s[t * 3] = jnp.where(low, first_s, mid_s)
        acc2s[t * 3 + 1] = mid_s
        acc2s[t * 3 + 2] = jnp.where(low, mid_s, last_s)

    @pl.loop(0, SIDE)
    def _(a):
        r = pl.multiple_of(a * 64, 64)
        own = me * 3 + jnp.where(a == 0, 0, jnp.where(a == SIDE - 1, 2, 1))
        own_x, own_s = acc2[own], acc2s[own]
        for b in range(4):
            pieces = []
            for i in range(2):
                c = a * 8 + 2 * b + i
                g, p = ix[2, CELLS + c], ix[3, c]
                pieces.append(own_x * pc[c] + own_s * ps[c] + acc2[g] * pc[p] + acc2s[g] * ps[p])
            h0, h1 = pair(*pieces)
            plane[pl.ds(r, 32), 128 * b : 128 * b + 128] = h0
            plane[pl.ds(r + 32, 32), 128 * b : 128 * b + 128] = h1

    for c in range(2):
        for g in range(2):
            v = dot3(halves(plane[256 * g : 256 * g + 256, 256 * c : 256 * c + 256]), (by[0], by[1]))
            vv[g, 0:256, 256 * c : 256 * c + 256] = v[:, 0:256]
            vv[g, 256:512, 256 * c : 256 * c + 256] = v[:, 256:512]
    for g in range(2):
        grad_out[256 * g : 256 * g + 256, :] = dot3((lx[0], lx[1]), halves(vv[g]))

    @pl.loop(1, n)
    def _(k):
        cell_copy(k).wait_recv()

    for q in range(RELAYS):
        @pl.when(me != first + 2 * q)
        def _():
            hop_copy(1, q).wait_recv()

    flag_out[0] = in2[0, EXTRA][0, 0]
    for m in range(EXTRA):
        in_cells[n * direct + m] = jnp.concatenate([in2[q, m] for q in range(RELAYS)], axis=0)

    @pl.loop(0, SIDE)
    def _(a):
        r = pl.multiple_of(a * 64, 64)
        for b in range(4):
            c = a * 8 + 2 * b
            both = pair(in_cells[ix[2, c]],
                          in_cells[ix[2, c + 1]])
            for h in range(2):
                where = (pl.ds(r + 32 * h, 32), slice(128 * b, 128 * b + 128))
                upd_out[where] = mask[where] + both[h]

    @pl.loop(1, n)
    def _(k):
        cell_copy(k).wait_send()
        spec_copy(k).wait_send()
        acc_copy(k).wait_send()

    for q in range(RELAYS):
        @pl.when(me != first + 2 * q)
        def _():
            for copy in to_relay(q, me):
                copy.wait_send()

    @pl.when(is_relay)
    def _():
        @pl.loop(1, n)
        def _(k):
            hop_copy(k, relay).wait_send()


def full_body(n, cap, tab, mask_hbm, both_out, mask, ix, tiles, out_cells, in_cells, tab_sem, cell_send, cell_recv):
    me = lax.axis_index("tile")
    low = lax.broadcasted_iota(jnp.int32, (32, 128), 1) < 64

    def pair(x, y):
        rx, ry = pltpu.roll(x, 64, 1), pltpu.roll(y, 64, 1)
        return jnp.where(low, x, ry), jnp.where(low, rx, y)

    barrier = pltpu.get_barrier_semaphore()

    @pl.loop(1, n)
    def _(k):
        pl.semaphore_signal(
            barrier, inc=1, device_id={"tile": jnp.bitwise_xor(me, k)}, device_id_type=pl.DeviceIdType.MESH
        )

    index_load = pltpu.make_async_copy(tab.at[pl.ds(0, 8)], ix, tab_sem.at[0])
    index_load.start()
    mask_load = pltpu.make_async_copy(mask_hbm, mask, tab_sem.at[1])
    mask_load.start()
    mask_load.wait()

    @pl.loop(0, SIDE)
    def _(a):
        r = pl.multiple_of(a * 64, 64)
        for b in range(4):
            h0 = mask[pl.ds(r, 32), 128 * b : 128 * b + 128]
            h1 = mask[pl.ds(r + 32, 32), 128 * b : 128 * b + 128]
            tiles[a * 8 + 2 * b], tiles[a * 8 + 2 * b + 1] = pair(h0, h1)

    index_load.wait()

    @pl.loop(0, n)
    def _(to):
        for r in range(cap):
            out_cells[to, r] = tiles[ix[0, to * cap + r]]

    in_cells[pl.ds(me * cap, cap)] = out_cells[me]
    pl.semaphore_wait(barrier, n - 1)

    def cell_copy(k):
        to = jnp.bitwise_xor(me, k)
        return pltpu.make_async_remote_copy(
            src_ref=out_cells.at[to], dst_ref=in_cells.at[pl.ds(me * cap, cap)],
            send_sem=cell_send.at[k], recv_sem=cell_recv.at[k],
            device_id={"tile": to}, device_id_type=pl.DeviceIdType.MESH,
        )

    @pl.loop(1, n)
    def _(k):
        cell_copy(k).start()

    @pl.loop(1, n)
    def _(k):
        cell_copy(k).wait()

    @pl.loop(0, SIDE)
    def _(a):
        r = pl.multiple_of(a * 64, 64)
        for b in range(4):
            c = a * 8 + 2 * b
            halves_of = pair(in_cells[ix[4, c]], in_cells[ix[4, c + 1]])
            for h in range(2):
                where = (pl.ds(r + 32 * h, 32), slice(128 * b, 128 * b + 128))
                both_out[where] = mask[where] + halves_of[h]


def full_exchange(n, cap, tab, mask):
    f32 = jnp.float32
    dma = pltpu.SemaphoreType.DMA((n,))
    vmem = pl.BlockSpec(memory_space=pltpu.VMEM)
    return pl.pallas_call(
        functools.partial(full_body, n, cap),
        out_shape=jax.ShapeDtypeStruct((TILE, TILE), f32),
        in_specs=[pl.BlockSpec(memory_space=pl.ANY), pl.BlockSpec(memory_space=pltpu.HBM)],
        out_specs=vmem,
        scratch_shapes=[
            pltpu.VMEM((TILE, TILE), f32),
            pltpu.SMEM((8, 128), jnp.int32),
            pltpu.VMEM((CELLS, 32, 128), f32),
            pltpu.VMEM((n, cap, 32, 128), f32),
            pltpu.VMEM((n * cap, 32, 128), f32),
            pltpu.SemaphoreType.DMA((2,)),
            dma, dma,
        ],
        compiler_params=pltpu.CompilerParams(
            collective_id=1, has_side_effects=True, vmem_limit_bytes=32 * 1024 * 1024
        ),
    )(tab, mask)


def local(consts, mask, target, partner, kernels, socs_weights, dose):
    n = lax.axis_size("tile")
    cap = 2 * CELLS // n
    owner = partner // CELLS
    pos = partner % CELLS
    ids = jnp.arange(CELLS, dtype=jnp.int32)
    same = owner[:, None] == owner[None, :]
    send_rank = jnp.sum((same & (pos[None, :] < pos[:, None])).astype(jnp.int32), axis=1)
    recv_rank = jnp.sum((same & (ids[None, :] < ids[:, None])).astype(jnp.int32), axis=1)
    send_slot = owner * cap + send_rank
    recv_slot = owner * cap + recv_rank
    hit = (jnp.arange(n * cap, dtype=jnp.int32)[:, None] == send_slot[None, :]).astype(jnp.int32)
    slot_cell = jnp.sum(hit * ids[None, :], axis=1)
    slot_pos = CELLS + jnp.sum(hit * (pos - CELLS)[None, :], axis=1)
    row = pos // SIDE
    kind = jnp.where(row == 0, 0, jnp.where(row == SIDE - 1, 2, 1))
    direct = cap // 2
    spare = send_rank >= direct
    ahead = jnp.sum((spare[None, :] & (owner[None, :] < owner[:, None])).astype(jnp.int32), axis=1)
    recv_index = jnp.where(
        recv_rank < direct, owner * direct + recv_rank,
        n * direct + jnp.minimum(ahead + recv_rank - direct, EXTRA - 1),
    )
    spare_slot = jnp.where(spare, ahead + send_rank - direct, -1)
    spare_cell = jnp.sum((ids[:, None] == spare_slot[None, :]).astype(jnp.int32) * ids[None, :], axis=1)
    dest = (jnp.arange(16 * n, dtype=jnp.int32) // 16)[:, None]
    count = jnp.sum((spare[None, :] & (owner[None, :] == dest)).astype(jnp.int32), axis=1)
    offset = jnp.sum((spare[None, :] & (owner[None, :] < dest)).astype(jnp.int32), axis=1)
    meta_lines = (2 * n // 8 + 7) // 8 * 8
    tab = jnp.concatenate(
        [slot_cell, slot_pos, recv_index, owner * 3 + kind, pos, spare_cell, recv_slot, recv_slot]
        + [jnp.zeros((3 * 128,), jnp.int32), count, offset, jnp.zeros((128 * meta_lines - 32 * n,), jnp.int32)]
    ).reshape(-1, 128)
    raw = kernels.reshape(2 * KERNELS * BAND, BAND)
    f32 = jnp.float32
    vmem = pl.BlockSpec(memory_space=pltpu.VMEM)
    hbm = pl.BlockSpec(memory_space=pltpu.HBM)
    arrays = [mask, target, raw, *consts]
    smem = pl.BlockSpec(memory_space=pltpu.SMEM)
    dma, few = pltpu.SemaphoreType.DMA((n,)), pltpu.SemaphoreType.DMA((RELAYS,))
    flags = pltpu.SemaphoreType.DMA((lax.axis_size("slab"),))
    twice, both, flag = pl.pallas_call(
        functools.partial(body, n, cap, len(arrays)),
        out_shape=(jax.ShapeDtypeStruct((TILE, TILE), f32),) * 2 + (jax.ShapeDtypeStruct((1,), f32),),
        in_specs=[smem] * 2 + [pl.BlockSpec(memory_space=pl.ANY)] + [hbm] * len(arrays),
        out_specs=(vmem, vmem, smem),
        scratch_shapes=[pltpu.VMEM(x.shape, x.dtype) for x in arrays] + [
            pltpu.SemaphoreType.DMA((len(arrays),)),
            pltpu.VMEM((CELLS + 1, 32, 128), f32),
            pltpu.VMEM((CELLS + 1, 32, 128), f32),
            pltpu.VMEM((n, direct, 32, 128), f32),
            pltpu.VMEM((n * direct + EXTRA, 32, 128), f32),
            pltpu.VMEM((CELLS, 32, 128), f32),
            pltpu.VMEM((TILE, TILE), f32),
            pltpu.VMEM((2, 512, 512), f32),
            pltpu.VMEM((n, 32, 128), f32),
            pltpu.VMEM((n, 16, 128), f32),
            pltpu.VMEM((n + 1, 32, 128), f32),
            pltpu.VMEM((n + 1, 32, 128), f32),
            pltpu.VMEM((n, 16, 128), f32),
            pltpu.VMEM((n, 16, 128), f32),
            pltpu.VMEM((3 * n, 32, 128), f32),
            pltpu.VMEM((3 * n, 32, 128), f32),
            pltpu.VMEM((64, 768), f32),
            pltpu.VMEM((128, 768), f32),
            pltpu.VMEM((192, 128), f32),
            pltpu.VMEM((192, 128), f32),
            pltpu.VMEM((192, 128), f32),
            pltpu.SMEM((8, 128), jnp.int32),
            pltpu.SemaphoreType.DMA((3,)),
            pltpu.VMEM((RELAYS, EXTRA, 8, 128), f32),
            pltpu.VMEM((n * EXTRA, 8, 128), f32),
            pltpu.VMEM((n, EXTRA + 1, 8, 128), f32),
            pltpu.VMEM((RELAYS, EXTRA + 1, 8, 128), f32),
            pltpu.VMEM((meta_lines, 128), jnp.int32),
            pltpu.VMEM((n, meta_lines, 128), jnp.int32),
            pltpu.VMEM((8, 128), jnp.int32),
            pltpu.SMEM((8, 128), jnp.int32),
            pltpu.VMEM((8, 128), f32),
            pltpu.VMEM((lax.axis_size("slab"), 8, 128), f32),
            few, dma, few, dma, dma, few, flags, flags,
            dma, dma, dma, dma, dma, dma,
        ],
        compiler_params=pltpu.CompilerParams(
            collective_id=0, has_side_effects=True, vmem_limit_bytes=VMEM_LIMIT
        ),
    )(socs_weights, dose, tab, *arrays)
    both = lax.cond(
        flag[0] > 0.5, lambda t, m, b: full_exchange(n, cap, t, m), lambda t, m, b: b, tab, mask, both
    )
    return 0.5 * twice, 0.5 * (both - 0.1 * twice)


def solution(mesh):
    consts = tables()

    def run(mask, target, partner, kernels, socs_weights, dose):
        return local([jnp.asarray(t) for t in consts], mask, target, partner, kernels, socs_weights, dose)

    return jax.shard_map(
        run,
        mesh=mesh,
        in_specs=(
            P(("slab", "tile"), None),
            P(("slab", "tile"), None),
            P(("slab", "tile")),
            P(),
            P(),
            P(),
        ),
        out_specs=(P(("slab", "tile"), None), P(("slab", "tile"), None)),
        check_vma=False,
    )
```

```python
import functools
import math

import numpy as np
import jax
import jax.numpy as jnp
from jax import lax
from jax.experimental import pallas as pl
from jax.experimental.pallas import tpu as pltpu
from jax.sharding import PartitionSpec as P

TILE = 512
CELL = 64
MARGIN = 32
BAND = 32
CELLS = 64
SIDE = 8
DOMAIN = 576
GRID = 64
KERNELS = 6
CUTS = (4, 7, 10, 15)
EXTRA = 12
RELAYS = 4
VMEM_LIMIT = 56 * 1024 * 1024
HIGHEST = lax.Precision.HIGHEST
BLUR = (0.0625, 0.25, 0.375, 0.25, 0.0625)


def tables():
    f = np.arange(BAND) - BAND // 2
    norm = 0.5 / math.sqrt(DOMAIN * TILE)
    ph_x = np.zeros((2, SIDE, BAND, 128))
    for h in range(2):
        ang = 2 * np.pi * np.outer(1 + 2 * np.arange(SIDE) + h, f) / 18.0
        ph_x[0, :, :, 64 * h : 64 * h + 64] = norm * np.cos(ang)[:, :, None]
        ph_x[1, :, :, 64 * h : 64 * h + 64] = norm * np.sin(ang)[:, :, None]
    ang = 2 * np.pi * np.outer(np.arange(SIDE), f) / 8.0
    ph_y = np.stack([np.tile(np.cos(ang), (1, 4)), np.tile(np.sin(ang), (1, 4))])
    ang = 2 * np.pi * f * 16 / 18.0
    one = np.ones((1, 32))
    cos16, sin16 = np.cos(ang)[:, None] * one, np.sin(ang)[:, None] * one
    sh = np.stack(
        [np.concatenate([cos16] * 4, 1), np.concatenate([-sin16, sin16] * 2, 1)]
    )
    q = np.arange(CELL)
    cy = np.cos(2 * np.pi * np.outer(f, q) / TILE)
    sy = np.sin(2 * np.pi * np.outer(f, q) / TILE)
    by = np.zeros((256, 512))
    for i in range(4):
        r, o = 64 * i, 64 * i
        by[r : r + 32, o : o + 64] = cy
        by[r : r + 32, 256 + o : 256 + o + 64] = sy
        by[r + 32 : r + 64, o : o + 64] = -sy
        by[r + 32 : r + 64, 256 + o : 256 + o + 64] = cy
    r32 = np.arange(32)
    cx = np.cos(2 * np.pi * np.outer(r32, f) / DOMAIN)
    sx = np.sin(2 * np.pi * np.outer(r32, f) / DOMAIN)
    lx = np.zeros((256, 512))
    for j in range(8):
        k = 32 * j
        lx[k : k + 32, k : k + 32] = cx
        lx[k : k + 32, 256 + k : 256 + k + 32] = -sx
    m = np.arange(GRID)
    c = np.cos(2 * np.pi * np.outer(f, m) / GRID)
    s = np.sin(2 * np.pi * np.outer(f, m) / GRID)
    yt = np.zeros((128, 128))
    yt[:32, :64], yt[:32, 64:], yt[32:64, :64], yt[32:64, 64:] = c, s, -s, c
    x1 = np.concatenate([c.T, s.T], 1) / BAND
    x2 = np.concatenate([c, s], 1) / BAND
    y2 = np.zeros((128, 128))
    half = np.concatenate([np.concatenate([c.T, -s.T], 1), np.concatenate([s.T, c.T], 1)], 0)
    y2[:, :64], y2[:, 64:] = half, half
    g = np.arange(-31, 32)

    def interp(extent):
        d = np.arange(extent)[:, None] / extent - m[None, :] / GRID
        return np.cos(2 * np.pi * g[:, None, None] * d[None]).sum(0) / GRID

    ux = interp(DOMAIN)
    ux = sum(BLUR[i] * ux[MARGIN - 2 + i : MARGIN - 2 + i + TILE] for i in range(5))
    uy = interp(TILE)
    uy = sum(BLUR[i] * np.roll(uy, i - 2, axis=0) for i in range(5))
    uyt = np.concatenate([uy.T, uy.T], 0)
    uy2 = np.concatenate([uy, uy], 1)
    whole = [ph_x, ph_y, sh, yt, x1, x2, y2, ux, uyt]
    return [np.ascontiguousarray(t, dtype=np.float32) for t in whole] + [
        split(np.ascontiguousarray(t, dtype=np.float32)) for t in (by, 2 * lx, lx.T, ux.T, uy2)
    ]


def split(t):
    hi = t.astype(jnp.bfloat16)
    return np.stack([hi, (t - hi.astype(np.float32)).astype(jnp.bfloat16)])


def dot(x, y):
    return jnp.dot(x, y, precision=HIGHEST, preferred_element_type=jnp.float32)


def halves(x):
    hi = x.astype(jnp.bfloat16)
    return hi, (x - hi.astype(jnp.float32)).astype(jnp.bfloat16)


def dot3(x, y, dims=((1,), (0,))):
    def one(p, q):
        return lax.dot_general(p, q, (dims, ((), ())), preferred_element_type=jnp.float32)

    return one(x[0], y[0]) + (one(x[0], y[1]) + one(x[1], y[0]))


def body(n, cap, n_in, wts, dose, tab, *refs):
    hbm, outs = refs[:n_in], refs[n_in : n_in + 3]
    vm = refs[n_in + 3 : 2 * n_in + 3]
    load_sem = refs[2 * n_in + 3]
    (
        mask, target, kraw, ph_x, ph_y, sh, yt, x1, x2, y2, ux, uyt, by, lx, lxt, uxt, uy2
    ) = vm
    main(n, cap, tab, wts, dose, hbm, vm, load_sem,
         mask, target, kraw, ph_x, ph_y, sh, yt, x1, x2, y2, ux, uyt, by, lx, lxt, uxt, uy2,
         *outs, *refs[2 * n_in + 4 :])


def main(
    n, cap, tab, wts, dose, hbm, vm, load_sem,
    mask, target, kraw, ph_x, ph_y, sh, yt, x1, x2, y2, ux, uyt, by, lx, lxt, uxt, uy2,
    grad_out, upd_out, flag_out, pc, ps,
    out_cells, in_cells, tiles, plane, vv, wide, part, shared, top, bot, spec_in, acc_all, acc2, acc2s, rhs, rhs2, stack,
    kr, ki, ix, tab_sem, out_ov, in_ov, out2, in2, meta_out, meta_in, route_v, route, flag_mine, flag_in,
    ov_send, ov_recv, meta_send, meta_recv, hop_send, hop_recv, flag_send, flag_recv,
    cell_send, cell_recv, spec_send, spec_recv, acc_send, acc_recv,
):
    me = lax.axis_index("tile")
    lane = lax.broadcasted_iota(jnp.int32, (32, 128), 1)
    low = lane < 64
    slabs = lax.axis_size("slab")
    slab = lax.axis_index("slab")
    direct = cap // 2
    first = n // 4
    relay = (me - first) // 2
    is_relay = (me >= first) & (me < first + 2 * RELAYS) & (lax.rem(me, 2) == 0)

    def swap(x):
        return jnp.where(lane % 64 < 32, pltpu.roll(x, 96, 1), pltpu.roll(x, 32, 1))

    def pair(x, y):
        rx, ry = pltpu.roll(x, 64, 1), pltpu.roll(y, 64, 1)
        return jnp.where(low, x, ry), jnp.where(low, rx, y)

    def to_tiles(src):
        @pl.loop(0, SIDE)
        def _(a):
            r = pl.multiple_of(a * 64, 64)
            for b in range(4):
                h0 = src[pl.ds(r, 32), 128 * b : 128 * b + 128]
                h1 = src[pl.ds(r + 32, 32), 128 * b : 128 * b + 128]
                x, y = pair(h0, h1)
                tiles[a * 8 + 2 * b] = x
                tiles[a * 8 + 2 * b + 1] = y

    def compact(x):
        return jnp.where(low[0:16], x[0:16], x[16:32])

    def expand(x):
        r = pltpu.roll(x, 64, 1)
        return jnp.concatenate([jnp.where(low[0:16], x, r), jnp.where(low[0:16], r, x)], axis=0)

    chips = n // 2
    core = lax.rem(me, 2)
    chip = me // 2

    def place(t):
        return lax.rem(t, 2) * chips + t // 2

    def peer_of(k):
        return jnp.bitwise_xor(me, k)

    barrier = pltpu.get_barrier_semaphore()

    @pl.loop(1, n)
    def _(k):
        pl.semaphore_signal(barrier, inc=1, device_id={"tile": peer_of(k)}, device_id_type=pl.DeviceIdType.MESH)

    for k in range(1, slabs):
        pl.semaphore_signal(
            barrier, inc=1, device_id={"slab": lax.rem(slab + k, slabs)}, device_id_type=pl.DeviceIdType.MESH
        )

    index_load = pltpu.make_async_copy(tab.at[pl.ds(0, 8)], ix, tab_sem.at[0])
    meta_load = pltpu.make_async_copy(tab.at[pl.ds(8, meta_out.shape[0])], meta_out, tab_sem.at[1])
    index_load.start()
    meta_load.start()

    loads = [pltpu.make_async_copy(hbm[i], vm[i], load_sem.at[i]) for i in range(len(hbm))]
    for load in loads:
        load.start()

    loads[0].wait()
    to_tiles(mask)

    in_cells[pl.ds(me * direct, direct)] = jnp.zeros((direct, 32, 128), jnp.float32)
    index_load.wait()
    meta_load.wait()

    @pl.loop(0, EXTRA, unroll=4)
    def _(o):
        x = tiles[ix[3, CELLS + o]]
        for q in range(RELAYS):
            out_ov[q, o] = x[8 * q : 8 * q + 8]

    pl.semaphore_wait(barrier, n + slabs - 2)

    def to_relay(q, source):
        where = {"device_id": {"tile": first + 2 * q}, "device_id_type": pl.DeviceIdType.MESH}
        return (
            pltpu.make_async_remote_copy(
                src_ref=meta_out, dst_ref=meta_in.at[source],
                send_sem=meta_send.at[q], recv_sem=meta_recv.at[source], **where,
            ),
            pltpu.make_async_remote_copy(
                src_ref=out_ov.at[q], dst_ref=in_ov.at[pl.ds(source * EXTRA, EXTRA)],
                send_sem=ov_send.at[q], recv_sem=ov_recv.at[source], **where,
            ),
        )

    for q in range(RELAYS):
        @pl.when(me != first + 2 * q)
        def _():
            for copy in to_relay(q, me):
                copy.start()

    def cell_copy(k):
        to = peer_of(k)
        return pltpu.make_async_remote_copy(
            src_ref=out_cells.at[to], dst_ref=in_cells.at[pl.ds(me * direct, direct)],
            send_sem=cell_send.at[k], recv_sem=cell_recv.at[k],
            device_id={"tile": to}, device_id_type=pl.DeviceIdType.MESH,
        )

    cuts = [(n - 1) * c // 15 for c in (0,) + CUTS + (15,)]

    def offset_of(j):
        return jnp.where(lax.rem(j, 2) == 0, n // 2 + j // 2, n // 2 - 1 - j // 2)

    def pack(k):
        to = peer_of(k)
        for r in range(direct):
            out_cells[to, r] = tiles[ix[0, to * cap + r]]

    def start_cells(stage):
        @pl.loop(cuts[stage], cuts[stage + 1])
        def _(j):
            cell_copy(offset_of(j)).start()

    @pl.loop(cuts[0], cuts[1])
    def _(j):
        pack(offset_of(j))
        cell_copy(offset_of(j)).start()

    @pl.loop(cuts[1], n - 1)
    def _(j):
        pack(offset_of(j))

    for load in loads[1:]:
        load.wait()

    zero = jnp.zeros((32, 128), jnp.float32)
    lane_sign = jnp.where(lane % 64 < 32, -1.0, 1.0)

    @pl.loop(0, SIDE)
    def _(a):
        c, s = ph_x[0, a], ph_x[1, a]
        for b in range(SIDE):
            cb, sb = ph_y[0, b : b + 1, :], ph_y[1, b : b + 1, :]
            pc[a * 8 + b] = c * cb - s * sb
            ps[a * 8 + b] = (s * cb + c * sb) * lane_sign

    pc[CELLS] = zero
    ps[CELLS] = zero

    lxt_pair = lxt[0], lxt[1]
    for g in range(2):
        vv[g] = dot3(lxt_pair, halves(mask[256 * g : 256 * g + 256, :]))
    for g in range(2):
        for c in range(2):
            cols = slice(256 * c, 256 * c + 256)
            left = jnp.concatenate([vv[g, 0:256, cols], vv[g, 256:512, cols]], axis=1)
            plane[256 * g : 256 * g + 256, cols] = dot3(halves(left), (by[0], by[1]), ((1,), (1,)))
    to_tiles(plane)

    top[n] = zero
    bot[0] = zero

    @pl.loop(0, n, unroll=2)
    def _(t):
        sums = [zero] * 6
        for r in range(cap):
            s = t * cap + r
            x = tiles[ix[0, s]]
            p = ix[1, s]
            u, w = x * pc[p], x * ps[p]
            wt = jnp.where(p < 8, 1.0, 0.0)
            wb = jnp.where(p >= 56, 1.0, 0.0)
            sums = [
                sums[0] + u, sums[1] + w, sums[2] + wt * u, sums[3] + wt * w,
                sums[4] + wb * u, sums[5] + wb * w,
            ]
        wide[t] = sums[0] + swap(sums[1])
        top[t] = sums[2] + swap(sums[3])
        bot[t + 1] = sums[4] + swap(sums[5])

    def own_row(a, carry):
        u, w = carry
        for b in range(8):
            x = tiles[a * 8 + b]
            u, w = u + x * pc[a * 8 + b], w + x * ps[a * 8 + b]
        return u, w

    u0, w0 = own_row(0, (zero, zero))
    u7, w7 = own_row(7, (zero, zero))
    u, w = lax.fori_loop(1, 7, own_row, (u0 + u7, w0 + w7))
    wide[me] += u + swap(w)
    top[me] += u0 + swap(w0)
    bot[me + 1] += u7 + swap(w7)

    @pl.loop(0, n, unroll=4)
    def _(t):
        tp = jnp.where(low, top[t + 1], 0.0)
        bt = jnp.where(low, 0.0, bot[t])
        tp = tp + pltpu.roll(tp, 64, 1)
        bt = bt + pltpu.roll(bt, 64, 1)
        x = wide[t]
        x = x + pltpu.roll(x, 64, 1)
        both = (tp + bt) * sh[0] + pltpu.roll((bt - tp), 32, 1) * sh[1]
        part[place(t)] = compact(x + both)

    def spec_copy(k):
        to = jnp.bitwise_xor(chip, k)
        return pltpu.make_async_remote_copy(
            src_ref=part.at[core * chips + to], dst_ref=spec_in.at[chip],
            send_sem=spec_send.at[k], recv_sem=spec_recv.at[k],
            device_id={"tile": 2 * to + core}, device_id_type=pl.DeviceIdType.MESH,
        )

    other = pl.ds((1 - core) * chips, chips)
    share = pltpu.make_async_remote_copy(
        src_ref=part.at[other], dst_ref=shared, send_sem=spec_send.at[0], recv_sem=spec_recv.at[0],
        device_id={"tile": jnp.bitwise_xor(me, 1)}, device_id_type=pl.DeviceIdType.MESH,
    )
    share.start()
    share.wait_recv()
    own_part = pl.ds(core * chips, chips)
    part[own_part] = part[own_part] + shared[...]

    @pl.loop(1, chips)
    def _(k):
        spec_copy(k).start()

    start_cells(1)

    def flag_copy(k):
        to = lax.rem(slab + k, slabs)
        return pltpu.make_async_remote_copy(
            src_ref=flag_mine, dst_ref=flag_in.at[k],
            send_sem=flag_send.at[k], recv_sem=flag_recv.at[k],
            device_id={"slab": to}, device_id_type=pl.DeviceIdType.MESH,
        )

    def hop_copy(k, source):
        to = peer_of(k)
        return pltpu.make_async_remote_copy(
            src_ref=out2.at[to], dst_ref=in2.at[source],
            send_sem=hop_send.at[k], recv_sem=hop_recv.at[source],
            device_id={"tile": to}, device_id_type=pl.DeviceIdType.MESH,
        )

    spec_in[chip] = part[core * chips + chip]

    for k in range(KERNELS):
        rows = slice(32 * k, 32 * k + 32)
        re, im = kraw[64 * k : 64 * k + 32, :], kraw[64 * k + 32 : 64 * k + 64, :]
        kr[rows, :] = jnp.concatenate([re] * 4, axis=1)
        ki[rows, :] = jnp.concatenate([-im, im] * 2, axis=1)

    @pl.loop(1, chips)
    def _(k):
        spec_copy(k).wait_recv()

    start_cells(2)
    spec = expand(sum((spec_in[t] for t in range(1, chips)), spec_in[0]))

    spec_s = pltpu.roll(spec, 32, 1)
    for k in range(KERNELS):
        rows = slice(32 * k, 32 * k + 32)
        stack[rows, :] = spec * kr[rows, :] + spec_s * ki[rows, :]
    fields_y = dot(stack[...], yt[...])
    sign = jnp.where(low, -1.0, 1.0)
    for k in range(KERNELS):
        part_k = fields_y[32 * k : 32 * k + 32]
        rhs[0:32, 128 * k : 128 * k + 128] = part_k
        rhs[32:64, 128 * k : 128 * k + 128] = pltpu.roll(part_k, 64, 1) * sign
    fields = dot(x1[...], rhs[...])
    inten = jnp.zeros((64, 128), jnp.float32)
    for k in range(KERNELS):
        e = fields[:, 128 * k : 128 * k + 128]
        inten = inten + wts[k] * (e * e)
    blurred = dot(ux[...], dot(inten, uyt[...]))
    d = dose[0]
    resist = jax.nn.sigmoid(4.0 * (d * blurred - 1.0))
    slope = 2.0 * (resist - target[...]) * (4.0 * d) * resist * (1.0 - resist)
    grad_i = dot3((uxt[0], uxt[1]), halves(dot3(halves(slope), (uy2[0], uy2[1]))))
    lane2 = lax.broadcasted_iota(jnp.int32, (64, 128), 1)
    sign2 = jnp.where(lane2 < 64, 1.0, -1.0)
    for k in range(KERNELS):
        ge = (2.0 * wts[k]) * grad_i * fields[:, 128 * k : 128 * k + 128]
        rhs2[0:64, 128 * k : 128 * k + 128] = ge
        rhs2[64:128, 128 * k : 128 * k + 128] = pltpu.roll(ge, 64, 1) * sign2
    grad_y = dot(x2[...], rhs2[...])
    for k in range(KERNELS):
        stack[32 * k : 32 * k + 32, :] = grad_y[:, 128 * k : 128 * k + 128]
    grad_a = dot(stack[...], y2[...])
    acc = zero
    for k in range(KERNELS):
        rows = slice(32 * k, 32 * k + 32)
        ga = grad_a[rows]
        acc = acc + kr[rows, :] * ga - ki[rows, :] * pltpu.roll(ga, 32, 1)
    acc_all[place(me)] = compact(acc)

    def acc_copy(k):
        to = jnp.bitwise_xor(chip, k)
        return pltpu.make_async_remote_copy(
            src_ref=acc_all.at[place(me)], dst_ref=acc_all.at[place(me)],
            send_sem=acc_send.at[k], recv_sem=acc_recv.at[k],
            device_id={"tile": 2 * to + core}, device_id_type=pl.DeviceIdType.MESH,
        )

    @pl.loop(1, chips)
    def _(k):
        acc_copy(k).start()

    start_cells(3)

    @pl.when(is_relay)
    def _():
        meta_in[me] = meta_out[...]
        in_ov[pl.ds(me * EXTRA, EXTRA)] = out_ov[relay]

        @pl.loop(1, n)
        def _(k):
            for copy in to_relay(0, peer_of(k)):
                copy.wait_recv()

        lines = n // 8
        slot = lax.broadcasted_iota(jnp.int32, (lines, 128), 1) % 16
        start = jnp.zeros((lines, 128), jnp.int32)
        found = jnp.zeros((lines, 128), jnp.int32)
        most = jnp.zeros((lines, 128), jnp.int32)
        for i in range(n):
            count, offset = meta_in[i, 0:lines], meta_in[i, lines : 2 * lines]
            rel = slot - start
            found = jnp.where((rel >= 0) & (rel < count), i * EXTRA + offset + rel, found)
            start = start + count
            most = jnp.maximum(most, count + offset)
        route_v[...] = jnp.zeros((8, 128), jnp.int32)
        route_v[0:lines] = jnp.clip(found, 0, n * EXTRA - 1)
        over = jnp.broadcast_to(jnp.max(jnp.where(most > EXTRA, 1.0, 0.0)), (8, 128))
        route_copy = pltpu.make_async_copy(route_v, route, tab_sem.at[2])
        route_copy.start()
        flag_mine[...] = over

        @pl.when(me == first)
        def _():
            for k in range(1, slabs):
                flag_copy(k).start()

        route_copy.wait()

        @pl.loop(0, n)
        def _(d):
            for m in range(EXTRA):
                out2[d, m] = in_ov[route[d // 8, lax.rem(d, 8) * 16 + m]]

        flag_in[0] = over

        @pl.when(me == first)
        def _():
            for k in range(1, slabs):
                flag_copy(k).wait()
                flag_in[0] = jnp.maximum(flag_in[0], flag_in[k])

        @pl.loop(0, n)
        def _(d):
            out2[d, EXTRA] = flag_in[0]

        @pl.loop(1, n)
        def _(k):
            hop_copy(k, relay).start()

        in2[relay] = out2[me]

    @pl.loop(1, chips)
    def _(k):
        acc_copy(k).wait_recv()

    give = pltpu.make_async_remote_copy(
        src_ref=acc_all.at[own_part], dst_ref=acc_all.at[own_part],
        send_sem=acc_send.at[0], recv_sem=acc_recv.at[0],
        device_id={"tile": jnp.bitwise_xor(me, 1)}, device_id_type=pl.DeviceIdType.MESH,
    )
    give.start()
    give.wait_recv()

    start_cells(4)

    @pl.loop(0, n, unroll=4)
    def _(t):
        mid = expand(acc_all[place(t)])
        before = expand(acc_all[place(jnp.maximum(t - 1, 0))]) * jnp.where(t > 0, 1.0, 0.0)
        after = expand(acc_all[place(jnp.minimum(t + 1, n - 1))]) * jnp.where(t < n - 1, 1.0, 0.0)
        first = mid + before * sh[0] + pltpu.roll(before, 32, 1) * sh[1]
        last = mid + after * sh[0] - pltpu.roll(after, 32, 1) * sh[1]
        mid_s, first_s, last_s = (pltpu.roll(v, 32, 1) for v in (mid, first, last))
        acc2[t * 3] = jnp.where(low, first, mid)
        acc2[t * 3 + 1] = mid
        acc2[t * 3 + 2] = jnp.where(low, mid, last)
        acc2s[t * 3] = jnp.where(low, first_s, mid_s)
        acc2s[t * 3 + 1] = mid_s
        acc2s[t * 3 + 2] = jnp.where(low, mid_s, last_s)

    @pl.loop(0, SIDE)
    def _(a):
        r = pl.multiple_of(a * 64, 64)
        own = me * 3 + jnp.where(a == 0, 0, jnp.where(a == SIDE - 1, 2, 1))
        own_x, own_s = acc2[own], acc2s[own]
        for b in range(4):
            pieces = []
            for i in range(2):
                c = a * 8 + 2 * b + i
                g, p = ix[2, CELLS + c], ix[3, c]
                pieces.append(own_x * pc[c] + own_s * ps[c] + acc2[g] * pc[p] + acc2s[g] * ps[p])
            h0, h1 = pair(*pieces)
            plane[pl.ds(r, 32), 128 * b : 128 * b + 128] = h0
            plane[pl.ds(r + 32, 32), 128 * b : 128 * b + 128] = h1

    for c in range(2):
        for g in range(2):
            v = dot3(halves(plane[256 * g : 256 * g + 256, 256 * c : 256 * c + 256]), (by[0], by[1]))
            vv[g, 0:256, 256 * c : 256 * c + 256] = v[:, 0:256]
            vv[g, 256:512, 256 * c : 256 * c + 256] = v[:, 256:512]
    for g in range(2):
        grad_out[256 * g : 256 * g + 256, :] = dot3((lx[0], lx[1]), halves(vv[g]))

    @pl.loop(1, n)
    def _(k):
        cell_copy(k).wait_recv()

    for q in range(RELAYS):
        @pl.when(me != first + 2 * q)
        def _():
            hop_copy(1, q).wait_recv()

    flag_out[0] = in2[0, EXTRA][0, 0]
    for m in range(EXTRA):
        in_cells[n * direct + m] = jnp.concatenate([in2[q, m] for q in range(RELAYS)], axis=0)

    @pl.loop(0, SIDE)
    def _(a):
        r = pl.multiple_of(a * 64, 64)
        for b in range(4):
            c = a * 8 + 2 * b
            both = pair(in_cells[ix[2, c]],
                          in_cells[ix[2, c + 1]])
            for h in range(2):
                where = (pl.ds(r + 32 * h, 32), slice(128 * b, 128 * b + 128))
                upd_out[where] = mask[where] + both[h]

    @pl.loop(1, n)
    def _(k):
        cell_copy(k).wait_send()

    @pl.loop(1, chips)
    def _(k):
        spec_copy(k).wait_send()
        acc_copy(k).wait_send()

    share.wait_send()
    give.wait_send()

    for q in range(RELAYS):
        @pl.when(me != first + 2 * q)
        def _():
            for copy in to_relay(q, me):
                copy.wait_send()

    @pl.when(is_relay)
    def _():
        @pl.loop(1, n)
        def _(k):
            hop_copy(k, relay).wait_send()


def full_body(n, cap, tab, mask_hbm, both_out, mask, ix, tiles, out_cells, in_cells, tab_sem, cell_send, cell_recv):
    me = lax.axis_index("tile")
    low = lax.broadcasted_iota(jnp.int32, (32, 128), 1) < 64

    def pair(x, y):
        rx, ry = pltpu.roll(x, 64, 1), pltpu.roll(y, 64, 1)
        return jnp.where(low, x, ry), jnp.where(low, rx, y)

    barrier = pltpu.get_barrier_semaphore()

    @pl.loop(1, n)
    def _(k):
        pl.semaphore_signal(
            barrier, inc=1, device_id={"tile": jnp.bitwise_xor(me, k)}, device_id_type=pl.DeviceIdType.MESH
        )

    index_load = pltpu.make_async_copy(tab.at[pl.ds(0, 8)], ix, tab_sem.at[0])
    index_load.start()
    mask_load = pltpu.make_async_copy(mask_hbm, mask, tab_sem.at[1])
    mask_load.start()
    mask_load.wait()

    @pl.loop(0, SIDE)
    def _(a):
        r = pl.multiple_of(a * 64, 64)
        for b in range(4):
            h0 = mask[pl.ds(r, 32), 128 * b : 128 * b + 128]
            h1 = mask[pl.ds(r + 32, 32), 128 * b : 128 * b + 128]
            tiles[a * 8 + 2 * b], tiles[a * 8 + 2 * b + 1] = pair(h0, h1)

    index_load.wait()

    @pl.loop(0, n)
    def _(to):
        for r in range(cap):
            out_cells[to, r] = tiles[ix[0, to * cap + r]]

    in_cells[pl.ds(me * cap, cap)] = out_cells[me]
    pl.semaphore_wait(barrier, n - 1)

    def cell_copy(k):
        to = jnp.bitwise_xor(me, k)
        return pltpu.make_async_remote_copy(
            src_ref=out_cells.at[to], dst_ref=in_cells.at[pl.ds(me * cap, cap)],
            send_sem=cell_send.at[k], recv_sem=cell_recv.at[k],
            device_id={"tile": to}, device_id_type=pl.DeviceIdType.MESH,
        )

    @pl.loop(1, n)
    def _(k):
        cell_copy(k).start()

    @pl.loop(1, n)
    def _(k):
        cell_copy(k).wait()

    @pl.loop(0, SIDE)
    def _(a):
        r = pl.multiple_of(a * 64, 64)
        for b in range(4):
            c = a * 8 + 2 * b
            halves_of = pair(in_cells[ix[4, c]], in_cells[ix[4, c + 1]])
            for h in range(2):
                where = (pl.ds(r + 32 * h, 32), slice(128 * b, 128 * b + 128))
                both_out[where] = mask[where] + halves_of[h]


def full_exchange(n, cap, tab, mask):
    f32 = jnp.float32
    dma = pltpu.SemaphoreType.DMA((n,))
    vmem = pl.BlockSpec(memory_space=pltpu.VMEM)
    return pl.pallas_call(
        functools.partial(full_body, n, cap),
        out_shape=jax.ShapeDtypeStruct((TILE, TILE), f32),
        in_specs=[pl.BlockSpec(memory_space=pl.ANY), pl.BlockSpec(memory_space=pltpu.HBM)],
        out_specs=vmem,
        scratch_shapes=[
            pltpu.VMEM((TILE, TILE), f32),
            pltpu.SMEM((8, 128), jnp.int32),
            pltpu.VMEM((CELLS, 32, 128), f32),
            pltpu.VMEM((n, cap, 32, 128), f32),
            pltpu.VMEM((n * cap, 32, 128), f32),
            pltpu.SemaphoreType.DMA((2,)),
            dma, dma,
        ],
        compiler_params=pltpu.CompilerParams(
            collective_id=1, has_side_effects=True, vmem_limit_bytes=32 * 1024 * 1024
        ),
    )(tab, mask)


def local(consts, mask, target, partner, kernels, socs_weights, dose):
    n = lax.axis_size("tile")
    cap = 2 * CELLS // n
    owner = partner // CELLS
    pos = partner % CELLS
    ids = jnp.arange(CELLS, dtype=jnp.int32)
    same = owner[:, None] == owner[None, :]
    send_rank = jnp.sum((same & (pos[None, :] < pos[:, None])).astype(jnp.int32), axis=1)
    recv_rank = jnp.sum((same & (ids[None, :] < ids[:, None])).astype(jnp.int32), axis=1)
    send_slot = owner * cap + send_rank
    recv_slot = owner * cap + recv_rank
    hit = (jnp.arange(n * cap, dtype=jnp.int32)[:, None] == send_slot[None, :]).astype(jnp.int32)
    slot_cell = jnp.sum(hit * ids[None, :], axis=1)
    slot_pos = CELLS + jnp.sum(hit * (pos - CELLS)[None, :], axis=1)
    row = pos // SIDE
    kind = jnp.where(row == 0, 0, jnp.where(row == SIDE - 1, 2, 1))
    direct = cap // 2
    spare = send_rank >= direct
    ahead = jnp.sum((spare[None, :] & (owner[None, :] < owner[:, None])).astype(jnp.int32), axis=1)
    recv_index = jnp.where(
        recv_rank < direct, owner * direct + recv_rank,
        n * direct + jnp.minimum(ahead + recv_rank - direct, EXTRA - 1),
    )
    spare_slot = jnp.where(spare, ahead + send_rank - direct, -1)
    spare_cell = jnp.sum((ids[:, None] == spare_slot[None, :]).astype(jnp.int32) * ids[None, :], axis=1)
    dest = (jnp.arange(16 * n, dtype=jnp.int32) // 16)[:, None]
    count = jnp.sum((spare[None, :] & (owner[None, :] == dest)).astype(jnp.int32), axis=1)
    offset = jnp.sum((spare[None, :] & (owner[None, :] < dest)).astype(jnp.int32), axis=1)
    meta_lines = (2 * n // 8 + 7) // 8 * 8
    tab = jnp.concatenate(
        [slot_cell, slot_pos, recv_index, owner * 3 + kind, pos, spare_cell, recv_slot, recv_slot]
        + [jnp.zeros((3 * 128,), jnp.int32), count, offset, jnp.zeros((128 * meta_lines - 32 * n,), jnp.int32)]
    ).reshape(-1, 128)
    raw = kernels.reshape(2 * KERNELS * BAND, BAND)
    f32 = jnp.float32
    vmem = pl.BlockSpec(memory_space=pltpu.VMEM)
    hbm = pl.BlockSpec(memory_space=pltpu.HBM)
    arrays = [mask, target, raw, *consts]
    smem = pl.BlockSpec(memory_space=pltpu.SMEM)
    dma, few = pltpu.SemaphoreType.DMA((n,)), pltpu.SemaphoreType.DMA((RELAYS,))
    flags = pltpu.SemaphoreType.DMA((lax.axis_size("slab"),))
    twice, both, flag = pl.pallas_call(
        functools.partial(body, n, cap, len(arrays)),
        out_shape=(jax.ShapeDtypeStruct((TILE, TILE), f32),) * 2 + (jax.ShapeDtypeStruct((1,), f32),),
        in_specs=[smem] * 2 + [pl.BlockSpec(memory_space=pl.ANY)] + [hbm] * len(arrays),
        out_specs=(vmem, vmem, smem),
        scratch_shapes=[pltpu.VMEM(x.shape, x.dtype) for x in arrays] + [
            pltpu.SemaphoreType.DMA((len(arrays),)),
            pltpu.VMEM((CELLS + 1, 32, 128), f32),
            pltpu.VMEM((CELLS + 1, 32, 128), f32),
            pltpu.VMEM((n, direct, 32, 128), f32),
            pltpu.VMEM((n * direct + EXTRA, 32, 128), f32),
            pltpu.VMEM((CELLS, 32, 128), f32),
            pltpu.VMEM((TILE, TILE), f32),
            pltpu.VMEM((2, 512, 512), f32),
            pltpu.VMEM((n, 32, 128), f32),
            pltpu.VMEM((n, 16, 128), f32),
            pltpu.VMEM((n // 2, 16, 128), f32),
            pltpu.VMEM((n + 1, 32, 128), f32),
            pltpu.VMEM((n + 1, 32, 128), f32),
            pltpu.VMEM((n, 16, 128), f32),
            pltpu.VMEM((n, 16, 128), f32),
            pltpu.VMEM((3 * n, 32, 128), f32),
            pltpu.VMEM((3 * n, 32, 128), f32),
            pltpu.VMEM((64, 768), f32),
            pltpu.VMEM((128, 768), f32),
            pltpu.VMEM((192, 128), f32),
            pltpu.VMEM((192, 128), f32),
            pltpu.VMEM((192, 128), f32),
            pltpu.SMEM((8, 128), jnp.int32),
            pltpu.SemaphoreType.DMA((3,)),
            pltpu.VMEM((RELAYS, EXTRA, 8, 128), f32),
            pltpu.VMEM((n * EXTRA, 8, 128), f32),
            pltpu.VMEM((n, EXTRA + 1, 8, 128), f32),
            pltpu.VMEM((RELAYS, EXTRA + 1, 8, 128), f32),
            pltpu.VMEM((meta_lines, 128), jnp.int32),
            pltpu.VMEM((n, meta_lines, 128), jnp.int32),
            pltpu.VMEM((8, 128), jnp.int32),
            pltpu.SMEM((8, 128), jnp.int32),
            pltpu.VMEM((8, 128), f32),
            pltpu.VMEM((lax.axis_size("slab"), 8, 128), f32),
            few, dma, few, dma, dma, few, flags, flags,
            dma, dma, dma, dma, dma, dma,
        ],
        compiler_params=pltpu.CompilerParams(
            collective_id=0, has_side_effects=True, vmem_limit_bytes=VMEM_LIMIT
        ),
    )(socs_weights, dose, tab, *arrays)
    def finish(g, b):
        return 0.5 * g, 0.5 * (b - 0.1 * g)

    return lax.cond(
        flag[0] > 0.5,
        lambda t, m, g, b: finish(g, full_exchange(n, cap, t, m)),
        lambda t, m, g, b: finish(g, b),
        tab, mask, twice, both,
    )


def solution(mesh):
    consts = tables()

    def run(mask, target, partner, kernels, socs_weights, dose):
        return local([jnp.asarray(t) for t in consts], mask, target, partner, kernels, socs_weights, dose)

    return jax.shard_map(
        run,
        mesh=mesh,
        in_specs=(
            P(("slab", "tile"), None),
            P(("slab", "tile"), None),
            P(("slab", "tile")),
            P(),
            P(),
            P(),
        ),
        out_specs=(P(("slab", "tile"), None), P(("slab", "tile"), None)),
        check_vma=False,
    )
```

```python
import functools
import math

import numpy as np
import jax
import jax.numpy as jnp
from jax import lax
from jax.experimental import pallas as pl
from jax.experimental.pallas import tpu as pltpu
from jax.sharding import PartitionSpec as P

TILE = 512
CELL = 64
MARGIN = 32
BAND = 32
CELLS = 64
SIDE = 8
DOMAIN = 576
GRID = 64
KERNELS = 6
CUTS = (4, 7, 10, 15)
EXTRA = 12
RELAYS = 4
VMEM_LIMIT = 56 * 1024 * 1024
HIGHEST = lax.Precision.HIGHEST
BLUR = (0.0625, 0.25, 0.375, 0.25, 0.0625)


def tables():
    f = np.arange(BAND) - BAND // 2
    norm = 0.5 / math.sqrt(DOMAIN * TILE)
    ph_x = np.zeros((2, SIDE, BAND, 128))
    for h in range(2):
        ang = 2 * np.pi * np.outer(1 + 2 * np.arange(SIDE) + h, f) / 18.0
        ph_x[0, :, :, 64 * h : 64 * h + 64] = norm * np.cos(ang)[:, :, None]
        ph_x[1, :, :, 64 * h : 64 * h + 64] = norm * np.sin(ang)[:, :, None]
    ang = 2 * np.pi * np.outer(np.arange(SIDE), f) / 8.0
    ph_y = np.stack([np.tile(np.cos(ang), (1, 4)), np.tile(np.sin(ang), (1, 4))])
    ang = 2 * np.pi * f * 16 / 18.0
    one = np.ones((1, 32))
    cos16, sin16 = np.cos(ang)[:, None] * one, np.sin(ang)[:, None] * one
    sh = np.stack(
        [np.concatenate([cos16] * 4, 1), np.concatenate([-sin16, sin16] * 2, 1)]
    )
    q = np.arange(CELL)
    cy = np.cos(2 * np.pi * np.outer(f, q) / TILE)
    sy = np.sin(2 * np.pi * np.outer(f, q) / TILE)
    by = np.zeros((256, 512))
    for i in range(4):
        r, o = 64 * i, 64 * i
        by[r : r + 32, o : o + 64] = cy
        by[r : r + 32, 256 + o : 256 + o + 64] = sy
        by[r + 32 : r + 64, o : o + 64] = -sy
        by[r + 32 : r + 64, 256 + o : 256 + o + 64] = cy
    r32 = np.arange(32)
    cx = np.cos(2 * np.pi * np.outer(r32, f) / DOMAIN)
    sx = np.sin(2 * np.pi * np.outer(r32, f) / DOMAIN)
    lx = np.zeros((256, 512))
    for j in range(8):
        k = 32 * j
        lx[k : k + 32, k : k + 32] = cx
        lx[k : k + 32, 256 + k : 256 + k + 32] = -sx
    m = np.arange(GRID)
    c = np.cos(2 * np.pi * np.outer(f, m) / GRID)
    s = np.sin(2 * np.pi * np.outer(f, m) / GRID)
    yt = np.zeros((128, 128))
    yt[:32, :64], yt[:32, 64:], yt[32:64, :64], yt[32:64, 64:] = c, s, -s, c
    x1 = np.concatenate([c.T, s.T], 1) / BAND
    x2 = np.concatenate([c, s], 1) / BAND
    y2 = np.zeros((128, 128))
    half = np.concatenate([np.concatenate([c.T, -s.T], 1), np.concatenate([s.T, c.T], 1)], 0)
    y2[:, :64], y2[:, 64:] = half, half
    g = np.arange(-31, 32)

    def interp(extent):
        d = np.arange(extent)[:, None] / extent - m[None, :] / GRID
        return np.cos(2 * np.pi * g[:, None, None] * d[None]).sum(0) / GRID

    ux = interp(DOMAIN)
    ux = sum(BLUR[i] * ux[MARGIN - 2 + i : MARGIN - 2 + i + TILE] for i in range(5))
    uy = interp(TILE)
    uy = sum(BLUR[i] * np.roll(uy, i - 2, axis=0) for i in range(5))
    uyt = np.concatenate([uy.T, uy.T], 0)
    uy2 = np.concatenate([uy, uy], 1)
    whole = [ph_x, ph_y, sh, yt, x1, x2, y2, ux, uyt]
    return [np.ascontiguousarray(t, dtype=np.float32) for t in whole] + [
        split(np.ascontiguousarray(t, dtype=np.float32)) for t in (by, 2 * lx, lx.T, ux.T, uy2)
    ]


def split(t):
    hi = t.astype(jnp.bfloat16)
    return np.stack([hi, (t - hi.astype(np.float32)).astype(jnp.bfloat16)])


def dot(x, y):
    return jnp.dot(x, y, precision=HIGHEST, preferred_element_type=jnp.float32)


def halves(x):
    hi = x.astype(jnp.bfloat16)
    return hi, (x - hi.astype(jnp.float32)).astype(jnp.bfloat16)


def dot3(x, y, dims=((1,), (0,))):
    def one(p, q):
        return lax.dot_general(p, q, (dims, ((), ())), preferred_element_type=jnp.float32)

    return one(x[0], y[0]) + (one(x[0], y[1]) + one(x[1], y[0]))


def build_tables(n, cap, mates, index_out, meta_out):
    direct, lines = cap // 2, n // 8
    row = jnp.concatenate([mates[...], mates[...]], axis=1)
    square = jnp.broadcast_to(row, (128, 128))
    across, down = square[0:CELLS], square.T[0:CELLS]
    lane = lax.broadcasted_iota(jnp.int32, (CELLS, 128), 1)
    cell = lax.broadcasted_iota(jnp.int32, (CELLS, 128), 0)
    own_r, pos_r, own_c, pos_c = across >> 6, across & 63, down >> 6, down & 63
    valid = lane < CELLS

    def over_cells(mask):
        return jnp.sum(jnp.where(mask, 1, 0), axis=0, keepdims=True)

    def over_lanes(mask):
        return jnp.sum(jnp.where(mask & valid, 1, 0), axis=1, keepdims=True)

    same = own_r == own_c
    rank_r = over_cells(same & (pos_c < pos_r))
    recv_r = over_cells(same & (cell < lane))
    rank_c = over_lanes(same & (pos_r < pos_c))
    spare_c = jnp.broadcast_to(rank_c, (CELLS, 128)) >= direct
    spare_r = jnp.broadcast_to(rank_r, (CELLS, 128)) >= direct
    ahead_r = over_cells(spare_c & (own_c < own_r))
    ahead_c = over_lanes(spare_r & (own_r < own_c))
    hit = own_c * cap + rank_c == lane
    own, pos, first = own_r[0:1], pos_r[0:1], lane[0:1] < CELLS
    kind = jnp.where(pos < SIDE, 0, jnp.where(pos >= CELLS - SIDE, 2, 1))
    recv = jnp.where(
        recv_r < direct, own * direct + recv_r,
        n * direct + jnp.minimum(ahead_r + recv_r - direct, EXTRA - 1),
    )
    index_out[0:1] = jnp.max(jnp.where(hit, cell, 0), axis=0, keepdims=True)
    index_out[1:2] = jnp.min(jnp.where(hit, pos_c, CELLS), axis=0, keepdims=True)
    index_out[2:3] = jnp.where(first, recv, own * 3 + kind)
    index_out[3:4] = jnp.where(
        first, pos,
        jnp.max(jnp.where(spare_c & (ahead_c + rank_c - direct == lane - CELLS), cell, 0), axis=0, keepdims=True),
    )
    index_out[4:8] = jnp.zeros((4, 128), jnp.int32)
    meta_out[...] = jnp.zeros(meta_out.shape, jnp.int32)
    for h in range(lines):
        dest = (lane + 128 * h) >> 4
        meta_out[h : h + 1] = over_cells(spare_c & (own_c == dest))
        meta_out[lines + h : lines + h + 1] = over_cells(spare_c & (own_c < dest))


def body(n, cap, n_in, wts, dose, tab, *refs):
    hbm, outs = refs[:n_in], refs[n_in : n_in + 3]
    vm = refs[n_in + 3 : 2 * n_in + 3]
    load_sem = refs[2 * n_in + 3]
    (
        mask, target, kraw, ph_x, ph_y, sh, yt, x1, x2, y2, ux, uyt, by, lx, lxt, uxt, uy2
    ) = vm
    main(n, cap, tab, wts, dose, hbm, vm, load_sem,
         mask, target, kraw, ph_x, ph_y, sh, yt, x1, x2, y2, ux, uyt, by, lx, lxt, uxt, uy2,
         *outs, *refs[2 * n_in + 4 :])


def main(
    n, cap, tab, wts, dose, hbm, vm, load_sem,
    mask, target, kraw, ph_x, ph_y, sh, yt, x1, x2, y2, ux, uyt, by, lx, lxt, uxt, uy2,
    grad_out, upd_out, flag_out, pc, ps,
    out_cells, in_cells, tiles, plane, vv, wide, part, shared, top, bot, spec_in, acc_all, acc2, acc2s, rhs, rhs2, stack,
    kr, ki, mates, ix_v, ix, tab_sem, mask_sem, out_ov, in_ov, out2, in2, meta_out, meta_in, route_v, route, flag_mine, flag_in,
    ov_send, ov_recv, meta_send, meta_recv, hop_send, hop_recv, flag_send, flag_recv,
    cell_send, cell_recv, spec_send, spec_recv, acc_send, acc_recv,
):
    me = lax.axis_index("tile")
    lane = lax.broadcasted_iota(jnp.int32, (32, 128), 1)
    low = lane < 64
    slabs = lax.axis_size("slab")
    slab = lax.axis_index("slab")
    direct = cap // 2
    first = n // 4
    relay = (me - first) // 2
    is_relay = (me >= first) & (me < first + 2 * RELAYS) & (lax.rem(me, 2) == 0)

    def swap(x):
        return jnp.where(lane % 64 < 32, pltpu.roll(x, 96, 1), pltpu.roll(x, 32, 1))

    def pair(x, y):
        rx, ry = pltpu.roll(x, 64, 1), pltpu.roll(y, 64, 1)
        return jnp.where(low, x, ry), jnp.where(low, rx, y)

    def to_tiles(src, start=0, stop=SIDE):
        @pl.loop(start, stop)
        def _(a):
            r = pl.multiple_of(a * 64, 64)
            for b in range(4):
                h0 = src[pl.ds(r, 32), 128 * b : 128 * b + 128]
                h1 = src[pl.ds(r + 32, 32), 128 * b : 128 * b + 128]
                x, y = pair(h0, h1)
                tiles[a * 8 + 2 * b] = x
                tiles[a * 8 + 2 * b + 1] = y

    def compact(x):
        return jnp.where(low[0:16], x[0:16], x[16:32])

    def expand(x):
        r = pltpu.roll(x, 64, 1)
        return jnp.concatenate([jnp.where(low[0:16], x, r), jnp.where(low[0:16], r, x)], axis=0)

    chips = n // 2
    core = lax.rem(me, 2)
    chip = me // 2

    def place(t):
        return lax.rem(t, 2) * chips + t // 2

    def peer_of(k):
        return jnp.bitwise_xor(me, k)

    barrier = pltpu.get_barrier_semaphore()

    partner_load = pltpu.make_async_copy(tab, mates, tab_sem.at[1])
    partner_load.start()
    rows = TILE // 4
    mask_loads = [
        pltpu.make_async_copy(hbm[0].at[pl.ds(rows * c, rows)], mask.at[pl.ds(rows * c, rows)], mask_sem.at[c])
        for c in range(4)
    ]
    for load in mask_loads:
        load.start()

    @pl.loop(1, n)
    def _(k):
        pl.semaphore_signal(barrier, inc=1, device_id={"tile": peer_of(k)}, device_id_type=pl.DeviceIdType.MESH)

    for k in range(1, slabs):
        pl.semaphore_signal(
            barrier, inc=1, device_id={"slab": lax.rem(slab + k, slabs)}, device_id_type=pl.DeviceIdType.MESH
        )

    loads = [pltpu.make_async_copy(hbm[i], vm[i], load_sem.at[i]) for i in range(1, len(hbm))]
    for load in loads:
        load.start()

    partner_load.wait()
    build_tables(n, cap, mates, ix_v, meta_out)
    index_load = pltpu.make_async_copy(ix_v, ix, tab_sem.at[0])
    index_load.start()

    for c in range(4):
        mask_loads[c].wait()
        to_tiles(mask, 2 * c, 2 * c + 2)

    in_cells[pl.ds(me * direct, direct)] = jnp.zeros((direct, 32, 128), jnp.float32)
    index_load.wait()

    @pl.loop(0, EXTRA, unroll=4)
    def _(o):
        x = tiles[ix[3, CELLS + o]]
        for q in range(RELAYS):
            out_ov[q, o] = x[8 * q : 8 * q + 8]

    pl.semaphore_wait(barrier, n + slabs - 2)

    def to_relay(q, source):
        where = {"device_id": {"tile": first + 2 * q}, "device_id_type": pl.DeviceIdType.MESH}
        return (
            pltpu.make_async_remote_copy(
                src_ref=meta_out, dst_ref=meta_in.at[source],
                send_sem=meta_send.at[q], recv_sem=meta_recv.at[source], **where,
            ),
            pltpu.make_async_remote_copy(
                src_ref=out_ov.at[q], dst_ref=in_ov.at[pl.ds(source * EXTRA, EXTRA)],
                send_sem=ov_send.at[q], recv_sem=ov_recv.at[source], **where,
            ),
        )

    for q in range(RELAYS):
        @pl.when(me != first + 2 * q)
        def _():
            for copy in to_relay(q, me):
                copy.start()

    def cell_copy(k):
        to = peer_of(k)
        return pltpu.make_async_remote_copy(
            src_ref=out_cells.at[to], dst_ref=in_cells.at[pl.ds(me * direct, direct)],
            send_sem=cell_send.at[k], recv_sem=cell_recv.at[k],
            device_id={"tile": to}, device_id_type=pl.DeviceIdType.MESH,
        )

    cuts = [(n - 1) * c // 15 for c in (0,) + CUTS + (15,)]

    def offset_of(j):
        return jnp.where(lax.rem(j, 2) == 0, n // 2 + j // 2, n // 2 - 1 - j // 2)

    def pack(k):
        to = peer_of(k)
        for r in range(direct):
            out_cells[to, r] = tiles[ix[0, to * cap + r]]

    def start_cells(stage):
        @pl.loop(cuts[stage], cuts[stage + 1])
        def _(j):
            cell_copy(offset_of(j)).start()

    @pl.loop(cuts[0], cuts[1])
    def _(j):
        pack(offset_of(j))
        cell_copy(offset_of(j)).start()

    @pl.loop(cuts[1], n - 1)
    def _(j):
        pack(offset_of(j))

    for load in loads:
        load.wait()

    zero = jnp.zeros((32, 128), jnp.float32)
    lane_sign = jnp.where(lane % 64 < 32, -1.0, 1.0)

    @pl.loop(0, SIDE)
    def _(a):
        c, s = ph_x[0, a], ph_x[1, a]
        for b in range(SIDE):
            cb, sb = ph_y[0, b : b + 1, :], ph_y[1, b : b + 1, :]
            pc[a * 8 + b] = c * cb - s * sb
            ps[a * 8 + b] = (s * cb + c * sb) * lane_sign

    pc[CELLS] = zero
    ps[CELLS] = zero

    lxt_pair = lxt[0], lxt[1]
    for g in range(2):
        vv[g] = dot3(lxt_pair, halves(mask[256 * g : 256 * g + 256, :]))
    for g in range(2):
        for c in range(2):
            cols = slice(256 * c, 256 * c + 256)
            left = jnp.concatenate([vv[g, 0:256, cols], vv[g, 256:512, cols]], axis=1)
            plane[256 * g : 256 * g + 256, cols] = dot3(halves(left), (by[0], by[1]), ((1,), (1,)))
    to_tiles(plane)

    top[n] = zero
    bot[0] = zero

    @pl.loop(0, n, unroll=2)
    def _(t):
        sums = [zero] * 6
        for r in range(cap):
            s = t * cap + r
            x = tiles[ix[0, s]]
            p = ix[1, s]
            u, w = x * pc[p], x * ps[p]
            wt = jnp.where(p < 8, 1.0, 0.0)
            wb = jnp.where(p >= 56, 1.0, 0.0)
            sums = [
                sums[0] + u, sums[1] + w, sums[2] + wt * u, sums[3] + wt * w,
                sums[4] + wb * u, sums[5] + wb * w,
            ]
        wide[t] = sums[0] + swap(sums[1])
        top[t] = sums[2] + swap(sums[3])
        bot[t + 1] = sums[4] + swap(sums[5])

    def own_row(a, carry):
        u, w = carry
        for b in range(8):
            x = tiles[a * 8 + b]
            u, w = u + x * pc[a * 8 + b], w + x * ps[a * 8 + b]
        return u, w

    u0, w0 = own_row(0, (zero, zero))
    u7, w7 = own_row(7, (zero, zero))
    u, w = lax.fori_loop(1, 7, own_row, (u0 + u7, w0 + w7))
    wide[me] += u + swap(w)
    top[me] += u0 + swap(w0)
    bot[me + 1] += u7 + swap(w7)

    @pl.loop(0, n, unroll=4)
    def _(t):
        tp = jnp.where(low, top[t + 1], 0.0)
        bt = jnp.where(low, 0.0, bot[t])
        tp = tp + pltpu.roll(tp, 64, 1)
        bt = bt + pltpu.roll(bt, 64, 1)
        x = wide[t]
        x = x + pltpu.roll(x, 64, 1)
        both = (tp + bt) * sh[0] + pltpu.roll((bt - tp), 32, 1) * sh[1]
        part[place(t)] = compact(x + both)

    def spec_copy(k):
        to = jnp.bitwise_xor(chip, k)
        return pltpu.make_async_remote_copy(
            src_ref=part.at[core * chips + to], dst_ref=spec_in.at[chip],
            send_sem=spec_send.at[k], recv_sem=spec_recv.at[k],
            device_id={"tile": 2 * to + core}, device_id_type=pl.DeviceIdType.MESH,
        )

    other = pl.ds((1 - core) * chips, chips)
    share = pltpu.make_async_remote_copy(
        src_ref=part.at[other], dst_ref=shared, send_sem=spec_send.at[0], recv_sem=spec_recv.at[0],
        device_id={"tile": jnp.bitwise_xor(me, 1)}, device_id_type=pl.DeviceIdType.MESH,
    )
    share.start()
    share.wait_recv()
    own_part = pl.ds(core * chips, chips)
    part[own_part] = part[own_part] + shared[...]

    @pl.loop(1, chips)
    def _(k):
        spec_copy(k).start()

    start_cells(1)

    def flag_copy(k):
        to = lax.rem(slab + k, slabs)
        return pltpu.make_async_remote_copy(
            src_ref=flag_mine, dst_ref=flag_in.at[k],
            send_sem=flag_send.at[k], recv_sem=flag_recv.at[k],
            device_id={"slab": to}, device_id_type=pl.DeviceIdType.MESH,
        )

    def hop_copy(k, source):
        to = peer_of(k)
        return pltpu.make_async_remote_copy(
            src_ref=out2.at[to], dst_ref=in2.at[source],
            send_sem=hop_send.at[k], recv_sem=hop_recv.at[source],
            device_id={"tile": to}, device_id_type=pl.DeviceIdType.MESH,
        )

    spec_in[chip] = part[core * chips + chip]

    for k in range(KERNELS):
        rows = slice(32 * k, 32 * k + 32)
        re, im = kraw[64 * k : 64 * k + 32, :], kraw[64 * k + 32 : 64 * k + 64, :]
        kr[rows, :] = jnp.concatenate([re] * 4, axis=1)
        ki[rows, :] = jnp.concatenate([-im, im] * 2, axis=1)

    @pl.loop(1, chips)
    def _(k):
        spec_copy(k).wait_recv()

    start_cells(2)
    spec = expand(sum((spec_in[t] for t in range(1, chips)), spec_in[0]))

    spec_s = pltpu.roll(spec, 32, 1)
    for k in range(KERNELS):
        rows = slice(32 * k, 32 * k + 32)
        stack[rows, :] = spec * kr[rows, :] + spec_s * ki[rows, :]
    fields_y = dot(stack[...], yt[...])
    sign = jnp.where(low, -1.0, 1.0)
    for k in range(KERNELS):
        part_k = fields_y[32 * k : 32 * k + 32]
        rhs[0:32, 128 * k : 128 * k + 128] = part_k
        rhs[32:64, 128 * k : 128 * k + 128] = pltpu.roll(part_k, 64, 1) * sign
    fields = dot(x1[...], rhs[...])
    inten = jnp.zeros((64, 128), jnp.float32)
    for k in range(KERNELS):
        e = fields[:, 128 * k : 128 * k + 128]
        inten = inten + wts[k] * (e * e)
    blurred = dot(ux[...], dot(inten, uyt[...]))
    d = dose[0]
    resist = jax.nn.sigmoid(4.0 * (d * blurred - 1.0))
    slope = 2.0 * (resist - target[...]) * (4.0 * d) * resist * (1.0 - resist)
    grad_i = dot3((uxt[0], uxt[1]), halves(dot3(halves(slope), (uy2[0], uy2[1]))))
    lane2 = lax.broadcasted_iota(jnp.int32, (64, 128), 1)
    sign2 = jnp.where(lane2 < 64, 1.0, -1.0)
    for k in range(KERNELS):
        ge = (2.0 * wts[k]) * grad_i * fields[:, 128 * k : 128 * k + 128]
        rhs2[0:64, 128 * k : 128 * k + 128] = ge
        rhs2[64:128, 128 * k : 128 * k + 128] = pltpu.roll(ge, 64, 1) * sign2
    grad_y = dot(x2[...], rhs2[...])
    for k in range(KERNELS):
        stack[32 * k : 32 * k + 32, :] = grad_y[:, 128 * k : 128 * k + 128]
    grad_a = dot(stack[...], y2[...])
    acc = zero
    for k in range(KERNELS):
        rows = slice(32 * k, 32 * k + 32)
        ga = grad_a[rows]
        acc = acc + kr[rows, :] * ga - ki[rows, :] * pltpu.roll(ga, 32, 1)
    acc_all[place(me)] = compact(acc)

    def acc_copy(k):
        to = jnp.bitwise_xor(chip, k)
        return pltpu.make_async_remote_copy(
            src_ref=acc_all.at[place(me)], dst_ref=acc_all.at[place(me)],
            send_sem=acc_send.at[k], recv_sem=acc_recv.at[k],
            device_id={"tile": 2 * to + core}, device_id_type=pl.DeviceIdType.MESH,
        )

    @pl.loop(1, chips)
    def _(k):
        acc_copy(k).start()

    start_cells(3)

    @pl.when(is_relay)
    def _():
        meta_in[me] = meta_out[...]
        in_ov[pl.ds(me * EXTRA, EXTRA)] = out_ov[relay]

        @pl.loop(1, n)
        def _(k):
            for copy in to_relay(0, peer_of(k)):
                copy.wait_recv()

        lines = n // 8
        slot = lax.broadcasted_iota(jnp.int32, (lines, 128), 1) % 16
        start = jnp.zeros((lines, 128), jnp.int32)
        found = jnp.zeros((lines, 128), jnp.int32)
        most = jnp.zeros((lines, 128), jnp.int32)
        for i in range(n):
            count, offset = meta_in[i, 0:lines], meta_in[i, lines : 2 * lines]
            rel = slot - start
            found = jnp.where((rel >= 0) & (rel < count), i * EXTRA + offset + rel, found)
            start = start + count
            most = jnp.maximum(most, count + offset)
        route_v[...] = jnp.zeros((8, 128), jnp.int32)
        route_v[0:lines] = jnp.clip(found, 0, n * EXTRA - 1)
        over = jnp.broadcast_to(jnp.max(jnp.where(most > EXTRA, 1.0, 0.0)), (8, 128))
        route_copy = pltpu.make_async_copy(route_v, route, tab_sem.at[2])
        route_copy.start()
        flag_mine[...] = over

        @pl.when(me == first)
        def _():
            for k in range(1, slabs):
                flag_copy(k).start()

        route_copy.wait()

        @pl.loop(0, n)
        def _(d):
            for m in range(EXTRA):
                out2[d, m] = in_ov[route[d // 8, lax.rem(d, 8) * 16 + m]]

        flag_in[0] = over

        @pl.when(me == first)
        def _():
            for k in range(1, slabs):
                flag_copy(k).wait()
                flag_in[0] = jnp.maximum(flag_in[0], flag_in[k])

        @pl.loop(0, n)
        def _(d):
            out2[d, EXTRA] = flag_in[0]

        @pl.loop(1, n)
        def _(k):
            hop_copy(k, relay).start()

        in2[relay] = out2[me]

    @pl.loop(1, chips)
    def _(k):
        acc_copy(k).wait_recv()

    give = pltpu.make_async_remote_copy(
        src_ref=acc_all.at[own_part], dst_ref=acc_all.at[own_part],
        send_sem=acc_send.at[0], recv_sem=acc_recv.at[0],
        device_id={"tile": jnp.bitwise_xor(me, 1)}, device_id_type=pl.DeviceIdType.MESH,
    )
    give.start()
    give.wait_recv()

    start_cells(4)

    @pl.loop(0, n, unroll=4)
    def _(t):
        mid = expand(acc_all[place(t)])
        before = expand(acc_all[place(jnp.maximum(t - 1, 0))]) * jnp.where(t > 0, 1.0, 0.0)
        after = expand(acc_all[place(jnp.minimum(t + 1, n - 1))]) * jnp.where(t < n - 1, 1.0, 0.0)
        first = mid + before * sh[0] + pltpu.roll(before, 32, 1) * sh[1]
        last = mid + after * sh[0] - pltpu.roll(after, 32, 1) * sh[1]
        mid_s, first_s, last_s = (pltpu.roll(v, 32, 1) for v in (mid, first, last))
        acc2[t * 3] = jnp.where(low, first, mid)
        acc2[t * 3 + 1] = mid
        acc2[t * 3 + 2] = jnp.where(low, mid, last)
        acc2s[t * 3] = jnp.where(low, first_s, mid_s)
        acc2s[t * 3 + 1] = mid_s
        acc2s[t * 3 + 2] = jnp.where(low, mid_s, last_s)

    @pl.loop(0, SIDE)
    def _(a):
        r = pl.multiple_of(a * 64, 64)
        own = me * 3 + jnp.where(a == 0, 0, jnp.where(a == SIDE - 1, 2, 1))
        own_x, own_s = acc2[own], acc2s[own]
        for b in range(4):
            pieces = []
            for i in range(2):
                c = a * 8 + 2 * b + i
                g, p = ix[2, CELLS + c], ix[3, c]
                pieces.append(own_x * pc[c] + own_s * ps[c] + acc2[g] * pc[p] + acc2s[g] * ps[p])
            h0, h1 = pair(*pieces)
            plane[pl.ds(r, 32), 128 * b : 128 * b + 128] = h0
            plane[pl.ds(r + 32, 32), 128 * b : 128 * b + 128] = h1

    for c in range(2):
        for g in range(2):
            v = dot3(halves(plane[256 * g : 256 * g + 256, 256 * c : 256 * c + 256]), (by[0], by[1]))
            vv[g, 0:256, 256 * c : 256 * c + 256] = v[:, 0:256]
            vv[g, 256:512, 256 * c : 256 * c + 256] = v[:, 256:512]
    for g in range(2):
        grad_out[256 * g : 256 * g + 256, :] = dot3((lx[0], lx[1]), halves(vv[g]))

    @pl.loop(1, n)
    def _(k):
        cell_copy(k).wait_recv()

    for q in range(RELAYS):
        @pl.when(me != first + 2 * q)
        def _():
            hop_copy(1, q).wait_recv()

    flag_out[0] = in2[0, EXTRA][0, 0]
    for m in range(EXTRA):
        in_cells[n * direct + m] = jnp.concatenate([in2[q, m] for q in range(RELAYS)], axis=0)

    @pl.loop(0, SIDE)
    def _(a):
        r = pl.multiple_of(a * 64, 64)
        for b in range(4):
            c = a * 8 + 2 * b
            both = pair(in_cells[ix[2, c]],
                          in_cells[ix[2, c + 1]])
            for h in range(2):
                where = (pl.ds(r + 32 * h, 32), slice(128 * b, 128 * b + 128))
                upd_out[where] = mask[where] + both[h]

    @pl.loop(1, n)
    def _(k):
        cell_copy(k).wait_send()

    @pl.loop(1, chips)
    def _(k):
        spec_copy(k).wait_send()
        acc_copy(k).wait_send()

    share.wait_send()
    give.wait_send()

    for q in range(RELAYS):
        @pl.when(me != first + 2 * q)
        def _():
            for copy in to_relay(q, me):
                copy.wait_send()

    @pl.when(is_relay)
    def _():
        @pl.loop(1, n)
        def _(k):
            hop_copy(k, relay).wait_send()


def full_body(n, cap, tab, mask_hbm, both_out, mask, ix, tiles, out_cells, in_cells, tab_sem, cell_send, cell_recv):
    me = lax.axis_index("tile")
    low = lax.broadcasted_iota(jnp.int32, (32, 128), 1) < 64

    def pair(x, y):
        rx, ry = pltpu.roll(x, 64, 1), pltpu.roll(y, 64, 1)
        return jnp.where(low, x, ry), jnp.where(low, rx, y)

    barrier = pltpu.get_barrier_semaphore()

    @pl.loop(1, n)
    def _(k):
        pl.semaphore_signal(
            barrier, inc=1, device_id={"tile": jnp.bitwise_xor(me, k)}, device_id_type=pl.DeviceIdType.MESH
        )

    index_load = pltpu.make_async_copy(tab.at[pl.ds(0, 8)], ix, tab_sem.at[0])
    index_load.start()
    mask_load = pltpu.make_async_copy(mask_hbm, mask, tab_sem.at[1])
    mask_load.start()
    mask_load.wait()

    @pl.loop(0, SIDE)
    def _(a):
        r = pl.multiple_of(a * 64, 64)
        for b in range(4):
            h0 = mask[pl.ds(r, 32), 128 * b : 128 * b + 128]
            h1 = mask[pl.ds(r + 32, 32), 128 * b : 128 * b + 128]
            tiles[a * 8 + 2 * b], tiles[a * 8 + 2 * b + 1] = pair(h0, h1)

    index_load.wait()

    @pl.loop(0, n)
    def _(to):
        for r in range(cap):
            out_cells[to, r] = tiles[ix[0, to * cap + r]]

    in_cells[pl.ds(me * cap, cap)] = out_cells[me]
    pl.semaphore_wait(barrier, n - 1)

    def cell_copy(k):
        to = jnp.bitwise_xor(me, k)
        return pltpu.make_async_remote_copy(
            src_ref=out_cells.at[to], dst_ref=in_cells.at[pl.ds(me * cap, cap)],
            send_sem=cell_send.at[k], recv_sem=cell_recv.at[k],
            device_id={"tile": to}, device_id_type=pl.DeviceIdType.MESH,
        )

    @pl.loop(1, n)
    def _(k):
        cell_copy(k).start()

    @pl.loop(1, n)
    def _(k):
        cell_copy(k).wait()

    @pl.loop(0, SIDE)
    def _(a):
        r = pl.multiple_of(a * 64, 64)
        for b in range(4):
            c = a * 8 + 2 * b
            halves_of = pair(in_cells[ix[1, c]], in_cells[ix[1, c + 1]])
            for h in range(2):
                where = (pl.ds(r + 32 * h, 32), slice(128 * b, 128 * b + 128))
                both_out[where] = mask[where] + halves_of[h]


def full_exchange(n, cap, partner, mask):
    owner = partner // CELLS
    pos = partner % CELLS
    ids = jnp.arange(CELLS, dtype=jnp.int32)
    same = owner[:, None] == owner[None, :]
    send_rank = jnp.sum((same & (pos[None, :] < pos[:, None])).astype(jnp.int32), axis=1)
    recv_rank = jnp.sum((same & (ids[None, :] < ids[:, None])).astype(jnp.int32), axis=1)
    send_slot = owner * cap + send_rank
    recv_slot = owner * cap + recv_rank
    hit = (jnp.arange(n * cap, dtype=jnp.int32)[:, None] == send_slot[None, :]).astype(jnp.int32)
    slot_cell = jnp.sum(hit * ids[None, :], axis=1)
    tab = jnp.concatenate([slot_cell, recv_slot, recv_slot, jnp.zeros((6 * 128,), jnp.int32)]).reshape(8, 128)
    f32 = jnp.float32
    dma = pltpu.SemaphoreType.DMA((n,))
    vmem = pl.BlockSpec(memory_space=pltpu.VMEM)
    return pl.pallas_call(
        functools.partial(full_body, n, cap),
        out_shape=jax.ShapeDtypeStruct((TILE, TILE), f32),
        in_specs=[pl.BlockSpec(memory_space=pl.ANY), pl.BlockSpec(memory_space=pltpu.HBM)],
        out_specs=vmem,
        scratch_shapes=[
            pltpu.VMEM((TILE, TILE), f32),
            pltpu.SMEM((8, 128), jnp.int32),
            pltpu.VMEM((CELLS, 32, 128), f32),
            pltpu.VMEM((n, cap, 32, 128), f32),
            pltpu.VMEM((n * cap, 32, 128), f32),
            pltpu.SemaphoreType.DMA((2,)),
            dma, dma,
        ],
        compiler_params=pltpu.CompilerParams(
            collective_id=1, has_side_effects=True, vmem_limit_bytes=32 * 1024 * 1024
        ),
    )(tab, mask)


def local(consts, mask, target, partner, kernels, socs_weights, dose):
    n = lax.axis_size("tile")
    cap, direct = 2 * CELLS // n, CELLS // n
    meta_lines = (2 * n // 8 + 7) // 8 * 8
    raw = kernels.reshape(2 * KERNELS * BAND, BAND)
    f32 = jnp.float32
    vmem = pl.BlockSpec(memory_space=pltpu.VMEM)
    hbm = pl.BlockSpec(memory_space=pltpu.HBM)
    arrays = [mask, target, raw, *consts]
    smem = pl.BlockSpec(memory_space=pltpu.SMEM)
    dma, few = pltpu.SemaphoreType.DMA((n,)), pltpu.SemaphoreType.DMA((RELAYS,))
    flags = pltpu.SemaphoreType.DMA((lax.axis_size("slab"),))
    twice, both, flag = pl.pallas_call(
        functools.partial(body, n, cap, len(arrays)),
        out_shape=(jax.ShapeDtypeStruct((TILE, TILE), f32),) * 2 + (jax.ShapeDtypeStruct((1,), f32),),
        in_specs=[smem] * 2 + [hbm] + [hbm] * len(arrays),
        out_specs=(vmem, vmem, smem),
        scratch_shapes=[pltpu.VMEM(x.shape, x.dtype) for x in arrays] + [
            pltpu.SemaphoreType.DMA((len(arrays),)),
            pltpu.VMEM((CELLS + 1, 32, 128), f32),
            pltpu.VMEM((CELLS + 1, 32, 128), f32),
            pltpu.VMEM((n, direct, 32, 128), f32),
            pltpu.VMEM((n * direct + EXTRA, 32, 128), f32),
            pltpu.VMEM((CELLS, 32, 128), f32),
            pltpu.VMEM((TILE, TILE), f32),
            pltpu.VMEM((2, 512, 512), f32),
            pltpu.VMEM((n, 32, 128), f32),
            pltpu.VMEM((n, 16, 128), f32),
            pltpu.VMEM((n // 2, 16, 128), f32),
            pltpu.VMEM((n + 1, 32, 128), f32),
            pltpu.VMEM((n + 1, 32, 128), f32),
            pltpu.VMEM((n, 16, 128), f32),
            pltpu.VMEM((n, 16, 128), f32),
            pltpu.VMEM((3 * n, 32, 128), f32),
            pltpu.VMEM((3 * n, 32, 128), f32),
            pltpu.VMEM((64, 768), f32),
            pltpu.VMEM((128, 768), f32),
            pltpu.VMEM((192, 128), f32),
            pltpu.VMEM((192, 128), f32),
            pltpu.VMEM((192, 128), f32),
            pltpu.VMEM((1, CELLS), jnp.int32),
            pltpu.VMEM((8, 128), jnp.int32),
            pltpu.SMEM((8, 128), jnp.int32),
            pltpu.SemaphoreType.DMA((3,)),
            pltpu.SemaphoreType.DMA((4,)),
            pltpu.VMEM((RELAYS, EXTRA, 8, 128), f32),
            pltpu.VMEM((n * EXTRA, 8, 128), f32),
            pltpu.VMEM((n, EXTRA + 1, 8, 128), f32),
            pltpu.VMEM((RELAYS, EXTRA + 1, 8, 128), f32),
            pltpu.VMEM((meta_lines, 128), jnp.int32),
            pltpu.VMEM((n, meta_lines, 128), jnp.int32),
            pltpu.VMEM((8, 128), jnp.int32),
            pltpu.SMEM((8, 128), jnp.int32),
            pltpu.VMEM((8, 128), f32),
            pltpu.VMEM((lax.axis_size("slab"), 8, 128), f32),
            few, dma, few, dma, dma, few, flags, flags,
            dma, dma, dma, dma, dma, dma,
        ],
        compiler_params=pltpu.CompilerParams(
            collective_id=0, has_side_effects=True, vmem_limit_bytes=VMEM_LIMIT
        ),
    )(socs_weights, dose, partner.reshape(1, CELLS), *arrays)
    def finish(g, b):
        return 0.5 * g, 0.5 * (b - 0.1 * g)

    return lax.cond(
        flag[0] > 0.5,
        lambda t, m, g, b: finish(g, full_exchange(n, cap, t, m)),
        lambda t, m, g, b: finish(g, b),
        partner, mask, twice, both,
    )


def solution(mesh):
    consts = tables()

    def run(mask, target, partner, kernels, socs_weights, dose):
        return local([jnp.asarray(t) for t in consts], mask, target, partner, kernels, socs_weights, dose)

    return jax.shard_map(
        run,
        mesh=mesh,
        in_specs=(
            P(("slab", "tile"), None),
            P(("slab", "tile"), None),
            P(("slab", "tile")),
            P(),
            P(),
            P(),
        ),
        out_specs=(P(("slab", "tile"), None), P(("slab", "tile"), None)),
        check_vma=False,
    )
```

```python
import functools
import math

import numpy as np
import jax
import jax.numpy as jnp
from jax import lax
from jax.experimental import pallas as pl
from jax.experimental.pallas import tpu as pltpu
from jax.sharding import PartitionSpec as P

TILE = 512
CELL = 64
MARGIN = 32
BAND = 32
CELLS = 64
SIDE = 8
DOMAIN = 576
GRID = 64
KERNELS = 6
CUTS = (4, 7, 9, 11)
EXTRA = 12
RELAYS = 4
VMEM_LIMIT = 56 * 1024 * 1024
HIGHEST = lax.Precision.HIGHEST
BLUR = (0.0625, 0.25, 0.375, 0.25, 0.0625)


def tables():
    f = np.arange(BAND) - BAND // 2
    norm = 0.5 / math.sqrt(DOMAIN * TILE)
    ph_x = np.zeros((2, SIDE, BAND, 128))
    for h in range(2):
        ang = 2 * np.pi * np.outer(1 + 2 * np.arange(SIDE) + h, f) / 18.0
        ph_x[0, :, :, 64 * h : 64 * h + 64] = norm * np.cos(ang)[:, :, None]
        ph_x[1, :, :, 64 * h : 64 * h + 64] = norm * np.sin(ang)[:, :, None]
    ang = 2 * np.pi * np.outer(np.arange(SIDE), f) / 8.0
    ph_y = np.stack([np.tile(np.cos(ang), (1, 4)), np.tile(np.sin(ang), (1, 4))])
    ang = 2 * np.pi * f * 16 / 18.0
    one = np.ones((1, 32))
    cos16, sin16 = np.cos(ang)[:, None] * one, np.sin(ang)[:, None] * one
    sh = np.stack(
        [np.concatenate([cos16] * 4, 1), np.concatenate([-sin16, sin16] * 2, 1)]
    )
    q = np.arange(CELL)
    cy = np.cos(2 * np.pi * np.outer(f, q) / TILE)
    sy = np.sin(2 * np.pi * np.outer(f, q) / TILE)
    by = np.zeros((256, 512))
    for i in range(4):
        r, o = 64 * i, 64 * i
        by[r : r + 32, o : o + 64] = cy
        by[r : r + 32, 256 + o : 256 + o + 64] = sy
        by[r + 32 : r + 64, o : o + 64] = -sy
        by[r + 32 : r + 64, 256 + o : 256 + o + 64] = cy
    r32 = np.arange(32)
    cx = np.cos(2 * np.pi * np.outer(r32, f) / DOMAIN)
    sx = np.sin(2 * np.pi * np.outer(r32, f) / DOMAIN)
    lx = np.zeros((256, 512))
    for j in range(8):
        k = 32 * j
        lx[k : k + 32, k : k + 32] = cx
        lx[k : k + 32, 256 + k : 256 + k + 32] = -sx
    m = np.arange(GRID)
    c = np.cos(2 * np.pi * np.outer(f, m) / GRID)
    s = np.sin(2 * np.pi * np.outer(f, m) / GRID)
    yt = np.zeros((128, 128))
    yt[:32, :64], yt[:32, 64:], yt[32:64, :64], yt[32:64, 64:] = c, s, -s, c
    x1 = np.concatenate([c.T, s.T], 1) / BAND
    x2 = np.concatenate([c, s], 1) / BAND
    y2 = np.zeros((128, 128))
    half = np.concatenate([np.concatenate([c.T, -s.T], 1), np.concatenate([s.T, c.T], 1)], 0)
    y2[:, :64], y2[:, 64:] = half, half
    g = np.arange(-31, 32)

    def interp(extent):
        d = np.arange(extent)[:, None] / extent - m[None, :] / GRID
        return np.cos(2 * np.pi * g[:, None, None] * d[None]).sum(0) / GRID

    ux = interp(DOMAIN)
    ux = sum(BLUR[i] * ux[MARGIN - 2 + i : MARGIN - 2 + i + TILE] for i in range(5))
    uy = interp(TILE)
    uy = sum(BLUR[i] * np.roll(uy, i - 2, axis=0) for i in range(5))
    uyt = np.concatenate([uy.T, uy.T], 0)
    uy2 = np.concatenate([uy, uy], 1)
    whole = [ph_x, ph_y, sh, yt, x1, x2, y2, ux, uyt]
    return [np.ascontiguousarray(t, dtype=np.float32) for t in whole] + [
        split(np.ascontiguousarray(t, dtype=np.float32)) for t in (by, lx, lx.T, ux.T, uy2)
    ]


def split(t):
    hi = t.astype(jnp.bfloat16)
    return np.stack([hi, (t - hi.astype(np.float32)).astype(jnp.bfloat16)])


def dot(x, y):
    return jnp.dot(x, y, precision=HIGHEST, preferred_element_type=jnp.float32)


def halves(x):
    hi = x.astype(jnp.bfloat16)
    return hi, (x - hi.astype(jnp.float32)).astype(jnp.bfloat16)


def dot3(x, y, dims=((1,), (0,))):
    def one(p, q):
        return lax.dot_general(p, q, (dims, ((), ())), preferred_element_type=jnp.float32)

    return one(x[0], y[0]) + (one(x[0], y[1]) + one(x[1], y[0]))


def build_tables(n, cap, mates, index_out, meta_out):
    direct, lines = cap // 2, n // 8
    row = jnp.concatenate([mates[...], mates[...]], axis=1)
    square = jnp.broadcast_to(row, (128, 128))
    across, down = square[0:CELLS], square.T[0:CELLS]
    lane = lax.broadcasted_iota(jnp.int32, (CELLS, 128), 1)
    cell = lax.broadcasted_iota(jnp.int32, (CELLS, 128), 0)
    own_r, pos_r, own_c, pos_c = across >> 6, across & 63, down >> 6, down & 63
    valid = lane < CELLS

    def over_cells(mask):
        return jnp.sum(jnp.where(mask, 1, 0), axis=0, keepdims=True)

    def over_lanes(mask):
        return jnp.sum(jnp.where(mask & valid, 1, 0), axis=1, keepdims=True)

    same = own_r == own_c
    rank_r = over_cells(same & (pos_c < pos_r))
    recv_r = over_cells(same & (cell < lane))
    rank_c = over_lanes(same & (pos_r < pos_c))
    spare_c = jnp.broadcast_to(rank_c, (CELLS, 128)) >= direct
    spare_r = jnp.broadcast_to(rank_r, (CELLS, 128)) >= direct
    ahead_r = over_cells(spare_c & (own_c < own_r))
    ahead_c = over_lanes(spare_r & (own_r < own_c))
    hit = own_c * cap + rank_c == lane
    own, pos, first = own_r[0:1], pos_r[0:1], lane[0:1] < CELLS
    kind = jnp.where(pos < SIDE, 0, jnp.where(pos >= CELLS - SIDE, 2, 1))
    recv = jnp.where(
        recv_r < direct, own * direct + recv_r,
        n * direct + jnp.minimum(ahead_r + recv_r - direct, EXTRA - 1),
    )
    index_out[0:1] = jnp.max(jnp.where(hit, cell, 0), axis=0, keepdims=True)
    index_out[1:2] = jnp.min(jnp.where(hit, pos_c, CELLS), axis=0, keepdims=True)
    index_out[2:3] = jnp.where(first, recv, own * 3 + kind)
    index_out[3:4] = jnp.where(
        first, pos,
        jnp.max(jnp.where(spare_c & (ahead_c + rank_c - direct == lane - CELLS), cell, 0), axis=0, keepdims=True),
    )
    index_out[4:8] = jnp.zeros((4, 128), jnp.int32)
    meta_out[...] = jnp.zeros(meta_out.shape, jnp.int32)
    for h in range(lines):
        dest = (lane + 128 * h) >> 4
        meta_out[h : h + 1] = over_cells(spare_c & (own_c == dest))
        meta_out[lines + h : lines + h + 1] = over_cells(spare_c & (own_c < dest))


def body(n, cap, n_in, wts, dose, tab, *refs):
    hbm, outs = refs[:n_in], refs[n_in : n_in + 3]
    vm = refs[n_in + 3 : 2 * n_in + 3]
    load_sem = refs[2 * n_in + 3]
    (
        mask, target, kraw, ph_x, ph_y, sh, yt, x1, x2, y2, ux, uyt, by, lx, lxt, uxt, uy2
    ) = vm
    main(n, cap, tab, wts, dose, hbm, vm, load_sem,
         mask, target, kraw, ph_x, ph_y, sh, yt, x1, x2, y2, ux, uyt, by, lx, lxt, uxt, uy2,
         *outs, *refs[2 * n_in + 4 :])


def main(
    n, cap, tab, wts, dose, hbm, vm, load_sem,
    mask, target, kraw, ph_x, ph_y, sh, yt, x1, x2, y2, ux, uyt, by, lx, lxt, uxt, uy2,
    grad_out, upd_out, flag_out, pc, ps,
    out_cells, in_cells, tiles, plane, vv, wide, part, shared, top, bot, spec_in, acc_all, acc2, acc2s, rhs, rhs2, stack,
    kr, ki, mates, ix_v, ix, tab_sem, mask_sem, out_ov, in_ov, out2, in2, meta_out, meta_in, route_v, route, flag_mine, flag_in,
    ov_send, ov_recv, meta_send, meta_recv, hop_send, hop_recv, flag_send, flag_recv,
    cell_send, cell_recv, spec_send, spec_recv, acc_send, acc_recv,
):
    me = lax.axis_index("tile")
    lane = lax.broadcasted_iota(jnp.int32, (32, 128), 1)
    low = lane < 64
    slabs = lax.axis_size("slab")
    slab = lax.axis_index("slab")
    direct = cap // 2
    first = n // 4
    relay = (me - first) // 2
    is_relay = (me >= first) & (me < first + 2 * RELAYS) & (lax.rem(me, 2) == 0)

    def swap(x):
        return jnp.where(lane % 64 < 32, pltpu.roll(x, 96, 1), pltpu.roll(x, 32, 1))

    def pair(x, y):
        rx, ry = pltpu.roll(x, 64, 1), pltpu.roll(y, 64, 1)
        return jnp.where(low, x, ry), jnp.where(low, rx, y)

    def to_tiles(src, start=0, stop=SIDE):
        @pl.loop(start, stop)
        def _(a):
            r = pl.multiple_of(a * 64, 64)
            for b in range(4):
                h0 = src[pl.ds(r, 32), 128 * b : 128 * b + 128]
                h1 = src[pl.ds(r + 32, 32), 128 * b : 128 * b + 128]
                x, y = pair(h0, h1)
                tiles[a * 8 + 2 * b] = x
                tiles[a * 8 + 2 * b + 1] = y

    def compact(x):
        return jnp.where(low[0:16], x[0:16], x[16:32])

    def expand(x):
        r = pltpu.roll(x, 64, 1)
        return jnp.concatenate([jnp.where(low[0:16], x, r), jnp.where(low[0:16], r, x)], axis=0)

    chips = n // 2
    core = lax.rem(me, 2)
    chip = me // 2
    half = chips // 2
    low_chip, high_chip = lax.rem(chip, half), chip // half
    mine = core * chips + 2 * low_chip
    across = 2 * (low_chip + half * (1 - high_chip)) + core

    def place(t):
        return lax.rem(t, 2) * chips + 2 * lax.rem(t // 2, half) + t // 2 // half

    def peer_of(k):
        return jnp.bitwise_xor(me, k)

    barrier = pltpu.get_barrier_semaphore()

    partner_load = pltpu.make_async_copy(tab, mates, tab_sem.at[1])
    partner_load.start()
    rows = TILE // 4
    mask_loads = [
        pltpu.make_async_copy(hbm[0].at[pl.ds(rows * c, rows)], mask.at[pl.ds(rows * c, rows)], mask_sem.at[c])
        for c in range(4)
    ]
    for load in mask_loads:
        load.start()

    @pl.loop(1, n)
    def _(k):
        pl.semaphore_signal(barrier, inc=1, device_id={"tile": peer_of(k)}, device_id_type=pl.DeviceIdType.MESH)

    for k in range(1, slabs):
        pl.semaphore_signal(
            barrier, inc=1, device_id={"slab": lax.rem(slab + k, slabs)}, device_id_type=pl.DeviceIdType.MESH
        )

    partner_load.wait()
    build_tables(n, cap, mates, ix_v, meta_out)
    index_load = pltpu.make_async_copy(ix_v, ix, tab_sem.at[0])
    index_load.start()

    for c in range(4):
        mask_loads[c].wait()
        to_tiles(mask, 2 * c, 2 * c + 2)

    in_cells[pl.ds(me * direct, direct)] = jnp.zeros((direct, 32, 128), jnp.float32)
    index_load.wait()

    @pl.loop(0, EXTRA, unroll=4)
    def _(o):
        x = tiles[ix[3, CELLS + o]]
        for q in range(RELAYS):
            out_ov[q, o] = x[8 * q : 8 * q + 8]

    pl.semaphore_wait(barrier, n + slabs - 2)

    def to_relay(q, source):
        where = {"device_id": {"tile": first + 2 * q}, "device_id_type": pl.DeviceIdType.MESH}
        return (
            pltpu.make_async_remote_copy(
                src_ref=meta_out, dst_ref=meta_in.at[source],
                send_sem=meta_send.at[q], recv_sem=meta_recv.at[source], **where,
            ),
            pltpu.make_async_remote_copy(
                src_ref=out_ov.at[q], dst_ref=in_ov.at[pl.ds(source * EXTRA, EXTRA)],
                send_sem=ov_send.at[q], recv_sem=ov_recv.at[source], **where,
            ),
        )

    for q in range(RELAYS):
        @pl.when(me != first + 2 * q)
        def _():
            for copy in to_relay(q, me):
                copy.start()
    loads = [pltpu.make_async_copy(hbm[i], vm[i], load_sem.at[i]) for i in range(1, len(hbm))]
    for load in loads:
        load.start()


    def cell_copy(k):
        to = peer_of(k)
        return pltpu.make_async_remote_copy(
            src_ref=out_cells.at[to], dst_ref=in_cells.at[pl.ds(me * direct, direct)],
            send_sem=cell_send.at[k], recv_sem=cell_recv.at[k],
            device_id={"tile": to}, device_id_type=pl.DeviceIdType.MESH,
        )

    cuts = [(n - 1) * c // 15 for c in (0,) + CUTS + (15,)]

    def offset_of(j):
        return jnp.where(lax.rem(j, 2) == 0, n // 2 + j // 2, n // 2 - 1 - j // 2)

    def pack(k):
        to = peer_of(k)
        for r in range(direct):
            out_cells[to, r] = tiles[ix[0, to * cap + r]]

    def start_cells(stage):
        @pl.loop(cuts[stage], cuts[stage + 1])
        def _(j):
            cell_copy(offset_of(j)).start()

    @pl.loop(cuts[0], cuts[1])
    def _(j):
        pack(offset_of(j))
        cell_copy(offset_of(j)).start()

    @pl.loop(cuts[1], n - 1)
    def _(j):
        pack(offset_of(j))

    for load in loads:
        load.wait()

    zero = jnp.zeros((32, 128), jnp.float32)
    lane_sign = jnp.where(lane % 64 < 32, -1.0, 1.0)

    @pl.loop(0, SIDE)
    def _(a):
        c, s = ph_x[0, a], ph_x[1, a]
        for b in range(SIDE):
            cb, sb = ph_y[0, b : b + 1, :], ph_y[1, b : b + 1, :]
            pc[a * 8 + b] = c * cb - s * sb
            ps[a * 8 + b] = (s * cb + c * sb) * lane_sign

    pc[CELLS] = zero
    ps[CELLS] = zero

    lxt_pair = lxt[0], lxt[1]
    for g in range(2):
        vv[g] = dot3(lxt_pair, halves(mask[256 * g : 256 * g + 256, :]))
    for g in range(2):
        for c in range(2):
            cols = slice(256 * c, 256 * c + 256)
            left = jnp.concatenate([vv[g, 0:256, cols], vv[g, 256:512, cols]], axis=1)
            plane[256 * g : 256 * g + 256, cols] = dot3(halves(left), (by[0], by[1]), ((1,), (1,)))
    to_tiles(plane)

    top[n] = zero
    bot[0] = zero

    @pl.loop(0, n, unroll=4)
    def _(t):
        sums = [zero] * 6
        for r in range(cap):
            s = t * cap + r
            x = tiles[ix[0, s]]
            p = ix[1, s]
            u, w = x * pc[p], x * ps[p]
            wt = jnp.where(p < 8, 1.0, 0.0)
            wb = jnp.where(p >= 56, 1.0, 0.0)
            sums = [
                sums[0] + u, sums[1] + w, sums[2] + wt * u, sums[3] + wt * w,
                sums[4] + wb * u, sums[5] + wb * w,
            ]
        wide[t] = sums[0] + swap(sums[1])
        top[t] = sums[2] + swap(sums[3])
        bot[t + 1] = sums[4] + swap(sums[5])

    def own_row(a, carry):
        u, w = carry
        for b in range(8):
            x = tiles[a * 8 + b]
            u, w = u + x * pc[a * 8 + b], w + x * ps[a * 8 + b]
        return u, w

    u0, w0 = own_row(0, (zero, zero))
    u7, w7 = own_row(7, (zero, zero))
    u, w = lax.fori_loop(1, 7, own_row, (u0 + u7, w0 + w7))
    wide[me] += u + swap(w)
    top[me] += u0 + swap(w0)
    bot[me + 1] += u7 + swap(w7)

    @pl.loop(0, n, unroll=8)
    def _(t):
        tp = jnp.where(low, top[t + 1], 0.0)
        bt = jnp.where(low, 0.0, bot[t])
        tp = tp + pltpu.roll(tp, 64, 1)
        bt = bt + pltpu.roll(bt, 64, 1)
        x = wide[t]
        x = x + pltpu.roll(x, 64, 1)
        both = (tp + bt) * sh[0] + pltpu.roll((bt - tp), 32, 1) * sh[1]
        part[place(t)] = compact(x + both)

    def spec_copy(k):
        to = jnp.bitwise_xor(chip, k)
        return pltpu.make_async_remote_copy(
            src_ref=part.at[place(2 * to + core)], dst_ref=spec_in.at[chip],
            send_sem=spec_send.at[k], recv_sem=spec_recv.at[k],
            device_id={"tile": 2 * to + core}, device_id_type=pl.DeviceIdType.MESH,
        )

    other = pl.ds((1 - core) * chips, chips)
    share = pltpu.make_async_remote_copy(
        src_ref=part.at[other], dst_ref=shared, send_sem=spec_send.at[0], recv_sem=spec_recv.at[0],
        device_id={"tile": jnp.bitwise_xor(me, 1)}, device_id_type=pl.DeviceIdType.MESH,
    )
    share.start()
    share.wait_recv()
    own_part = pl.ds(core * chips, chips)
    part[own_part] = part[own_part] + shared[...]

    @pl.loop(1, chips)
    def _(k):
        spec_copy(k).start()

    start_cells(1)

    def flag_copy(k):
        to = lax.rem(slab + k, slabs)
        return pltpu.make_async_remote_copy(
            src_ref=flag_mine, dst_ref=flag_in.at[k],
            send_sem=flag_send.at[k], recv_sem=flag_recv.at[k],
            device_id={"slab": to}, device_id_type=pl.DeviceIdType.MESH,
        )

    def hop_copy(k, source):
        to = peer_of(k)
        return pltpu.make_async_remote_copy(
            src_ref=out2.at[to], dst_ref=in2.at[source],
            send_sem=hop_send.at[k], recv_sem=hop_recv.at[source],
            device_id={"tile": to}, device_id_type=pl.DeviceIdType.MESH,
        )

    spec_in[chip] = part[place(me)]

    for k in range(KERNELS):
        rows = slice(32 * k, 32 * k + 32)
        re, im = kraw[64 * k : 64 * k + 32, :], kraw[64 * k + 32 : 64 * k + 64, :]
        kr[rows, :] = jnp.concatenate([re] * 4, axis=1)
        ki[rows, :] = jnp.concatenate([-im, im] * 2, axis=1)

    @pl.loop(1, chips)
    def _(k):
        spec_copy(k).wait_recv()

    start_cells(2)
    spec = expand(sum((spec_in[t] for t in range(1, chips)), spec_in[0]))

    spec_s = pltpu.roll(spec, 32, 1)
    for k in range(KERNELS):
        rows = slice(32 * k, 32 * k + 32)
        stack[rows, :] = spec * kr[rows, :] + spec_s * ki[rows, :]
    fields_y = dot(stack[...], yt[...])
    sign = jnp.where(low, -1.0, 1.0)
    for k in range(KERNELS):
        part_k = fields_y[32 * k : 32 * k + 32]
        rhs[0:32, 128 * k : 128 * k + 128] = part_k
        rhs[32:64, 128 * k : 128 * k + 128] = pltpu.roll(part_k, 64, 1) * sign
    fields = dot(x1[...], rhs[...])
    inten = jnp.zeros((64, 128), jnp.float32)
    for k in range(KERNELS):
        e = fields[:, 128 * k : 128 * k + 128]
        inten = inten + wts[k] * (e * e)
    blurred = dot(ux[...], dot(inten, uyt[...]))
    d = dose[0]
    resist = jax.nn.sigmoid(4.0 * (d * blurred - 1.0))
    slope = 2.0 * (resist - target[...]) * (4.0 * d) * resist * (1.0 - resist)
    grad_i = dot3((uxt[0], uxt[1]), halves(dot3(halves(slope), (uy2[0], uy2[1]))))
    lane2 = lax.broadcasted_iota(jnp.int32, (64, 128), 1)
    sign2 = jnp.where(lane2 < 64, 1.0, -1.0)
    for k in range(KERNELS):
        ge = (2.0 * wts[k]) * grad_i * fields[:, 128 * k : 128 * k + 128]
        rhs2[0:64, 128 * k : 128 * k + 128] = ge
        rhs2[64:128, 128 * k : 128 * k + 128] = pltpu.roll(ge, 64, 1) * sign2
    grad_y = dot(x2[...], rhs2[...])
    for k in range(KERNELS):
        stack[32 * k : 32 * k + 32, :] = grad_y[:, 128 * k : 128 * k + 128]
    grad_a = dot(stack[...], y2[...])
    acc = zero
    for k in range(KERNELS):
        rows = slice(32 * k, 32 * k + 32)
        ga = grad_a[rows]
        acc = acc + kr[rows, :] * ga - ki[rows, :] * pltpu.roll(ga, 32, 1)
    acc_all[place(me)] = compact(acc)

    def acc_copy(k):
        to = jnp.bitwise_xor(low_chip, k)
        return pltpu.make_async_remote_copy(
            src_ref=acc_all.at[pl.ds(mine, 2)], dst_ref=acc_all.at[pl.ds(mine, 2)],
            send_sem=acc_send.at[k], recv_sem=acc_recv.at[k],
            device_id={"tile": 2 * (to + half * high_chip) + core}, device_id_type=pl.DeviceIdType.MESH,
        )

    acc_cross = pltpu.make_async_remote_copy(
        src_ref=acc_all.at[place(me)], dst_ref=acc_all.at[place(me)],
        send_sem=acc_send.at[half], recv_sem=acc_recv.at[half],
        device_id={"tile": across}, device_id_type=pl.DeviceIdType.MESH,
    )
    acc_cross.start()
    start_cells(3)
    acc_cross.wait_recv()

    @pl.loop(1, half)
    def _(k):
        acc_copy(k).start()

    start_cells(4)

    @pl.when(is_relay)
    def _():
        meta_in[me] = meta_out[...]
        in_ov[pl.ds(me * EXTRA, EXTRA)] = out_ov[relay]

        @pl.loop(1, n)
        def _(k):
            for copy in to_relay(0, peer_of(k)):
                copy.wait_recv()

        lines = n // 8
        slot = lax.broadcasted_iota(jnp.int32, (lines, 128), 1) % 16
        start = jnp.zeros((lines, 128), jnp.int32)
        found = jnp.zeros((lines, 128), jnp.int32)
        most = jnp.zeros((lines, 128), jnp.int32)
        for i in range(n):
            count, offset = meta_in[i, 0:lines], meta_in[i, lines : 2 * lines]
            rel = slot - start
            found = jnp.where((rel >= 0) & (rel < count), i * EXTRA + offset + rel, found)
            start = start + count
            most = jnp.maximum(most, count + offset)
        route_v[...] = jnp.zeros((8, 128), jnp.int32)
        route_v[0:lines] = jnp.clip(found, 0, n * EXTRA - 1)
        over = jnp.broadcast_to(jnp.max(jnp.where(most > EXTRA, 1.0, 0.0)), (8, 128))
        route_copy = pltpu.make_async_copy(route_v, route, tab_sem.at[2])
        route_copy.start()
        flag_mine[...] = over

        @pl.when(me == first)
        def _():
            for k in range(1, slabs):
                flag_copy(k).start()

        route_copy.wait()

        @pl.loop(0, n)
        def _(d):
            for m in range(EXTRA):
                out2[d, m] = in_ov[route[d // 8, lax.rem(d, 8) * 16 + m]]

        flag_in[0] = over

        @pl.when(me == first)
        def _():
            for k in range(1, slabs):
                flag_copy(k).wait()
                flag_in[0] = jnp.maximum(flag_in[0], flag_in[k])

        @pl.loop(0, n)
        def _(d):
            out2[d, EXTRA] = flag_in[0]

        @pl.loop(1, n)
        def _(k):
            hop_copy(k, relay).start()

        in2[relay] = out2[me]

    @pl.loop(1, half)
    def _(k):
        acc_copy(k).wait_recv()

    give = pltpu.make_async_remote_copy(
        src_ref=acc_all.at[own_part], dst_ref=acc_all.at[own_part],
        send_sem=acc_send.at[0], recv_sem=acc_recv.at[0],
        device_id={"tile": jnp.bitwise_xor(me, 1)}, device_id_type=pl.DeviceIdType.MESH,
    )
    give.start()
    give.wait_recv()


    @pl.loop(0, n, unroll=8)
    def _(t):
        mid = expand(acc_all[place(t)])
        before = expand(acc_all[place(jnp.maximum(t - 1, 0))]) * jnp.where(t > 0, 1.0, 0.0)
        after = expand(acc_all[place(jnp.minimum(t + 1, n - 1))]) * jnp.where(t < n - 1, 1.0, 0.0)
        first = mid + before * sh[0] + pltpu.roll(before, 32, 1) * sh[1]
        last = mid + after * sh[0] - pltpu.roll(after, 32, 1) * sh[1]
        mid_s, first_s, last_s = (pltpu.roll(v, 32, 1) for v in (mid, first, last))
        acc2[t * 3] = jnp.where(low, first, mid)
        acc2[t * 3 + 1] = mid
        acc2[t * 3 + 2] = jnp.where(low, mid, last)
        acc2s[t * 3] = jnp.where(low, first_s, mid_s)
        acc2s[t * 3 + 1] = mid_s
        acc2s[t * 3 + 2] = jnp.where(low, mid_s, last_s)

    @pl.loop(0, SIDE, unroll=2)
    def _(a):
        r = pl.multiple_of(a * 64, 64)
        own = me * 3 + jnp.where(a == 0, 0, jnp.where(a == SIDE - 1, 2, 1))
        own_x, own_s = acc2[own], acc2s[own]
        for b in range(4):
            pieces = []
            for i in range(2):
                c = a * 8 + 2 * b + i
                g, p = ix[2, CELLS + c], ix[3, c]
                pieces.append(own_x * pc[c] + own_s * ps[c] + acc2[g] * pc[p] + acc2s[g] * ps[p])
            h0, h1 = pair(*pieces)
            plane[pl.ds(r, 32), 128 * b : 128 * b + 128] = h0
            plane[pl.ds(r + 32, 32), 128 * b : 128 * b + 128] = h1

    for c in range(2):
        for g in range(2):
            v = dot3(halves(plane[256 * g : 256 * g + 256, 256 * c : 256 * c + 256]), (by[0], by[1]))
            vv[g, 0:256, 256 * c : 256 * c + 256] = v[:, 0:256]
            vv[g, 256:512, 256 * c : 256 * c + 256] = v[:, 256:512]
    for g in range(2):
        grad_out[256 * g : 256 * g + 256, :] = dot3((lx[0], lx[1]), halves(vv[g]))

    @pl.loop(1, n)
    def _(k):
        cell_copy(k).wait_recv()

    for q in range(RELAYS):
        @pl.when(me != first + 2 * q)
        def _():
            hop_copy(1, q).wait_recv()

    flag_out[0] = in2[0, EXTRA][0, 0]
    for m in range(EXTRA):
        in_cells[n * direct + m] = jnp.concatenate([in2[q, m] for q in range(RELAYS)], axis=0)

    @pl.loop(0, SIDE, unroll=2)
    def _(a):
        r = pl.multiple_of(a * 64, 64)
        for b in range(4):
            c = a * 8 + 2 * b
            both = pair(in_cells[ix[2, c]],
                          in_cells[ix[2, c + 1]])
            for h in range(2):
                where = (pl.ds(r + 32 * h, 32), slice(128 * b, 128 * b + 128))
                upd_out[where] = 0.5 * (mask[where] + both[h]) - 0.1 * grad_out[where]

    @pl.loop(1, n)
    def _(k):
        cell_copy(k).wait_send()

    @pl.loop(1, chips)
    def _(k):
        spec_copy(k).wait_send()

    @pl.loop(1, half)
    def _(k):
        acc_copy(k).wait_send()

    acc_cross.wait_send()

    share.wait_send()
    give.wait_send()

    for q in range(RELAYS):
        @pl.when(me != first + 2 * q)
        def _():
            for copy in to_relay(q, me):
                copy.wait_send()

    @pl.when(is_relay)
    def _():
        @pl.loop(1, n)
        def _(k):
            hop_copy(k, relay).wait_send()


def full_body(n, cap, tab, mask_hbm, both_out, mask, ix, tiles, out_cells, in_cells, tab_sem, cell_send, cell_recv):
    me = lax.axis_index("tile")
    low = lax.broadcasted_iota(jnp.int32, (32, 128), 1) < 64

    def pair(x, y):
        rx, ry = pltpu.roll(x, 64, 1), pltpu.roll(y, 64, 1)
        return jnp.where(low, x, ry), jnp.where(low, rx, y)

    barrier = pltpu.get_barrier_semaphore()

    @pl.loop(1, n)
    def _(k):
        pl.semaphore_signal(
            barrier, inc=1, device_id={"tile": jnp.bitwise_xor(me, k)}, device_id_type=pl.DeviceIdType.MESH
        )

    index_load = pltpu.make_async_copy(tab.at[pl.ds(0, 8)], ix, tab_sem.at[0])
    index_load.start()
    mask_load = pltpu.make_async_copy(mask_hbm, mask, tab_sem.at[1])
    mask_load.start()
    mask_load.wait()

    @pl.loop(0, SIDE)
    def _(a):
        r = pl.multiple_of(a * 64, 64)
        for b in range(4):
            h0 = mask[pl.ds(r, 32), 128 * b : 128 * b + 128]
            h1 = mask[pl.ds(r + 32, 32), 128 * b : 128 * b + 128]
            tiles[a * 8 + 2 * b], tiles[a * 8 + 2 * b + 1] = pair(h0, h1)

    index_load.wait()

    @pl.loop(0, n)
    def _(to):
        for r in range(cap):
            out_cells[to, r] = tiles[ix[0, to * cap + r]]

    in_cells[pl.ds(me * cap, cap)] = out_cells[me]
    pl.semaphore_wait(barrier, n - 1)

    def cell_copy(k):
        to = jnp.bitwise_xor(me, k)
        return pltpu.make_async_remote_copy(
            src_ref=out_cells.at[to], dst_ref=in_cells.at[pl.ds(me * cap, cap)],
            send_sem=cell_send.at[k], recv_sem=cell_recv.at[k],
            device_id={"tile": to}, device_id_type=pl.DeviceIdType.MESH,
        )

    @pl.loop(1, n)
    def _(k):
        cell_copy(k).start()

    @pl.loop(1, n)
    def _(k):
        cell_copy(k).wait()

    @pl.loop(0, SIDE)
    def _(a):
        r = pl.multiple_of(a * 64, 64)
        for b in range(4):
            c = a * 8 + 2 * b
            halves_of = pair(in_cells[ix[1, c]], in_cells[ix[1, c + 1]])
            for h in range(2):
                where = (pl.ds(r + 32 * h, 32), slice(128 * b, 128 * b + 128))
                both_out[where] = mask[where] + halves_of[h]


def full_exchange(n, cap, partner, mask):
    owner = partner // CELLS
    pos = partner % CELLS
    ids = jnp.arange(CELLS, dtype=jnp.int32)
    same = owner[:, None] == owner[None, :]
    send_rank = jnp.sum((same & (pos[None, :] < pos[:, None])).astype(jnp.int32), axis=1)
    recv_rank = jnp.sum((same & (ids[None, :] < ids[:, None])).astype(jnp.int32), axis=1)
    send_slot = owner * cap + send_rank
    recv_slot = owner * cap + recv_rank
    hit = (jnp.arange(n * cap, dtype=jnp.int32)[:, None] == send_slot[None, :]).astype(jnp.int32)
    slot_cell = jnp.sum(hit * ids[None, :], axis=1)
    tab = jnp.concatenate([slot_cell, recv_slot, recv_slot, jnp.zeros((6 * 128,), jnp.int32)]).reshape(8, 128)
    f32 = jnp.float32
    dma = pltpu.SemaphoreType.DMA((n,))
    vmem = pl.BlockSpec(memory_space=pltpu.VMEM)
    return pl.pallas_call(
        functools.partial(full_body, n, cap),
        out_shape=jax.ShapeDtypeStruct((TILE, TILE), f32),
        in_specs=[pl.BlockSpec(memory_space=pl.ANY), pl.BlockSpec(memory_space=pltpu.HBM)],
        out_specs=vmem,
        scratch_shapes=[
            pltpu.VMEM((TILE, TILE), f32),
            pltpu.SMEM((8, 128), jnp.int32),
            pltpu.VMEM((CELLS, 32, 128), f32),
            pltpu.VMEM((n, cap, 32, 128), f32),
            pltpu.VMEM((n * cap, 32, 128), f32),
            pltpu.SemaphoreType.DMA((2,)),
            dma, dma,
        ],
        compiler_params=pltpu.CompilerParams(
            collective_id=1, has_side_effects=True, vmem_limit_bytes=32 * 1024 * 1024
        ),
    )(tab, mask)


def local(consts, mask, target, partner, kernels, socs_weights, dose):
    n = lax.axis_size("tile")
    cap, direct = 2 * CELLS // n, CELLS // n
    meta_lines = (2 * n // 8 + 7) // 8 * 8
    raw = kernels.reshape(2 * KERNELS * BAND, BAND)
    f32 = jnp.float32
    vmem = pl.BlockSpec(memory_space=pltpu.VMEM)
    hbm = pl.BlockSpec(memory_space=pltpu.HBM)
    arrays = [mask, target, raw, *consts]
    smem = pl.BlockSpec(memory_space=pltpu.SMEM)
    dma, few = pltpu.SemaphoreType.DMA((n,)), pltpu.SemaphoreType.DMA((RELAYS,))
    flags = pltpu.SemaphoreType.DMA((lax.axis_size("slab"),))
    twice, both, flag = pl.pallas_call(
        functools.partial(body, n, cap, len(arrays)),
        out_shape=(jax.ShapeDtypeStruct((TILE, TILE), f32),) * 2 + (jax.ShapeDtypeStruct((1,), f32),),
        in_specs=[smem] * 2 + [hbm] + [hbm] * len(arrays),
        out_specs=(vmem, vmem, smem),
        scratch_shapes=[pltpu.VMEM(x.shape, x.dtype) for x in arrays] + [
            pltpu.SemaphoreType.DMA((len(arrays),)),
            pltpu.VMEM((CELLS + 1, 32, 128), f32),
            pltpu.VMEM((CELLS + 1, 32, 128), f32),
            pltpu.VMEM((n, direct, 32, 128), f32),
            pltpu.VMEM((n * direct + EXTRA, 32, 128), f32),
            pltpu.VMEM((CELLS, 32, 128), f32),
            pltpu.VMEM((TILE, TILE), f32),
            pltpu.VMEM((2, 512, 512), f32),
            pltpu.VMEM((n, 32, 128), f32),
            pltpu.VMEM((n, 16, 128), f32),
            pltpu.VMEM((n // 2, 16, 128), f32),
            pltpu.VMEM((n + 1, 32, 128), f32),
            pltpu.VMEM((n + 1, 32, 128), f32),
            pltpu.VMEM((n, 16, 128), f32),
            pltpu.VMEM((n, 16, 128), f32),
            pltpu.VMEM((3 * n, 32, 128), f32),
            pltpu.VMEM((3 * n, 32, 128), f32),
            pltpu.VMEM((64, 768), f32),
            pltpu.VMEM((128, 768), f32),
            pltpu.VMEM((192, 128), f32),
            pltpu.VMEM((192, 128), f32),
            pltpu.VMEM((192, 128), f32),
            pltpu.VMEM((1, CELLS), jnp.int32),
            pltpu.VMEM((8, 128), jnp.int32),
            pltpu.SMEM((8, 128), jnp.int32),
            pltpu.SemaphoreType.DMA((3,)),
            pltpu.SemaphoreType.DMA((4,)),
            pltpu.VMEM((RELAYS, EXTRA, 8, 128), f32),
            pltpu.VMEM((n * EXTRA, 8, 128), f32),
            pltpu.VMEM((n, EXTRA + 1, 8, 128), f32),
            pltpu.VMEM((RELAYS, EXTRA + 1, 8, 128), f32),
            pltpu.VMEM((meta_lines, 128), jnp.int32),
            pltpu.VMEM((n, meta_lines, 128), jnp.int32),
            pltpu.VMEM((8, 128), jnp.int32),
            pltpu.SMEM((8, 128), jnp.int32),
            pltpu.VMEM((8, 128), f32),
            pltpu.VMEM((lax.axis_size("slab"), 8, 128), f32),
            few, dma, few, dma, dma, few, flags, flags,
            dma, dma, dma, dma, dma, dma,
        ],
        compiler_params=pltpu.CompilerParams(
            collective_id=0, has_side_effects=True, vmem_limit_bytes=VMEM_LIMIT
        ),
    )(socs_weights, dose, partner.reshape(1, CELLS), *arrays)
    def finish(p, m, g, u):
        return write_out(g, u)

    def redo(p, m, g, u):
        return write_out(g, 0.5 * full_exchange(n, cap, p, m) - 0.1 * g)

    return lax.cond(flag[0] > 0.5, redo, finish, partner, mask, twice, both)


def write_body(parts, g, u, g_out, u_out, sem):
    rows = TILE // parts
    copies = []
    for c in range(parts):
        where = pl.ds(rows * c, rows)
        for i, (src, dst) in enumerate(((g, g_out), (u, u_out))):
            copies.append(pltpu.make_async_copy(src.at[where], dst.at[where], sem.at[i, c]))
    for copy in copies:
        copy.start()
    for copy in copies:
        copy.wait()


def write_out(g, u):
    parts = 4
    vmem = pl.BlockSpec(memory_space=pltpu.VMEM)
    hbm = pl.BlockSpec(memory_space=pltpu.HBM)
    return tuple(pl.pallas_call(
        functools.partial(write_body, parts),
        out_shape=(jax.ShapeDtypeStruct((TILE, TILE), jnp.float32),) * 2,
        in_specs=[vmem, vmem],
        out_specs=(hbm, hbm),
        scratch_shapes=[pltpu.SemaphoreType.DMA((2, parts))],
        compiler_params=pltpu.CompilerParams(vmem_limit_bytes=4 * 1024 * 1024),
    )(g, u))


def solution(mesh):
    consts = tables()

    def run(mask, target, partner, kernels, socs_weights, dose):
        return local([jnp.asarray(t) for t in consts], mask, target, partner, kernels, socs_weights, dose)

    return jax.shard_map(
        run,
        mesh=mesh,
        in_specs=(
            P(("slab", "tile"), None),
            P(("slab", "tile"), None),
            P(("slab", "tile")),
            P(),
            P(),
            P(),
        ),
        out_specs=(P(("slab", "tile"), None), P(("slab", "tile"), None)),
        check_vma=False,
    )
```

```python
import functools
import math

import numpy as np
import jax
import jax.numpy as jnp
from jax import lax
from jax.experimental import pallas as pl
from jax.experimental.pallas import tpu as pltpu
from jax.sharding import PartitionSpec as P

TILE = 512
CELL = 64
MARGIN = 32
BAND = 32
CELLS = 64
SIDE = 8
DOMAIN = 576
GRID = 64
KERNELS = 6
CUTS = (3, 7, 9, 11)
EXTRA = 12
RELAYS = 4
VMEM_LIMIT = 56 * 1024 * 1024
HIGHEST = lax.Precision.HIGHEST
BLUR = (0.0625, 0.25, 0.375, 0.25, 0.0625)


def tables():
    f = np.arange(BAND) - BAND // 2
    norm = 0.5 / math.sqrt(DOMAIN * TILE)
    ph_x = np.zeros((2, SIDE, BAND, 128))
    for h in range(2):
        ang = 2 * np.pi * np.outer(1 + 2 * np.arange(SIDE) + h, f) / 18.0
        ph_x[0, :, :, 64 * h : 64 * h + 64] = norm * np.cos(ang)[:, :, None]
        ph_x[1, :, :, 64 * h : 64 * h + 64] = norm * np.sin(ang)[:, :, None]
    ang = 2 * np.pi * np.outer(np.arange(SIDE), f) / 8.0
    ph_y = np.stack([np.tile(np.cos(ang), (1, 4)), np.tile(np.sin(ang), (1, 4))])
    ang = 2 * np.pi * f * 16 / 18.0
    one = np.ones((1, 32))
    cos16, sin16 = np.cos(ang)[:, None] * one, np.sin(ang)[:, None] * one
    sh = np.stack(
        [np.concatenate([cos16] * 4, 1), np.concatenate([-sin16, sin16] * 2, 1)]
    )
    q = np.arange(CELL)
    cy = np.cos(2 * np.pi * np.outer(f, q) / TILE)
    sy = np.sin(2 * np.pi * np.outer(f, q) / TILE)
    by = np.zeros((256, 512))
    for i in range(4):
        r, o = 64 * i, 64 * i
        by[r : r + 32, o : o + 64] = cy
        by[r : r + 32, 256 + o : 256 + o + 64] = sy
        by[r + 32 : r + 64, o : o + 64] = -sy
        by[r + 32 : r + 64, 256 + o : 256 + o + 64] = cy
    r32 = np.arange(32)
    cx = np.cos(2 * np.pi * np.outer(r32, f) / DOMAIN)
    sx = np.sin(2 * np.pi * np.outer(r32, f) / DOMAIN)
    lx = np.zeros((256, 512))
    for j in range(8):
        k = 32 * j
        lx[k : k + 32, k : k + 32] = cx
        lx[k : k + 32, 256 + k : 256 + k + 32] = -sx
    m = np.arange(GRID)
    c = np.cos(2 * np.pi * np.outer(f, m) / GRID)
    s = np.sin(2 * np.pi * np.outer(f, m) / GRID)
    yt = np.zeros((128, 128))
    yt[:32, :64], yt[:32, 64:], yt[32:64, :64], yt[32:64, 64:] = c, s, -s, c
    x1 = np.concatenate([c.T, s.T], 1) / BAND
    x2 = np.concatenate([c, s], 1) / BAND
    y2 = np.zeros((128, 128))
    half = np.concatenate([np.concatenate([c.T, -s.T], 1), np.concatenate([s.T, c.T], 1)], 0)
    y2[:, :64], y2[:, 64:] = half, half
    g = np.arange(-31, 32)

    def interp(extent):
        d = np.arange(extent)[:, None] / extent - m[None, :] / GRID
        return np.cos(2 * np.pi * g[:, None, None] * d[None]).sum(0) / GRID

    ux = interp(DOMAIN)
    ux = sum(BLUR[i] * ux[MARGIN - 2 + i : MARGIN - 2 + i + TILE] for i in range(5))
    uy = interp(TILE)
    uy = sum(BLUR[i] * np.roll(uy, i - 2, axis=0) for i in range(5))
    uyt = np.concatenate([uy.T, uy.T], 0)
    uy2 = np.concatenate([uy, uy], 1)
    whole = [ph_x, ph_y, sh, yt, x1, x2, y2, ux, uyt]
    return [np.ascontiguousarray(t, dtype=np.float32) for t in whole] + [
        split(np.ascontiguousarray(t, dtype=np.float32)) for t in (by, lx, lx.T, ux.T, uy2)
    ]


def split(t):
    hi = t.astype(jnp.bfloat16)
    return np.stack([hi, (t - hi.astype(np.float32)).astype(jnp.bfloat16)])


def dot(x, y):
    return jnp.dot(x, y, precision=HIGHEST, preferred_element_type=jnp.float32)


def halves(x):
    hi = x.astype(jnp.bfloat16)
    return hi, (x - hi.astype(jnp.float32)).astype(jnp.bfloat16)


def dot3(x, y, dims=((1,), (0,))):
    def one(p, q):
        return lax.dot_general(p, q, (dims, ((), ())), preferred_element_type=jnp.float32)

    return one(x[0], y[0]) + (one(x[0], y[1]) + one(x[1], y[0]))


def build_tables(n, cap, mates, index_out, meta_out):
    direct, lines = cap // 2, n // 8
    row = jnp.concatenate([mates[...], mates[...]], axis=1)
    square = jnp.broadcast_to(row, (128, 128))
    across, down = square[0:CELLS], square.T[0:CELLS]
    lane = lax.broadcasted_iota(jnp.int32, (CELLS, 128), 1)
    cell = lax.broadcasted_iota(jnp.int32, (CELLS, 128), 0)
    own_r, pos_r, own_c, pos_c = across >> 6, across & 63, down >> 6, down & 63
    valid = lane < CELLS

    def over_cells(mask):
        return jnp.sum(jnp.where(mask, 1, 0), axis=0, keepdims=True)

    def over_lanes(mask):
        return jnp.sum(jnp.where(mask & valid, 1, 0), axis=1, keepdims=True)

    same = own_r == own_c
    rank_r = over_cells(same & (pos_c < pos_r))
    recv_r = over_cells(same & (cell < lane))
    rank_c = over_lanes(same & (pos_r < pos_c))
    spare_c = jnp.broadcast_to(rank_c, (CELLS, 128)) >= direct
    spare_r = jnp.broadcast_to(rank_r, (CELLS, 128)) >= direct
    ahead_r = over_cells(spare_c & (own_c < own_r))
    ahead_c = over_lanes(spare_r & (own_r < own_c))
    hit = own_c * cap + rank_c == lane
    own, pos, first = own_r[0:1], pos_r[0:1], lane[0:1] < CELLS
    kind = jnp.where(pos < SIDE, 0, jnp.where(pos >= CELLS - SIDE, 2, 1))
    recv = jnp.where(
        recv_r < direct, own * direct + recv_r,
        n * direct + jnp.minimum(ahead_r + recv_r - direct, EXTRA - 1),
    )
    index_out[0:1] = jnp.max(jnp.where(hit, cell, 0), axis=0, keepdims=True)
    index_out[1:2] = jnp.min(jnp.where(hit, pos_c, CELLS), axis=0, keepdims=True)
    index_out[2:3] = jnp.where(first, recv, own * 3 + kind)
    index_out[3:4] = jnp.where(
        first, pos,
        jnp.max(jnp.where(spare_c & (ahead_c + rank_c - direct == lane - CELLS), cell, 0), axis=0, keepdims=True),
    )
    index_out[4:8] = jnp.zeros((4, 128), jnp.int32)
    meta_out[...] = jnp.zeros(meta_out.shape, jnp.int32)
    for h in range(lines):
        dest = (lane + 128 * h) >> 4
        meta_out[h : h + 1] = over_cells(spare_c & (own_c == dest))
        meta_out[lines + h : lines + h + 1] = over_cells(spare_c & (own_c < dest))


def body(n, cap, n_in, wts, dose, tab, *refs):
    hbm, outs = refs[:n_in], refs[n_in : n_in + 3]
    vm = refs[n_in + 3 : 2 * n_in + 3]
    load_sem = refs[2 * n_in + 3]
    (
        mask, target, kraw, ph_x, ph_y, sh, yt, x1, x2, y2, ux, uyt, by, lx, lxt, uxt, uy2
    ) = vm
    main(n, cap, tab, wts, dose, hbm, vm, load_sem,
         mask, target, kraw, ph_x, ph_y, sh, yt, x1, x2, y2, ux, uyt, by, lx, lxt, uxt, uy2,
         *outs, *refs[2 * n_in + 4 :])


def main(
    n, cap, tab, wts, dose, hbm, vm, load_sem,
    mask, target, kraw, ph_x, ph_y, sh, yt, x1, x2, y2, ux, uyt, by, lx, lxt, uxt, uy2,
    grad_out, upd_out, flag_out, pc, ps,
    out_cells, in_cells, tiles, plane, vv, wide, part, shared, top, bot, spec_in, acc_all, acc2, acc2s, rhs, rhs2, stack,
    kr, ki, mates, ix_v, ix, tab_sem, mask_sem, out_ov, in_ov, out2, in2, meta_out, meta_in, route_v, route, flag_mine, flag_in,
    ov_send, ov_recv, meta_send, meta_recv, hop_send, hop_recv, flag_send, flag_recv,
    cell_send, cell_recv, spec_send, spec_recv, acc_send, acc_recv,
):
    me = lax.axis_index("tile")
    lane = lax.broadcasted_iota(jnp.int32, (32, 128), 1)
    low = lane < 64
    slabs = lax.axis_size("slab")
    slab = lax.axis_index("slab")
    direct = cap // 2
    first = n // 4
    relay = (me - first) // 2
    is_relay = (me >= first) & (me < first + 2 * RELAYS) & (lax.rem(me, 2) == 0)

    def swap(x):
        return jnp.where(lane % 64 < 32, pltpu.roll(x, 96, 1), pltpu.roll(x, 32, 1))

    def pair(x, y):
        rx, ry = pltpu.roll(x, 64, 1), pltpu.roll(y, 64, 1)
        return jnp.where(low, x, ry), jnp.where(low, rx, y)

    def to_tiles(src, start=0, stop=SIDE):
        @pl.loop(start, stop)
        def _(a):
            r = pl.multiple_of(a * 64, 64)
            for b in range(4):
                h0 = src[pl.ds(r, 32), 128 * b : 128 * b + 128]
                h1 = src[pl.ds(r + 32, 32), 128 * b : 128 * b + 128]
                x, y = pair(h0, h1)
                tiles[a * 8 + 2 * b] = x
                tiles[a * 8 + 2 * b + 1] = y

    def compact(x):
        return jnp.where(low[0:16], x[0:16], x[16:32])

    def expand(x):
        r = pltpu.roll(x, 64, 1)
        return jnp.concatenate([jnp.where(low[0:16], x, r), jnp.where(low[0:16], r, x)], axis=0)

    chips = n // 2
    core = lax.rem(me, 2)
    chip = me // 2
    half = chips // 2
    low_chip, high_chip = lax.rem(chip, half), chip // half
    mine = core * chips + 2 * low_chip
    across = 2 * (low_chip + half * (1 - high_chip)) + core

    def place(t):
        return lax.rem(t, 2) * chips + 2 * lax.rem(t // 2, half) + t // 2 // half

    def peer_of(k):
        return jnp.bitwise_xor(me, k)

    barrier = pltpu.get_barrier_semaphore()

    partner_load = pltpu.make_async_copy(tab, mates, tab_sem.at[1])
    partner_load.start()
    rows = TILE // 4
    mask_loads = [
        pltpu.make_async_copy(hbm[0].at[pl.ds(rows * c, rows)], mask.at[pl.ds(rows * c, rows)], mask_sem.at[c])
        for c in range(4)
    ]
    for load in mask_loads:
        load.start()

    @pl.loop(1, n)
    def _(k):
        pl.semaphore_signal(barrier, inc=1, device_id={"tile": peer_of(k)}, device_id_type=pl.DeviceIdType.MESH)

    for k in range(1, slabs):
        pl.semaphore_signal(
            barrier, inc=1, device_id={"slab": lax.rem(slab + k, slabs)}, device_id_type=pl.DeviceIdType.MESH
        )

    partner_load.wait()
    build_tables(n, cap, mates, ix_v, meta_out)
    index_load = pltpu.make_async_copy(ix_v, ix, tab_sem.at[0])
    index_load.start()

    for c in range(4):
        mask_loads[c].wait()
        to_tiles(mask, 2 * c, 2 * c + 2)

    in_cells[pl.ds(me * direct, direct)] = jnp.zeros((direct, 32, 128), jnp.float32)
    index_load.wait()

    @pl.loop(0, EXTRA, unroll=4)
    def _(o):
        x = tiles[ix[3, CELLS + o]]
        for q in range(RELAYS):
            out_ov[q, o] = x[8 * q : 8 * q + 8]

    pl.semaphore_wait(barrier, n + slabs - 2)

    def to_relay(q, source):
        where = {"device_id": {"tile": first + 2 * q}, "device_id_type": pl.DeviceIdType.MESH}
        return (
            pltpu.make_async_remote_copy(
                src_ref=meta_out, dst_ref=meta_in.at[source],
                send_sem=meta_send.at[q], recv_sem=meta_recv.at[source], **where,
            ),
            pltpu.make_async_remote_copy(
                src_ref=out_ov.at[q], dst_ref=in_ov.at[pl.ds(source * EXTRA, EXTRA)],
                send_sem=ov_send.at[q], recv_sem=ov_recv.at[source], **where,
            ),
        )

    for q in range(RELAYS):
        @pl.when(me != first + 2 * q)
        def _():
            for copy in to_relay(q, me):
                copy.start()
    loads = [pltpu.make_async_copy(hbm[i], vm[i], load_sem.at[i]) for i in range(1, len(hbm))]
    for load in loads:
        load.start()


    def cell_copy(k):
        to = peer_of(k)
        return pltpu.make_async_remote_copy(
            src_ref=out_cells.at[to], dst_ref=in_cells.at[pl.ds(me * direct, direct)],
            send_sem=cell_send.at[k], recv_sem=cell_recv.at[k],
            device_id={"tile": to}, device_id_type=pl.DeviceIdType.MESH,
        )

    cuts = [(n - 1) * c // 15 for c in (0,) + CUTS + (15,)]

    def offset_of(j):
        return jnp.where(lax.rem(j, 2) == 0, n // 2 + j // 2, n // 2 - 1 - j // 2)

    def pack(k):
        to = peer_of(k)
        for r in range(direct):
            out_cells[to, r] = tiles[ix[0, to * cap + r]]

    def start_cells(stage):
        @pl.loop(cuts[stage], cuts[stage + 1])
        def _(j):
            cell_copy(offset_of(j)).start()

    @pl.loop(cuts[0], cuts[1])
    def _(j):
        pack(offset_of(j))
        cell_copy(offset_of(j)).start()

    @pl.loop(cuts[1], n - 1)
    def _(j):
        pack(offset_of(j))

    for load in loads:
        load.wait()

    zero = jnp.zeros((32, 128), jnp.float32)
    lane_sign = jnp.where(lane % 64 < 32, -1.0, 1.0)

    @pl.loop(0, SIDE)
    def _(a):
        c, s = ph_x[0, a], ph_x[1, a]
        for b in range(SIDE):
            cb, sb = ph_y[0, b : b + 1, :], ph_y[1, b : b + 1, :]
            pc[a * 8 + b] = c * cb - s * sb
            ps[a * 8 + b] = (s * cb + c * sb) * lane_sign

    pc[CELLS] = zero
    ps[CELLS] = zero

    lxt_pair = lxt[0], lxt[1]
    for g in range(2):
        vv[g] = dot3(lxt_pair, halves(mask[256 * g : 256 * g + 256, :]))
    for g in range(2):
        for c in range(2):
            cols = slice(256 * c, 256 * c + 256)
            left = jnp.concatenate([vv[g, 0:256, cols], vv[g, 256:512, cols]], axis=1)
            plane[256 * g : 256 * g + 256, cols] = dot3(halves(left), (by[0], by[1]), ((1,), (1,)))
    to_tiles(plane)

    top[n] = zero
    bot[0] = zero

    @pl.loop(0, n, unroll=4)
    def _(t):
        sums = [zero] * 6
        for r in range(cap):
            s = t * cap + r
            x = tiles[ix[0, s]]
            p = ix[1, s]
            u, w = x * pc[p], x * ps[p]
            wt = jnp.where(p < 8, 1.0, 0.0)
            wb = jnp.where(p >= 56, 1.0, 0.0)
            sums = [
                sums[0] + u, sums[1] + w, sums[2] + wt * u, sums[3] + wt * w,
                sums[4] + wb * u, sums[5] + wb * w,
            ]
        wide[t] = sums[0] + swap(sums[1])
        top[t] = sums[2] + swap(sums[3])
        bot[t + 1] = sums[4] + swap(sums[5])

    def own_row(a, carry):
        u, w = carry
        for b in range(8):
            x = tiles[a * 8 + b]
            u, w = u + x * pc[a * 8 + b], w + x * ps[a * 8 + b]
        return u, w

    u0, w0 = own_row(0, (zero, zero))
    u7, w7 = own_row(7, (zero, zero))
    u, w = lax.fori_loop(1, 7, own_row, (u0 + u7, w0 + w7))
    wide[me] += u + swap(w)
    top[me] += u0 + swap(w0)
    bot[me + 1] += u7 + swap(w7)

    @pl.loop(0, n, unroll=8)
    def _(t):
        tp = jnp.where(low, top[t + 1], 0.0)
        bt = jnp.where(low, 0.0, bot[t])
        tp = tp + pltpu.roll(tp, 64, 1)
        bt = bt + pltpu.roll(bt, 64, 1)
        x = wide[t]
        x = x + pltpu.roll(x, 64, 1)
        both = (tp + bt) * sh[0] + pltpu.roll((bt - tp), 32, 1) * sh[1]
        part[place(t)] = compact(x + both)

    def spec_copy(k):
        to = jnp.bitwise_xor(chip, k)
        return pltpu.make_async_remote_copy(
            src_ref=part.at[place(2 * to + core)], dst_ref=spec_in.at[chip],
            send_sem=spec_send.at[k], recv_sem=spec_recv.at[k],
            device_id={"tile": 2 * to + core}, device_id_type=pl.DeviceIdType.MESH,
        )

    other = pl.ds((1 - core) * chips, chips)
    share = pltpu.make_async_remote_copy(
        src_ref=part.at[other], dst_ref=shared, send_sem=spec_send.at[0], recv_sem=spec_recv.at[0],
        device_id={"tile": jnp.bitwise_xor(me, 1)}, device_id_type=pl.DeviceIdType.MESH,
    )
    share.start()
    share.wait_recv()
    own_part = pl.ds(core * chips, chips)
    part[own_part] = part[own_part] + shared[...]

    @pl.loop(1, chips)
    def _(k):
        spec_copy(k).start()

    start_cells(1)

    def flag_copy(k):
        to = lax.rem(slab + k, slabs)
        return pltpu.make_async_remote_copy(
            src_ref=flag_mine, dst_ref=flag_in.at[k],
            send_sem=flag_send.at[k], recv_sem=flag_recv.at[k],
            device_id={"slab": to}, device_id_type=pl.DeviceIdType.MESH,
        )

    def hop_copy(k, source):
        to = peer_of(k)
        return pltpu.make_async_remote_copy(
            src_ref=out2.at[to], dst_ref=in2.at[source],
            send_sem=hop_send.at[k], recv_sem=hop_recv.at[source],
            device_id={"tile": to}, device_id_type=pl.DeviceIdType.MESH,
        )

    spec_in[chip] = part[place(me)]

    for k in range(KERNELS):
        rows = slice(32 * k, 32 * k + 32)
        re, im = kraw[64 * k : 64 * k + 32, :], kraw[64 * k + 32 : 64 * k + 64, :]
        kr[rows, :] = jnp.concatenate([re] * 4, axis=1)
        ki[rows, :] = jnp.concatenate([-im, im] * 2, axis=1)

    @pl.loop(1, chips)
    def _(k):
        spec_copy(k).wait_recv()

    start_cells(2)
    spec = expand(sum((spec_in[t] for t in range(1, chips)), spec_in[0]))

    spec_s = pltpu.roll(spec, 32, 1)
    for k in range(KERNELS):
        rows = slice(32 * k, 32 * k + 32)
        stack[rows, :] = spec * kr[rows, :] + spec_s * ki[rows, :]
    fields_y = dot(stack[...], yt[...])
    sign = jnp.where(low, -1.0, 1.0)
    for k in range(KERNELS):
        part_k = fields_y[32 * k : 32 * k + 32]
        rhs[0:32, 128 * k : 128 * k + 128] = part_k
        rhs[32:64, 128 * k : 128 * k + 128] = pltpu.roll(part_k, 64, 1) * sign
    fields = dot(x1[...], rhs[...])
    inten = jnp.zeros((64, 128), jnp.float32)
    for k in range(KERNELS):
        e = fields[:, 128 * k : 128 * k + 128]
        inten = inten + wts[k] * (e * e)
    blurred = dot(ux[...], dot(inten, uyt[...]))
    d = dose[0]
    resist = jax.nn.sigmoid(4.0 * (d * blurred - 1.0))
    slope = 2.0 * (resist - target[...]) * (4.0 * d) * resist * (1.0 - resist)
    grad_i = dot3((uxt[0], uxt[1]), halves(dot3(halves(slope), (uy2[0], uy2[1]))))
    lane2 = lax.broadcasted_iota(jnp.int32, (64, 128), 1)
    sign2 = jnp.where(lane2 < 64, 1.0, -1.0)
    for k in range(KERNELS):
        ge = (2.0 * wts[k]) * grad_i * fields[:, 128 * k : 128 * k + 128]
        rhs2[0:64, 128 * k : 128 * k + 128] = ge
        rhs2[64:128, 128 * k : 128 * k + 128] = pltpu.roll(ge, 64, 1) * sign2
    grad_y = dot(x2[...], rhs2[...])
    for k in range(KERNELS):
        stack[32 * k : 32 * k + 32, :] = grad_y[:, 128 * k : 128 * k + 128]
    grad_a = dot(stack[...], y2[...])
    acc = zero
    for k in range(KERNELS):
        rows = slice(32 * k, 32 * k + 32)
        ga = grad_a[rows]
        acc = acc + kr[rows, :] * ga - ki[rows, :] * pltpu.roll(ga, 32, 1)
    acc_all[place(me)] = compact(acc)

    def acc_copy(k):
        to = jnp.bitwise_xor(low_chip, k)
        return pltpu.make_async_remote_copy(
            src_ref=acc_all.at[pl.ds(mine, 2)], dst_ref=acc_all.at[pl.ds(mine, 2)],
            send_sem=acc_send.at[k], recv_sem=acc_recv.at[k],
            device_id={"tile": 2 * (to + half * high_chip) + core}, device_id_type=pl.DeviceIdType.MESH,
        )

    acc_cross = pltpu.make_async_remote_copy(
        src_ref=acc_all.at[place(me)], dst_ref=acc_all.at[place(me)],
        send_sem=acc_send.at[half], recv_sem=acc_recv.at[half],
        device_id={"tile": across}, device_id_type=pl.DeviceIdType.MESH,
    )
    acc_cross.start()
    start_cells(3)
    acc_cross.wait_recv()

    @pl.loop(1, half)
    def _(k):
        acc_copy(k).start()

    start_cells(4)

    @pl.when(is_relay)
    def _():
        meta_in[me] = meta_out[...]
        in_ov[pl.ds(me * EXTRA, EXTRA)] = out_ov[relay]

        @pl.loop(1, n)
        def _(k):
            for copy in to_relay(0, peer_of(k)):
                copy.wait_recv()

        lines = n // 8
        slot = lax.broadcasted_iota(jnp.int32, (lines, 128), 1) % 16
        start = jnp.zeros((lines, 128), jnp.int32)
        found = jnp.zeros((lines, 128), jnp.int32)
        most = jnp.zeros((lines, 128), jnp.int32)
        for i in range(n):
            count, offset = meta_in[i, 0:lines], meta_in[i, lines : 2 * lines]
            rel = slot - start
            found = jnp.where((rel >= 0) & (rel < count), i * EXTRA + offset + rel, found)
            start = start + count
            most = jnp.maximum(most, count + offset)
        route_v[...] = jnp.zeros((8, 128), jnp.int32)
        route_v[0:lines] = jnp.clip(found, 0, n * EXTRA - 1)
        over = jnp.broadcast_to(jnp.max(jnp.where(most > EXTRA, 1.0, 0.0)), (8, 128))
        route_copy = pltpu.make_async_copy(route_v, route, tab_sem.at[2])
        route_copy.start()
        flag_mine[...] = over

        @pl.when(me == first)
        def _():
            for k in range(1, slabs):
                flag_copy(k).start()

        route_copy.wait()

        @pl.loop(0, n)
        def _(d):
            for m in range(EXTRA):
                out2[d, m] = in_ov[route[d // 8, lax.rem(d, 8) * 16 + m]]

        flag_in[0] = over

        @pl.when(me == first)
        def _():
            for k in range(1, slabs):
                flag_copy(k).wait()
                flag_in[0] = jnp.maximum(flag_in[0], flag_in[k])

        @pl.loop(0, n)
        def _(d):
            out2[d, EXTRA] = flag_in[0]

        @pl.loop(1, n)
        def _(k):
            hop_copy(k, relay).start()

        in2[relay] = out2[me]

    @pl.loop(1, half)
    def _(k):
        acc_copy(k).wait_recv()

    give = pltpu.make_async_remote_copy(
        src_ref=acc_all.at[own_part], dst_ref=acc_all.at[own_part],
        send_sem=acc_send.at[0], recv_sem=acc_recv.at[0],
        device_id={"tile": jnp.bitwise_xor(me, 1)}, device_id_type=pl.DeviceIdType.MESH,
    )
    give.start()
    give.wait_recv()


    @pl.loop(0, n, unroll=8)
    def _(t):
        mid = expand(acc_all[place(t)])
        before = expand(acc_all[place(jnp.maximum(t - 1, 0))]) * jnp.where(t > 0, 1.0, 0.0)
        after = expand(acc_all[place(jnp.minimum(t + 1, n - 1))]) * jnp.where(t < n - 1, 1.0, 0.0)
        first = mid + before * sh[0] + pltpu.roll(before, 32, 1) * sh[1]
        last = mid + after * sh[0] - pltpu.roll(after, 32, 1) * sh[1]
        mid_s, first_s, last_s = (pltpu.roll(v, 32, 1) for v in (mid, first, last))
        acc2[t * 3] = jnp.where(low, first, mid)
        acc2[t * 3 + 1] = mid
        acc2[t * 3 + 2] = jnp.where(low, mid, last)
        acc2s[t * 3] = jnp.where(low, first_s, mid_s)
        acc2s[t * 3 + 1] = mid_s
        acc2s[t * 3 + 2] = jnp.where(low, mid_s, last_s)

    @pl.loop(0, SIDE, unroll=2)
    def _(a):
        r = pl.multiple_of(a * 64, 64)
        own = me * 3 + jnp.where(a == 0, 0, jnp.where(a == SIDE - 1, 2, 1))
        own_x, own_s = acc2[own], acc2s[own]
        for b in range(4):
            pieces = []
            for i in range(2):
                c = a * 8 + 2 * b + i
                g, p = ix[2, CELLS + c], ix[3, c]
                pieces.append(own_x * pc[c] + own_s * ps[c] + acc2[g] * pc[p] + acc2s[g] * ps[p])
            h0, h1 = pair(*pieces)
            plane[pl.ds(r, 32), 128 * b : 128 * b + 128] = h0
            plane[pl.ds(r + 32, 32), 128 * b : 128 * b + 128] = h1

    for c in range(2):
        for g in range(2):
            v = dot3(halves(plane[256 * g : 256 * g + 256, 256 * c : 256 * c + 256]), (by[0], by[1]))
            vv[g, 0:256, 256 * c : 256 * c + 256] = v[:, 0:256]
            vv[g, 256:512, 256 * c : 256 * c + 256] = v[:, 256:512]
    for g in range(2):
        grad_out[256 * g : 256 * g + 256, :] = dot3((lx[0], lx[1]), halves(vv[g]))

    @pl.loop(0, SIDE)
    def _(a):
        r = pl.multiple_of(a * 64, 64)
        for b in range(4):
            for h in range(2):
                where = (pl.ds(r + 32 * h, 32), slice(128 * b, 128 * b + 128))
                upd_out[where] = 0.5 * mask[where] - 0.1 * grad_out[where]

    @pl.loop(1, n)
    def _(k):
        cell_copy(k).wait_send()

    @pl.loop(1, chips)
    def _(k):
        spec_copy(k).wait_send()

    @pl.loop(1, half)
    def _(k):
        acc_copy(k).wait_send()

    acc_cross.wait_send()

    share.wait_send()
    give.wait_send()

    for q in range(RELAYS):
        @pl.when(me != first + 2 * q)
        def _():
            for copy in to_relay(q, me):
                copy.wait_send()

    @pl.when(is_relay)
    def _():
        @pl.loop(1, n)
        def _(k):
            hop_copy(k, relay).wait_send()

    @pl.loop(1, n)
    def _(k):
        cell_copy(k).wait_recv()

    for q in range(RELAYS):
        @pl.when(me != first + 2 * q)
        def _():
            hop_copy(1, q).wait_recv()

    flag_out[0] = in2[0, EXTRA][0, 0]
    for m in range(EXTRA):
        in_cells[n * direct + m] = jnp.concatenate([in2[q, m] for q in range(RELAYS)], axis=0)

    @pl.loop(0, SIDE, unroll=2)
    def _(a):
        r = pl.multiple_of(a * 64, 64)
        for b in range(4):
            c = a * 8 + 2 * b
            both = pair(in_cells[ix[2, c]],
                          in_cells[ix[2, c + 1]])
            for h in range(2):
                where = (pl.ds(r + 32 * h, 32), slice(128 * b, 128 * b + 128))
                upd_out[where] = upd_out[where] + 0.5 * both[h]


def full_body(n, cap, tab, mask_hbm, both_out, mask, ix, tiles, out_cells, in_cells, tab_sem, cell_send, cell_recv):
    me = lax.axis_index("tile")
    low = lax.broadcasted_iota(jnp.int32, (32, 128), 1) < 64

    def pair(x, y):
        rx, ry = pltpu.roll(x, 64, 1), pltpu.roll(y, 64, 1)
        return jnp.where(low, x, ry), jnp.where(low, rx, y)

    barrier = pltpu.get_barrier_semaphore()

    @pl.loop(1, n)
    def _(k):
        pl.semaphore_signal(
            barrier, inc=1, device_id={"tile": jnp.bitwise_xor(me, k)}, device_id_type=pl.DeviceIdType.MESH
        )

    index_load = pltpu.make_async_copy(tab.at[pl.ds(0, 8)], ix, tab_sem.at[0])
    index_load.start()
    mask_load = pltpu.make_async_copy(mask_hbm, mask, tab_sem.at[1])
    mask_load.start()
    mask_load.wait()

    @pl.loop(0, SIDE)
    def _(a):
        r = pl.multiple_of(a * 64, 64)
        for b in range(4):
            h0 = mask[pl.ds(r, 32), 128 * b : 128 * b + 128]
            h1 = mask[pl.ds(r + 32, 32), 128 * b : 128 * b + 128]
            tiles[a * 8 + 2 * b], tiles[a * 8 + 2 * b + 1] = pair(h0, h1)

    index_load.wait()

    @pl.loop(0, n)
    def _(to):
        for r in range(cap):
            out_cells[to, r] = tiles[ix[0, to * cap + r]]

    in_cells[pl.ds(me * cap, cap)] = out_cells[me]
    pl.semaphore_wait(barrier, n - 1)

    def cell_copy(k):
        to = jnp.bitwise_xor(me, k)
        return pltpu.make_async_remote_copy(
            src_ref=out_cells.at[to], dst_ref=in_cells.at[pl.ds(me * cap, cap)],
            send_sem=cell_send.at[k], recv_sem=cell_recv.at[k],
            device_id={"tile": to}, device_id_type=pl.DeviceIdType.MESH,
        )

    @pl.loop(1, n)
    def _(k):
        cell_copy(k).start()

    @pl.loop(1, n)
    def _(k):
        cell_copy(k).wait()

    @pl.loop(0, SIDE)
    def _(a):
        r = pl.multiple_of(a * 64, 64)
        for b in range(4):
            c = a * 8 + 2 * b
            halves_of = pair(in_cells[ix[1, c]], in_cells[ix[1, c + 1]])
            for h in range(2):
                where = (pl.ds(r + 32 * h, 32), slice(128 * b, 128 * b + 128))
                both_out[where] = mask[where] + halves_of[h]


def full_exchange(n, cap, partner, mask):
    owner = partner // CELLS
    pos = partner % CELLS
    ids = jnp.arange(CELLS, dtype=jnp.int32)
    same = owner[:, None] == owner[None, :]
    send_rank = jnp.sum((same & (pos[None, :] < pos[:, None])).astype(jnp.int32), axis=1)
    recv_rank = jnp.sum((same & (ids[None, :] < ids[:, None])).astype(jnp.int32), axis=1)
    send_slot = owner * cap + send_rank
    recv_slot = owner * cap + recv_rank
    hit = (jnp.arange(n * cap, dtype=jnp.int32)[:, None] == send_slot[None, :]).astype(jnp.int32)
    slot_cell = jnp.sum(hit * ids[None, :], axis=1)
    tab = jnp.concatenate([slot_cell, recv_slot, recv_slot, jnp.zeros((6 * 128,), jnp.int32)]).reshape(8, 128)
    f32 = jnp.float32
    dma = pltpu.SemaphoreType.DMA((n,))
    vmem = pl.BlockSpec(memory_space=pltpu.VMEM)
    return pl.pallas_call(
        functools.partial(full_body, n, cap),
        out_shape=jax.ShapeDtypeStruct((TILE, TILE), f32),
        in_specs=[pl.BlockSpec(memory_space=pl.ANY), pl.BlockSpec(memory_space=pltpu.HBM)],
        out_specs=vmem,
        scratch_shapes=[
            pltpu.VMEM((TILE, TILE), f32),
            pltpu.SMEM((8, 128), jnp.int32),
            pltpu.VMEM((CELLS, 32, 128), f32),
            pltpu.VMEM((n, cap, 32, 128), f32),
            pltpu.VMEM((n * cap, 32, 128), f32),
            pltpu.SemaphoreType.DMA((2,)),
            dma, dma,
        ],
        compiler_params=pltpu.CompilerParams(
            collective_id=1, has_side_effects=True, vmem_limit_bytes=32 * 1024 * 1024
        ),
    )(tab, mask)


def local(consts, mask, target, partner, kernels, socs_weights, dose):
    n = lax.axis_size("tile")
    cap, direct = 2 * CELLS // n, CELLS // n
    meta_lines = (2 * n // 8 + 7) // 8 * 8
    raw = kernels.reshape(2 * KERNELS * BAND, BAND)
    f32 = jnp.float32
    vmem = pl.BlockSpec(memory_space=pltpu.VMEM)
    hbm = pl.BlockSpec(memory_space=pltpu.HBM)
    arrays = [mask, target, raw, *consts]
    smem = pl.BlockSpec(memory_space=pltpu.SMEM)
    dma, few = pltpu.SemaphoreType.DMA((n,)), pltpu.SemaphoreType.DMA((RELAYS,))
    flags = pltpu.SemaphoreType.DMA((lax.axis_size("slab"),))
    twice, both, flag = pl.pallas_call(
        functools.partial(body, n, cap, len(arrays)),
        out_shape=(jax.ShapeDtypeStruct((TILE, TILE), f32),) * 2 + (jax.ShapeDtypeStruct((1,), f32),),
        in_specs=[smem] * 2 + [hbm] + [hbm] * len(arrays),
        out_specs=(vmem, vmem, smem),
        scratch_shapes=[pltpu.VMEM(x.shape, x.dtype) for x in arrays] + [
            pltpu.SemaphoreType.DMA((len(arrays),)),
            pltpu.VMEM((CELLS + 1, 32, 128), f32),
            pltpu.VMEM((CELLS + 1, 32, 128), f32),
            pltpu.VMEM((n, direct, 32, 128), f32),
            pltpu.VMEM((n * direct + EXTRA, 32, 128), f32),
            pltpu.VMEM((CELLS, 32, 128), f32),
            pltpu.VMEM((TILE, TILE), f32),
            pltpu.VMEM((2, 512, 512), f32),
            pltpu.VMEM((n, 32, 128), f32),
            pltpu.VMEM((n, 16, 128), f32),
            pltpu.VMEM((n // 2, 16, 128), f32),
            pltpu.VMEM((n + 1, 32, 128), f32),
            pltpu.VMEM((n + 1, 32, 128), f32),
            pltpu.VMEM((n, 16, 128), f32),
            pltpu.VMEM((n, 16, 128), f32),
            pltpu.VMEM((3 * n, 32, 128), f32),
            pltpu.VMEM((3 * n, 32, 128), f32),
            pltpu.VMEM((64, 768), f32),
            pltpu.VMEM((128, 768), f32),
            pltpu.VMEM((192, 128), f32),
            pltpu.VMEM((192, 128), f32),
            pltpu.VMEM((192, 128), f32),
            pltpu.VMEM((1, CELLS), jnp.int32),
            pltpu.VMEM((8, 128), jnp.int32),
            pltpu.SMEM((8, 128), jnp.int32),
            pltpu.SemaphoreType.DMA((3,)),
            pltpu.SemaphoreType.DMA((4,)),
            pltpu.VMEM((RELAYS, EXTRA, 8, 128), f32),
            pltpu.VMEM((n * EXTRA, 8, 128), f32),
            pltpu.VMEM((n, EXTRA + 1, 8, 128), f32),
            pltpu.VMEM((RELAYS, EXTRA + 1, 8, 128), f32),
            pltpu.VMEM((meta_lines, 128), jnp.int32),
            pltpu.VMEM((n, meta_lines, 128), jnp.int32),
            pltpu.VMEM((8, 128), jnp.int32),
            pltpu.SMEM((8, 128), jnp.int32),
            pltpu.VMEM((8, 128), f32),
            pltpu.VMEM((lax.axis_size("slab"), 8, 128), f32),
            few, dma, few, dma, dma, few, flags, flags,
            dma, dma, dma, dma, dma, dma,
        ],
        compiler_params=pltpu.CompilerParams(
            collective_id=0, has_side_effects=True, vmem_limit_bytes=VMEM_LIMIT
        ),
    )(socs_weights, dose, partner.reshape(1, CELLS), *arrays)
    def finish(p, m, g, u):
        return write_out(g, u)

    def redo(p, m, g, u):
        return write_out(g, 0.5 * full_exchange(n, cap, p, m) - 0.1 * g)

    return lax.cond(flag[0] > 0.5, redo, finish, partner, mask, twice, both)


def write_body(parts, g, u, g_out, u_out, sem):
    rows = TILE // parts
    copies = []
    for c in range(parts):
        where = pl.ds(rows * c, rows)
        for i, (src, dst) in enumerate(((g, g_out), (u, u_out))):
            copies.append(pltpu.make_async_copy(src.at[where], dst.at[where], sem.at[i, c]))
    for copy in copies:
        copy.start()
    for copy in copies:
        copy.wait()


def write_out(g, u):
    parts = 4
    vmem = pl.BlockSpec(memory_space=pltpu.VMEM)
    hbm = pl.BlockSpec(memory_space=pltpu.HBM)
    return tuple(pl.pallas_call(
        functools.partial(write_body, parts),
        out_shape=(jax.ShapeDtypeStruct((TILE, TILE), jnp.float32),) * 2,
        in_specs=[vmem, vmem],
        out_specs=(hbm, hbm),
        scratch_shapes=[pltpu.SemaphoreType.DMA((2, parts))],
        compiler_params=pltpu.CompilerParams(vmem_limit_bytes=4 * 1024 * 1024),
    )(g, u))


def solution(mesh):
    consts = tables()

    def run(mask, target, partner, kernels, socs_weights, dose):
        return local([jnp.asarray(t) for t in consts], mask, target, partner, kernels, socs_weights, dose)

    return jax.shard_map(
        run,
        mesh=mesh,
        in_specs=(
            P(("slab", "tile"), None),
            P(("slab", "tile"), None),
            P(("slab", "tile")),
            P(),
            P(),
            P(),
        ),
        out_specs=(P(("slab", "tile"), None), P(("slab", "tile"), None)),
        check_vma=False,
    )
```

```python
import functools
import math

import numpy as np
import jax
import jax.numpy as jnp
from jax import lax
from jax.experimental import pallas as pl
from jax.experimental.pallas import tpu as pltpu
from jax.sharding import PartitionSpec as P

TILE = 512
CELL = 64
MARGIN = 32
BAND = 32
CELLS = 64
SIDE = 8
DOMAIN = 576
GRID = 64
KERNELS = 6
CUTS = (3, 7, 9, 11)
EXTRA = 12
RELAYS = 4
VMEM_LIMIT = 56 * 1024 * 1024
HIGHEST = lax.Precision.HIGHEST
BLUR = (0.0625, 0.25, 0.375, 0.25, 0.0625)


def tables():
    f = np.arange(BAND) - BAND // 2
    norm = 0.5 / math.sqrt(DOMAIN * TILE)
    ph_x = np.zeros((2, SIDE, BAND, 128))
    for h in range(2):
        ang = 2 * np.pi * np.outer(1 + 2 * np.arange(SIDE) + h, f) / 18.0
        ph_x[0, :, :, 64 * h : 64 * h + 64] = norm * np.cos(ang)[:, :, None]
        ph_x[1, :, :, 64 * h : 64 * h + 64] = norm * np.sin(ang)[:, :, None]
    ang = 2 * np.pi * np.outer(np.arange(SIDE), f) / 8.0
    ph_y = np.stack([np.tile(np.cos(ang), (1, 4)), np.tile(np.sin(ang), (1, 4))])
    ang = 2 * np.pi * f * 16 / 18.0
    one = np.ones((1, 32))
    cos16, sin16 = np.cos(ang)[:, None] * one, np.sin(ang)[:, None] * one
    sh = np.stack(
        [np.concatenate([cos16] * 4, 1), np.concatenate([-sin16, sin16] * 2, 1)]
    )
    q = np.arange(CELL)
    cy = np.cos(2 * np.pi * np.outer(f, q) / TILE)
    sy = np.sin(2 * np.pi * np.outer(f, q) / TILE)
    by = np.zeros((256, 512))
    for i in range(4):
        r, o = 64 * i, 64 * i
        by[r : r + 32, o : o + 64] = cy
        by[r : r + 32, 256 + o : 256 + o + 64] = sy
        by[r + 32 : r + 64, o : o + 64] = -sy
        by[r + 32 : r + 64, 256 + o : 256 + o + 64] = cy
    r32 = np.arange(32)
    cx = np.cos(2 * np.pi * np.outer(r32, f) / DOMAIN)
    sx = np.sin(2 * np.pi * np.outer(r32, f) / DOMAIN)
    lx = np.zeros((256, 512))
    for j in range(8):
        k = 32 * j
        lx[k : k + 32, k : k + 32] = cx
        lx[k : k + 32, 256 + k : 256 + k + 32] = -sx
    m = np.arange(GRID)
    c = np.cos(2 * np.pi * np.outer(f, m) / GRID)
    s = np.sin(2 * np.pi * np.outer(f, m) / GRID)
    yt = np.zeros((128, 128))
    yt[:32, :64], yt[:32, 64:], yt[32:64, :64], yt[32:64, 64:] = c, s, -s, c
    x1 = np.concatenate([c.T, s.T], 1) / BAND
    x2 = np.concatenate([c, s], 1) / BAND
    y2 = np.zeros((128, 128))
    half = np.concatenate([np.concatenate([c.T, -s.T], 1), np.concatenate([s.T, c.T], 1)], 0)
    y2[:, :64], y2[:, 64:] = half, half
    g = np.arange(-31, 32)

    def interp(extent):
        d = np.arange(extent)[:, None] / extent - m[None, :] / GRID
        return np.cos(2 * np.pi * g[:, None, None] * d[None]).sum(0) / GRID

    ux = interp(DOMAIN)
    ux = sum(BLUR[i] * ux[MARGIN - 2 + i : MARGIN - 2 + i + TILE] for i in range(5))
    uy = interp(TILE)
    uy = sum(BLUR[i] * np.roll(uy, i - 2, axis=0) for i in range(5))
    uyt = np.concatenate([uy.T, uy.T], 0)
    uy2 = np.concatenate([uy, uy], 1)
    whole = [ph_x, ph_y, sh, yt, x1, x2, y2, ux, uyt]
    return [np.ascontiguousarray(t, dtype=np.float32) for t in whole] + [
        split(np.ascontiguousarray(t, dtype=np.float32)) for t in (by, lx, lx.T, ux.T, uy2)
    ]


def split(t):
    hi = t.astype(jnp.bfloat16)
    return np.stack([hi, (t - hi.astype(np.float32)).astype(jnp.bfloat16)])


def dot(x, y):
    return jnp.dot(x, y, precision=HIGHEST, preferred_element_type=jnp.float32)


def halves(x):
    hi = x.astype(jnp.bfloat16)
    return hi, (x - hi.astype(jnp.float32)).astype(jnp.bfloat16)


def dot3(x, y, dims=((1,), (0,))):
    def one(p, q):
        return lax.dot_general(p, q, (dims, ((), ())), preferred_element_type=jnp.float32)

    return one(x[0], y[0]) + (one(x[0], y[1]) + one(x[1], y[0]))


def build_tables(n, cap, mates, index_out, meta_out):
    direct, lines = cap // 2, n // 8
    row = jnp.concatenate([mates[...], mates[...]], axis=1)
    square = jnp.broadcast_to(row, (128, 128))
    across, down = square[0:CELLS], square.T[0:CELLS]
    lane = lax.broadcasted_iota(jnp.int32, (CELLS, 128), 1)
    cell = lax.broadcasted_iota(jnp.int32, (CELLS, 128), 0)
    own_r, pos_r, own_c, pos_c = across >> 6, across & 63, down >> 6, down & 63
    valid = lane < CELLS

    def over_cells(mask):
        return jnp.sum(jnp.where(mask, 1, 0), axis=0, keepdims=True)

    def over_lanes(mask):
        return jnp.sum(jnp.where(mask & valid, 1, 0), axis=1, keepdims=True)

    same = own_r == own_c
    rank_r = over_cells(same & (pos_c < pos_r))
    recv_r = over_cells(same & (cell < lane))
    rank_c = over_lanes(same & (pos_r < pos_c))
    spare_c = jnp.broadcast_to(rank_c, (CELLS, 128)) >= direct
    spare_r = jnp.broadcast_to(rank_r, (CELLS, 128)) >= direct
    ahead_r = over_cells(spare_c & (own_c < own_r))
    ahead_c = over_lanes(spare_r & (own_r < own_c))
    hit = own_c * cap + rank_c == lane
    own, pos, first = own_r[0:1], pos_r[0:1], lane[0:1] < CELLS
    kind = jnp.where(pos < SIDE, 0, jnp.where(pos >= CELLS - SIDE, 2, 1))
    recv = jnp.where(
        recv_r < direct, own * direct + recv_r,
        n * direct + jnp.minimum(ahead_r + recv_r - direct, EXTRA - 1),
    )
    index_out[0:1] = jnp.max(jnp.where(hit, cell, 0), axis=0, keepdims=True)
    index_out[1:2] = jnp.min(jnp.where(hit, pos_c, CELLS), axis=0, keepdims=True)
    index_out[2:3] = jnp.where(first, recv, own * 3 + kind)
    index_out[3:4] = jnp.where(
        first, pos,
        jnp.max(jnp.where(spare_c & (ahead_c + rank_c - direct == lane - CELLS), cell, 0), axis=0, keepdims=True),
    )
    index_out[4:8] = jnp.zeros((4, 128), jnp.int32)
    meta_out[...] = jnp.zeros(meta_out.shape, jnp.int32)
    for h in range(lines):
        dest = (lane + 128 * h) >> 4
        meta_out[h : h + 1] = over_cells(spare_c & (own_c == dest))
        meta_out[lines + h : lines + h + 1] = over_cells(spare_c & (own_c < dest))


def body(n, cap, n_in, wts, dose, tab, *refs):
    hbm, outs = refs[:n_in], refs[n_in : n_in + 3]
    vm = refs[n_in + 3 : 2 * n_in + 3]
    load_sem = refs[2 * n_in + 3]
    (
        mask, target, kraw, ph_x, ph_y, sh, yt, x1, x2, y2, ux, uyt, by, lx, lxt, uxt, uy2
    ) = vm
    main(n, cap, tab, wts, dose, hbm, vm, load_sem,
         mask, target, kraw, ph_x, ph_y, sh, yt, x1, x2, y2, ux, uyt, by, lx, lxt, uxt, uy2,
         *outs, *refs[2 * n_in + 4 :])


def main(
    n, cap, tab, wts, dose, hbm, vm, load_sem,
    mask, target, kraw, ph_x, ph_y, sh, yt, x1, x2, y2, ux, uyt, by, lx, lxt, uxt, uy2,
    grad_out, upd_out, flag_out, pc, ps,
    out_cells, in_cells, tiles, plane, vv, wide, part, shared, top, bot, spec_in, acc_all, acc2, acc2s, rhs, rhs2, stack,
    kr, ki, mates, ix_v, ix, tab_sem, mask_sem, out_ov, in_ov, out2, in2, meta_out, meta_in, route_v, route, flag_mine, flag_in,
    ov_send, ov_recv, meta_send, meta_recv, hop_send, hop_recv, flag_send, flag_recv,
    cell_send, cell_recv, spec_send, spec_recv, acc_send, acc_recv,
):
    me = lax.axis_index("tile")
    lane = lax.broadcasted_iota(jnp.int32, (32, 128), 1)
    low = lane < 64
    slabs = lax.axis_size("slab")
    slab = lax.axis_index("slab")
    direct = cap // 2
    first = n // 4
    relay = (me - first) // 2
    is_relay = (me >= first) & (me < first + 2 * RELAYS) & (lax.rem(me, 2) == 0)

    def swap(x):
        return jnp.where(lane % 64 < 32, pltpu.roll(x, 96, 1), pltpu.roll(x, 32, 1))

    def pair(x, y):
        rx, ry = pltpu.roll(x, 64, 1), pltpu.roll(y, 64, 1)
        return jnp.where(low, x, ry), jnp.where(low, rx, y)

    def to_tiles(src, start=0, stop=SIDE):
        @pl.loop(start, stop)
        def _(a):
            r = pl.multiple_of(a * 64, 64)
            for b in range(4):
                h0 = src[pl.ds(r, 32), 128 * b : 128 * b + 128]
                h1 = src[pl.ds(r + 32, 32), 128 * b : 128 * b + 128]
                x, y = pair(h0, h1)
                tiles[a * 8 + 2 * b] = x
                tiles[a * 8 + 2 * b + 1] = y

    def compact(x):
        return jnp.where(low[0:16], x[0:16], x[16:32])

    def expand(x):
        r = pltpu.roll(x, 64, 1)
        return jnp.concatenate([jnp.where(low[0:16], x, r), jnp.where(low[0:16], r, x)], axis=0)

    chips = n // 2
    core = lax.rem(me, 2)
    chip = me // 2
    half = chips // 2
    low_chip, high_chip = lax.rem(chip, half), chip // half
    mine = core * chips + 2 * low_chip
    across = 2 * (low_chip + half * (1 - high_chip)) + core

    def place(t):
        return lax.rem(t, 2) * chips + 2 * lax.rem(t // 2, half) + t // 2 // half

    def peer_of(k):
        return jnp.bitwise_xor(me, k)

    barrier = pltpu.get_barrier_semaphore()

    partner_load = pltpu.make_async_copy(tab, mates, tab_sem.at[1])
    partner_load.start()
    rows = TILE // 4
    mask_loads = [
        pltpu.make_async_copy(hbm[0].at[pl.ds(rows * c, rows)], mask.at[pl.ds(rows * c, rows)], mask_sem.at[c])
        for c in range(4)
    ]
    for load in mask_loads:
        load.start()

    @pl.loop(1, n)
    def _(k):
        pl.semaphore_signal(barrier, inc=1, device_id={"tile": peer_of(k)}, device_id_type=pl.DeviceIdType.MESH)

    for k in range(1, slabs):
        pl.semaphore_signal(
            barrier, inc=1, device_id={"slab": lax.rem(slab + k, slabs)}, device_id_type=pl.DeviceIdType.MESH
        )

    partner_load.wait()
    build_tables(n, cap, mates, ix_v, meta_out)
    index_load = pltpu.make_async_copy(ix_v, ix, tab_sem.at[0])
    index_load.start()

    for c in range(4):
        mask_loads[c].wait()
        to_tiles(mask, 2 * c, 2 * c + 2)

    in_cells[pl.ds(me * direct, direct)] = jnp.zeros((direct, 32, 128), jnp.float32)
    index_load.wait()

    @pl.loop(0, EXTRA, unroll=4)
    def _(o):
        x = tiles[ix[3, CELLS + o]]
        for q in range(RELAYS):
            out_ov[q, o] = x[8 * q : 8 * q + 8]

    pl.semaphore_wait(barrier, n + slabs - 2)

    def to_relay(q, source):
        where = {"device_id": {"tile": first + 2 * q}, "device_id_type": pl.DeviceIdType.MESH}
        return (
            pltpu.make_async_remote_copy(
                src_ref=meta_out, dst_ref=meta_in.at[source],
                send_sem=meta_send.at[q], recv_sem=meta_recv.at[source], **where,
            ),
            pltpu.make_async_remote_copy(
                src_ref=out_ov.at[q], dst_ref=in_ov.at[pl.ds(source * EXTRA, EXTRA)],
                send_sem=ov_send.at[q], recv_sem=ov_recv.at[source], **where,
            ),
        )

    for q in range(RELAYS):
        @pl.when(me != first + 2 * q)
        def _():
            for copy in to_relay(q, me):
                copy.start()
    loads = [pltpu.make_async_copy(hbm[i], vm[i], load_sem.at[i]) for i in range(1, len(hbm))]
    for load in loads:
        load.start()


    def cell_copy(k):
        to = peer_of(k)
        return pltpu.make_async_remote_copy(
            src_ref=out_cells.at[to], dst_ref=in_cells.at[pl.ds(me * direct, direct)],
            send_sem=cell_send.at[k], recv_sem=cell_recv.at[k],
            device_id={"tile": to}, device_id_type=pl.DeviceIdType.MESH,
        )

    cuts = [(n - 1) * c // 15 for c in (0,) + CUTS + (15,)]

    def offset_of(j):
        return jnp.where(lax.rem(j, 2) == 0, n - 1 - j // 2, n // 2 - 1 - j // 2)

    def pack(k):
        to = peer_of(k)
        for r in range(direct):
            out_cells[to, r] = tiles[ix[0, to * cap + r]]

    def start_cells(stage):
        @pl.loop(cuts[stage], cuts[stage + 1])
        def _(j):
            cell_copy(offset_of(j)).start()

    @pl.loop(cuts[0], cuts[1])
    def _(j):
        pack(offset_of(j))
        cell_copy(offset_of(j)).start()

    @pl.loop(cuts[1], n - 1)
    def _(j):
        pack(offset_of(j))

    for load in loads:
        load.wait()

    zero = jnp.zeros((32, 128), jnp.float32)
    lane_sign = jnp.where(lane % 64 < 32, -1.0, 1.0)

    @pl.loop(0, SIDE)
    def _(a):
        c, s = ph_x[0, a], ph_x[1, a]
        for b in range(SIDE):
            cb, sb = ph_y[0, b : b + 1, :], ph_y[1, b : b + 1, :]
            pc[a * 8 + b] = c * cb - s * sb
            ps[a * 8 + b] = (s * cb + c * sb) * lane_sign

    pc[CELLS] = zero
    ps[CELLS] = zero

    lxt_pair = lxt[0], lxt[1]
    for g in range(2):
        vv[g] = dot3(lxt_pair, halves(mask[256 * g : 256 * g + 256, :]))
    for g in range(2):
        for c in range(2):
            cols = slice(256 * c, 256 * c + 256)
            left = jnp.concatenate([vv[g, 0:256, cols], vv[g, 256:512, cols]], axis=1)
            plane[256 * g : 256 * g + 256, cols] = dot3(halves(left), (by[0], by[1]), ((1,), (1,)))
    to_tiles(plane)

    top[n] = zero
    bot[0] = zero

    @pl.loop(0, n, unroll=4)
    def _(t):
        sums = [zero] * 6
        for r in range(cap):
            s = t * cap + r
            x = tiles[ix[0, s]]
            p = ix[1, s]
            u, w = x * pc[p], x * ps[p]
            wt = jnp.where(p < 8, 1.0, 0.0)
            wb = jnp.where(p >= 56, 1.0, 0.0)
            sums = [
                sums[0] + u, sums[1] + w, sums[2] + wt * u, sums[3] + wt * w,
                sums[4] + wb * u, sums[5] + wb * w,
            ]
        wide[t] = sums[0] + swap(sums[1])
        top[t] = sums[2] + swap(sums[3])
        bot[t + 1] = sums[4] + swap(sums[5])

    def own_row(a, carry):
        u, w = carry
        for b in range(8):
            x = tiles[a * 8 + b]
            u, w = u + x * pc[a * 8 + b], w + x * ps[a * 8 + b]
        return u, w

    u0, w0 = own_row(0, (zero, zero))
    u7, w7 = own_row(7, (zero, zero))
    u, w = lax.fori_loop(1, 7, own_row, (u0 + u7, w0 + w7))
    wide[me] += u + swap(w)
    top[me] += u0 + swap(w0)
    bot[me + 1] += u7 + swap(w7)

    @pl.loop(0, n, unroll=8)
    def _(t):
        tp = jnp.where(low, top[t + 1], 0.0)
        bt = jnp.where(low, 0.0, bot[t])
        tp = tp + pltpu.roll(tp, 64, 1)
        bt = bt + pltpu.roll(bt, 64, 1)
        x = wide[t]
        x = x + pltpu.roll(x, 64, 1)
        both = (tp + bt) * sh[0] + pltpu.roll((bt - tp), 32, 1) * sh[1]
        part[place(t)] = compact(x + both)

    def spec_copy(k):
        to = jnp.bitwise_xor(chip, k)
        return pltpu.make_async_remote_copy(
            src_ref=part.at[place(2 * to + core)], dst_ref=spec_in.at[chip],
            send_sem=spec_send.at[k], recv_sem=spec_recv.at[k],
            device_id={"tile": 2 * to + core}, device_id_type=pl.DeviceIdType.MESH,
        )

    other = pl.ds((1 - core) * chips, chips)
    share = pltpu.make_async_remote_copy(
        src_ref=part.at[other], dst_ref=shared, send_sem=spec_send.at[0], recv_sem=spec_recv.at[0],
        device_id={"tile": jnp.bitwise_xor(me, 1)}, device_id_type=pl.DeviceIdType.MESH,
    )
    share.start()
    share.wait_recv()
    own_part = pl.ds(core * chips, chips)
    part[own_part] = part[own_part] + shared[...]

    @pl.loop(1, chips)
    def _(k):
        spec_copy(k).start()

    start_cells(1)

    def flag_copy(k):
        to = lax.rem(slab + k, slabs)
        return pltpu.make_async_remote_copy(
            src_ref=flag_mine, dst_ref=flag_in.at[k],
            send_sem=flag_send.at[k], recv_sem=flag_recv.at[k],
            device_id={"slab": to}, device_id_type=pl.DeviceIdType.MESH,
        )

    def hop_copy(k, source):
        to = peer_of(k)
        return pltpu.make_async_remote_copy(
            src_ref=out2.at[to], dst_ref=in2.at[source],
            send_sem=hop_send.at[k], recv_sem=hop_recv.at[source],
            device_id={"tile": to}, device_id_type=pl.DeviceIdType.MESH,
        )

    spec_in[chip] = part[place(me)]

    for k in range(KERNELS):
        rows = slice(32 * k, 32 * k + 32)
        re, im = kraw[64 * k : 64 * k + 32, :], kraw[64 * k + 32 : 64 * k + 64, :]
        kr[rows, :] = jnp.concatenate([re] * 4, axis=1)
        ki[rows, :] = jnp.concatenate([-im, im] * 2, axis=1)

    @pl.loop(1, chips)
    def _(k):
        spec_copy(k).wait_recv()

    start_cells(2)
    spec = expand(sum((spec_in[t] for t in range(1, chips)), spec_in[0]))

    spec_s = pltpu.roll(spec, 32, 1)
    for k in range(KERNELS):
        rows = slice(32 * k, 32 * k + 32)
        stack[rows, :] = spec * kr[rows, :] + spec_s * ki[rows, :]
    fields_y = dot(stack[...], yt[...])
    sign = jnp.where(low, -1.0, 1.0)
    for k in range(KERNELS):
        part_k = fields_y[32 * k : 32 * k + 32]
        rhs[0:32, 128 * k : 128 * k + 128] = part_k
        rhs[32:64, 128 * k : 128 * k + 128] = pltpu.roll(part_k, 64, 1) * sign
    fields = dot(x1[...], rhs[...])
    inten = jnp.zeros((64, 128), jnp.float32)
    for k in range(KERNELS):
        e = fields[:, 128 * k : 128 * k + 128]
        inten = inten + wts[k] * (e * e)
    blurred = dot(ux[...], dot(inten, uyt[...]))
    d = dose[0]
    resist = jax.nn.sigmoid(4.0 * (d * blurred - 1.0))
    slope = 2.0 * (resist - target[...]) * (4.0 * d) * resist * (1.0 - resist)
    grad_i = dot3((uxt[0], uxt[1]), halves(dot3(halves(slope), (uy2[0], uy2[1]))))
    lane2 = lax.broadcasted_iota(jnp.int32, (64, 128), 1)
    sign2 = jnp.where(lane2 < 64, 1.0, -1.0)
    for k in range(KERNELS):
        ge = (2.0 * wts[k]) * grad_i * fields[:, 128 * k : 128 * k + 128]
        rhs2[0:64, 128 * k : 128 * k + 128] = ge
        rhs2[64:128, 128 * k : 128 * k + 128] = pltpu.roll(ge, 64, 1) * sign2
    grad_y = dot(x2[...], rhs2[...])
    for k in range(KERNELS):
        stack[32 * k : 32 * k + 32, :] = grad_y[:, 128 * k : 128 * k + 128]
    grad_a = dot(stack[...], y2[...])
    acc = zero
    for k in range(KERNELS):
        rows = slice(32 * k, 32 * k + 32)
        ga = grad_a[rows]
        acc = acc + kr[rows, :] * ga - ki[rows, :] * pltpu.roll(ga, 32, 1)
    acc_all[place(me)] = compact(acc)

    def acc_copy(k):
        to = jnp.bitwise_xor(low_chip, k)
        return pltpu.make_async_remote_copy(
            src_ref=acc_all.at[pl.ds(mine, 2)], dst_ref=acc_all.at[pl.ds(mine, 2)],
            send_sem=acc_send.at[k], recv_sem=acc_recv.at[k],
            device_id={"tile": 2 * (to + half * high_chip) + core}, device_id_type=pl.DeviceIdType.MESH,
        )

    acc_cross = pltpu.make_async_remote_copy(
        src_ref=acc_all.at[place(me)], dst_ref=acc_all.at[place(me)],
        send_sem=acc_send.at[half], recv_sem=acc_recv.at[half],
        device_id={"tile": across}, device_id_type=pl.DeviceIdType.MESH,
    )
    acc_cross.start()
    start_cells(3)
    acc_cross.wait_recv()

    @pl.loop(1, half)
    def _(k):
        acc_copy(k).start()

    start_cells(4)

    @pl.when(is_relay)
    def _():
        meta_in[me] = meta_out[...]
        in_ov[pl.ds(me * EXTRA, EXTRA)] = out_ov[relay]

        @pl.loop(1, n)
        def _(k):
            for copy in to_relay(0, peer_of(k)):
                copy.wait_recv()

        lines = n // 8
        slot = lax.broadcasted_iota(jnp.int32, (lines, 128), 1) % 16
        start = jnp.zeros((lines, 128), jnp.int32)
        found = jnp.zeros((lines, 128), jnp.int32)
        most = jnp.zeros((lines, 128), jnp.int32)
        for i in range(n):
            count, offset = meta_in[i, 0:lines], meta_in[i, lines : 2 * lines]
            rel = slot - start
            found = jnp.where((rel >= 0) & (rel < count), i * EXTRA + offset + rel, found)
            start = start + count
            most = jnp.maximum(most, count + offset)
        route_v[...] = jnp.zeros((8, 128), jnp.int32)
        route_v[0:lines] = jnp.clip(found, 0, n * EXTRA - 1)
        over = jnp.broadcast_to(jnp.max(jnp.where(most > EXTRA, 1.0, 0.0)), (8, 128))
        route_copy = pltpu.make_async_copy(route_v, route, tab_sem.at[2])
        route_copy.start()
        flag_mine[...] = over

        @pl.when(me == first)
        def _():
            for k in range(1, slabs):
                flag_copy(k).start()

        route_copy.wait()

        @pl.loop(0, n)
        def _(d):
            for m in range(EXTRA):
                out2[d, m] = in_ov[route[d // 8, lax.rem(d, 8) * 16 + m]]

        flag_in[0] = over

        @pl.when(me == first)
        def _():
            for k in range(1, slabs):
                flag_copy(k).wait()
                flag_in[0] = jnp.maximum(flag_in[0], flag_in[k])

        @pl.loop(0, n)
        def _(d):
            out2[d, EXTRA] = flag_in[0]

        @pl.loop(1, n)
        def _(k):
            hop_copy(k, relay).start()

        in2[relay] = out2[me]

    @pl.loop(1, half)
    def _(k):
        acc_copy(k).wait_recv()

    give = pltpu.make_async_remote_copy(
        src_ref=acc_all.at[own_part], dst_ref=acc_all.at[own_part],
        send_sem=acc_send.at[0], recv_sem=acc_recv.at[0],
        device_id={"tile": jnp.bitwise_xor(me, 1)}, device_id_type=pl.DeviceIdType.MESH,
    )
    give.start()
    give.wait_recv()


    @pl.loop(0, n, unroll=8)
    def _(t):
        mid = expand(acc_all[place(t)])
        before = expand(acc_all[place(jnp.maximum(t - 1, 0))]) * jnp.where(t > 0, 1.0, 0.0)
        after = expand(acc_all[place(jnp.minimum(t + 1, n - 1))]) * jnp.where(t < n - 1, 1.0, 0.0)
        first = mid + before * sh[0] + pltpu.roll(before, 32, 1) * sh[1]
        last = mid + after * sh[0] - pltpu.roll(after, 32, 1) * sh[1]
        mid_s, first_s, last_s = (pltpu.roll(v, 32, 1) for v in (mid, first, last))
        acc2[t * 3] = jnp.where(low, first, mid)
        acc2[t * 3 + 1] = mid
        acc2[t * 3 + 2] = jnp.where(low, mid, last)
        acc2s[t * 3] = jnp.where(low, first_s, mid_s)
        acc2s[t * 3 + 1] = mid_s
        acc2s[t * 3 + 2] = jnp.where(low, mid_s, last_s)

    @pl.loop(0, SIDE, unroll=2)
    def _(a):
        r = pl.multiple_of(a * 64, 64)
        own = me * 3 + jnp.where(a == 0, 0, jnp.where(a == SIDE - 1, 2, 1))
        own_x, own_s = acc2[own], acc2s[own]
        for b in range(4):
            pieces = []
            for i in range(2):
                c = a * 8 + 2 * b + i
                g, p = ix[2, CELLS + c], ix[3, c]
                pieces.append(own_x * pc[c] + own_s * ps[c] + acc2[g] * pc[p] + acc2s[g] * ps[p])
            h0, h1 = pair(*pieces)
            plane[pl.ds(r, 32), 128 * b : 128 * b + 128] = h0
            plane[pl.ds(r + 32, 32), 128 * b : 128 * b + 128] = h1

    for c in range(2):
        for g in range(2):
            v = dot3(halves(plane[256 * g : 256 * g + 256, 256 * c : 256 * c + 256]), (by[0], by[1]))
            vv[g, 0:256, 256 * c : 256 * c + 256] = v[:, 0:256]
            vv[g, 256:512, 256 * c : 256 * c + 256] = v[:, 256:512]
    for g in range(2):
        grad_out[256 * g : 256 * g + 256, :] = dot3((lx[0], lx[1]), halves(vv[g]))

    @pl.loop(0, SIDE)
    def _(a):
        r = pl.multiple_of(a * 64, 64)
        for b in range(4):
            for h in range(2):
                where = (pl.ds(r + 32 * h, 32), slice(128 * b, 128 * b + 128))
                upd_out[where] = 0.5 * mask[where] - 0.1 * grad_out[where]

    @pl.loop(1, n)
    def _(k):
        cell_copy(k).wait_send()

    @pl.loop(1, chips)
    def _(k):
        spec_copy(k).wait_send()

    @pl.loop(1, half)
    def _(k):
        acc_copy(k).wait_send()

    acc_cross.wait_send()

    share.wait_send()
    give.wait_send()

    for q in range(RELAYS):
        @pl.when(me != first + 2 * q)
        def _():
            for copy in to_relay(q, me):
                copy.wait_send()

    @pl.when(is_relay)
    def _():
        @pl.loop(1, n)
        def _(k):
            hop_copy(k, relay).wait_send()

    @pl.loop(1, n)
    def _(k):
        cell_copy(k).wait_recv()

    for q in range(RELAYS):
        @pl.when(me != first + 2 * q)
        def _():
            hop_copy(1, q).wait_recv()

    flag_out[0] = in2[0, EXTRA][0, 0]
    for m in range(EXTRA):
        in_cells[n * direct + m] = jnp.concatenate([in2[q, m] for q in range(RELAYS)], axis=0)

    @pl.loop(0, SIDE, unroll=2)
    def _(a):
        r = pl.multiple_of(a * 64, 64)
        for b in range(4):
            c = a * 8 + 2 * b
            both = pair(in_cells[ix[2, c]],
                          in_cells[ix[2, c + 1]])
            for h in range(2):
                where = (pl.ds(r + 32 * h, 32), slice(128 * b, 128 * b + 128))
                upd_out[where] = upd_out[where] + 0.5 * both[h]


def full_body(n, cap, tab, mask_hbm, both_out, mask, ix, tiles, out_cells, in_cells, tab_sem, cell_send, cell_recv):
    me = lax.axis_index("tile")
    low = lax.broadcasted_iota(jnp.int32, (32, 128), 1) < 64

    def pair(x, y):
        rx, ry = pltpu.roll(x, 64, 1), pltpu.roll(y, 64, 1)
        return jnp.where(low, x, ry), jnp.where(low, rx, y)

    barrier = pltpu.get_barrier_semaphore()

    @pl.loop(1, n)
    def _(k):
        pl.semaphore_signal(
            barrier, inc=1, device_id={"tile": jnp.bitwise_xor(me, k)}, device_id_type=pl.DeviceIdType.MESH
        )

    index_load = pltpu.make_async_copy(tab.at[pl.ds(0, 8)], ix, tab_sem.at[0])
    index_load.start()
    mask_load = pltpu.make_async_copy(mask_hbm, mask, tab_sem.at[1])
    mask_load.start()
    mask_load.wait()

    @pl.loop(0, SIDE)
    def _(a):
        r = pl.multiple_of(a * 64, 64)
        for b in range(4):
            h0 = mask[pl.ds(r, 32), 128 * b : 128 * b + 128]
            h1 = mask[pl.ds(r + 32, 32), 128 * b : 128 * b + 128]
            tiles[a * 8 + 2 * b], tiles[a * 8 + 2 * b + 1] = pair(h0, h1)

    index_load.wait()

    @pl.loop(0, n)
    def _(to):
        for r in range(cap):
            out_cells[to, r] = tiles[ix[0, to * cap + r]]

    in_cells[pl.ds(me * cap, cap)] = out_cells[me]
    pl.semaphore_wait(barrier, n - 1)

    def cell_copy(k):
        to = jnp.bitwise_xor(me, k)
        return pltpu.make_async_remote_copy(
            src_ref=out_cells.at[to], dst_ref=in_cells.at[pl.ds(me * cap, cap)],
            send_sem=cell_send.at[k], recv_sem=cell_recv.at[k],
            device_id={"tile": to}, device_id_type=pl.DeviceIdType.MESH,
        )

    @pl.loop(1, n)
    def _(k):
        cell_copy(k).start()

    @pl.loop(1, n)
    def _(k):
        cell_copy(k).wait()

    @pl.loop(0, SIDE)
    def _(a):
        r = pl.multiple_of(a * 64, 64)
        for b in range(4):
            c = a * 8 + 2 * b
            halves_of = pair(in_cells[ix[1, c]], in_cells[ix[1, c + 1]])
            for h in range(2):
                where = (pl.ds(r + 32 * h, 32), slice(128 * b, 128 * b + 128))
                both_out[where] = mask[where] + halves_of[h]


def full_exchange(n, cap, partner, mask):
    owner = partner // CELLS
    pos = partner % CELLS
    ids = jnp.arange(CELLS, dtype=jnp.int32)
    same = owner[:, None] == owner[None, :]
    send_rank = jnp.sum((same & (pos[None, :] < pos[:, None])).astype(jnp.int32), axis=1)
    recv_rank = jnp.sum((same & (ids[None, :] < ids[:, None])).astype(jnp.int32), axis=1)
    send_slot = owner * cap + send_rank
    recv_slot = owner * cap + recv_rank
    hit = (jnp.arange(n * cap, dtype=jnp.int32)[:, None] == send_slot[None, :]).astype(jnp.int32)
    slot_cell = jnp.sum(hit * ids[None, :], axis=1)
    tab = jnp.concatenate([slot_cell, recv_slot, recv_slot, jnp.zeros((6 * 128,), jnp.int32)]).reshape(8, 128)
    f32 = jnp.float32
    dma = pltpu.SemaphoreType.DMA((n,))
    vmem = pl.BlockSpec(memory_space=pltpu.VMEM)
    return pl.pallas_call(
        functools.partial(full_body, n, cap),
        out_shape=jax.ShapeDtypeStruct((TILE, TILE), f32),
        in_specs=[pl.BlockSpec(memory_space=pl.ANY), pl.BlockSpec(memory_space=pltpu.HBM)],
        out_specs=vmem,
        scratch_shapes=[
            pltpu.VMEM((TILE, TILE), f32),
            pltpu.SMEM((8, 128), jnp.int32),
            pltpu.VMEM((CELLS, 32, 128), f32),
            pltpu.VMEM((n, cap, 32, 128), f32),
            pltpu.VMEM((n * cap, 32, 128), f32),
            pltpu.SemaphoreType.DMA((2,)),
            dma, dma,
        ],
        compiler_params=pltpu.CompilerParams(
            collective_id=1, has_side_effects=True, vmem_limit_bytes=32 * 1024 * 1024
        ),
    )(tab, mask)


def local(consts, mask, target, partner, kernels, socs_weights, dose):
    n = lax.axis_size("tile")
    cap, direct = 2 * CELLS // n, CELLS // n
    meta_lines = (2 * n // 8 + 7) // 8 * 8
    raw = kernels.reshape(2 * KERNELS * BAND, BAND)
    f32 = jnp.float32
    vmem = pl.BlockSpec(memory_space=pltpu.VMEM)
    hbm = pl.BlockSpec(memory_space=pltpu.HBM)
    arrays = [mask, target, raw, *consts]
    smem = pl.BlockSpec(memory_space=pltpu.SMEM)
    dma, few = pltpu.SemaphoreType.DMA((n,)), pltpu.SemaphoreType.DMA((RELAYS,))
    flags = pltpu.SemaphoreType.DMA((lax.axis_size("slab"),))
    twice, both, flag = pl.pallas_call(
        functools.partial(body, n, cap, len(arrays)),
        out_shape=(jax.ShapeDtypeStruct((TILE, TILE), f32),) * 2 + (jax.ShapeDtypeStruct((1,), f32),),
        in_specs=[smem] * 2 + [hbm] + [hbm] * len(arrays),
        out_specs=(vmem, vmem, smem),
        scratch_shapes=[pltpu.VMEM(x.shape, x.dtype) for x in arrays] + [
            pltpu.SemaphoreType.DMA((len(arrays),)),
            pltpu.VMEM((CELLS + 1, 32, 128), f32),
            pltpu.VMEM((CELLS + 1, 32, 128), f32),
            pltpu.VMEM((n, direct, 32, 128), f32),
            pltpu.VMEM((n * direct + EXTRA, 32, 128), f32),
            pltpu.VMEM((CELLS, 32, 128), f32),
            pltpu.VMEM((TILE, TILE), f32),
            pltpu.VMEM((2, 512, 512), f32),
            pltpu.VMEM((n, 32, 128), f32),
            pltpu.VMEM((n, 16, 128), f32),
            pltpu.VMEM((n // 2, 16, 128), f32),
            pltpu.VMEM((n + 1, 32, 128), f32),
            pltpu.VMEM((n + 1, 32, 128), f32),
            pltpu.VMEM((n, 16, 128), f32),
            pltpu.VMEM((n, 16, 128), f32),
            pltpu.VMEM((3 * n, 32, 128), f32),
            pltpu.VMEM((3 * n, 32, 128), f32),
            pltpu.VMEM((64, 768), f32),
            pltpu.VMEM((128, 768), f32),
            pltpu.VMEM((192, 128), f32),
            pltpu.VMEM((192, 128), f32),
            pltpu.VMEM((192, 128), f32),
            pltpu.VMEM((1, CELLS), jnp.int32),
            pltpu.VMEM((8, 128), jnp.int32),
            pltpu.SMEM((8, 128), jnp.int32),
            pltpu.SemaphoreType.DMA((3,)),
            pltpu.SemaphoreType.DMA((4,)),
            pltpu.VMEM((RELAYS, EXTRA, 8, 128), f32),
            pltpu.VMEM((n * EXTRA, 8, 128), f32),
            pltpu.VMEM((n, EXTRA + 1, 8, 128), f32),
            pltpu.VMEM((RELAYS, EXTRA + 1, 8, 128), f32),
            pltpu.VMEM((meta_lines, 128), jnp.int32),
            pltpu.VMEM((n, meta_lines, 128), jnp.int32),
            pltpu.VMEM((8, 128), jnp.int32),
            pltpu.SMEM((8, 128), jnp.int32),
            pltpu.VMEM((8, 128), f32),
            pltpu.VMEM((lax.axis_size("slab"), 8, 128), f32),
            few, dma, few, dma, dma, few, flags, flags,
            dma, dma, dma, dma, dma, dma,
        ],
        compiler_params=pltpu.CompilerParams(
            collective_id=0, has_side_effects=True, vmem_limit_bytes=VMEM_LIMIT
        ),
    )(socs_weights, dose, partner.reshape(1, CELLS), *arrays)
    def finish(p, m, g, u):
        return write_out(g, u)

    def redo(p, m, g, u):
        return write_out(g, 0.5 * full_exchange(n, cap, p, m) - 0.1 * g)

    return lax.cond(flag[0] > 0.5, redo, finish, partner, mask, twice, both)


def write_body(parts, g, u, g_out, u_out, sem):
    rows = TILE // parts
    copies = []
    for c in range(parts):
        where = pl.ds(rows * c, rows)
        for i, (src, dst) in enumerate(((g, g_out), (u, u_out))):
            copies.append(pltpu.make_async_copy(src.at[where], dst.at[where], sem.at[i, c]))
    for copy in copies:
        copy.start()
    for copy in copies:
        copy.wait()


def write_out(g, u):
    parts = 4
    vmem = pl.BlockSpec(memory_space=pltpu.VMEM)
    hbm = pl.BlockSpec(memory_space=pltpu.HBM)
    return tuple(pl.pallas_call(
        functools.partial(write_body, parts),
        out_shape=(jax.ShapeDtypeStruct((TILE, TILE), jnp.float32),) * 2,
        in_specs=[vmem, vmem],
        out_specs=(hbm, hbm),
        scratch_shapes=[pltpu.SemaphoreType.DMA((2, parts))],
        compiler_params=pltpu.CompilerParams(vmem_limit_bytes=4 * 1024 * 1024),
    )(g, u))


def solution(mesh):
    consts = tables()

    def run(mask, target, partner, kernels, socs_weights, dose):
        return local([jnp.asarray(t) for t in consts], mask, target, partner, kernels, socs_weights, dose)

    return jax.shard_map(
        run,
        mesh=mesh,
        in_specs=(
            P(("slab", "tile"), None),
            P(("slab", "tile"), None),
            P(("slab", "tile")),
            P(),
            P(),
            P(),
        ),
        out_specs=(P(("slab", "tile"), None), P(("slab", "tile"), None)),
        check_vma=False,
    )
```

```python
import functools
import math

import numpy as np
import jax
import jax.numpy as jnp
from jax import lax
from jax.experimental import pallas as pl
from jax.experimental.pallas import tpu as pltpu
from jax.sharding import PartitionSpec as P

TILE = 512
CELL = 64
MARGIN = 32
BAND = 32
CELLS = 64
SIDE = 8
DOMAIN = 576
GRID = 64
KERNELS = 6
CUTS = (3, 8, 10, 11)
EXTRA = 12
RELAYS = 4
VMEM_LIMIT = 56 * 1024 * 1024
HIGHEST = lax.Precision.HIGHEST
BLUR = (0.0625, 0.25, 0.375, 0.25, 0.0625)


def tables():
    f = np.arange(BAND) - BAND // 2
    norm = 0.5 / math.sqrt(DOMAIN * TILE)
    ph_x = np.zeros((2, SIDE, BAND, 128))
    for h in range(2):
        ang = 2 * np.pi * np.outer(1 + 2 * np.arange(SIDE) + h, f) / 18.0
        ph_x[0, :, :, 64 * h : 64 * h + 64] = norm * np.cos(ang)[:, :, None]
        ph_x[1, :, :, 64 * h : 64 * h + 64] = norm * np.sin(ang)[:, :, None]
    ang = 2 * np.pi * np.outer(np.arange(SIDE), f) / 8.0
    ph_y = np.stack([np.tile(np.cos(ang), (1, 4)), np.tile(np.sin(ang), (1, 4))])
    ang = 2 * np.pi * f * 16 / 18.0
    one = np.ones((1, 32))
    cos16, sin16 = np.cos(ang)[:, None] * one, np.sin(ang)[:, None] * one
    sh = np.stack(
        [np.concatenate([cos16] * 4, 1), np.concatenate([-sin16, sin16] * 2, 1)]
    )
    q = np.arange(CELL)
    cy = np.cos(2 * np.pi * np.outer(f, q) / TILE)
    sy = np.sin(2 * np.pi * np.outer(f, q) / TILE)
    by = np.zeros((256, 512))
    for i in range(4):
        r, o = 64 * i, 64 * i
        by[r : r + 32, o : o + 64] = cy
        by[r : r + 32, 256 + o : 256 + o + 64] = sy
        by[r + 32 : r + 64, o : o + 64] = -sy
        by[r + 32 : r + 64, 256 + o : 256 + o + 64] = cy
    r32 = np.arange(32)
    cx = np.cos(2 * np.pi * np.outer(r32, f) / DOMAIN)
    sx = np.sin(2 * np.pi * np.outer(r32, f) / DOMAIN)
    lx = np.zeros((256, 512))
    for j in range(8):
        k = 32 * j
        lx[k : k + 32, k : k + 32] = cx
        lx[k : k + 32, 256 + k : 256 + k + 32] = -sx
    m = np.arange(GRID)
    c = np.cos(2 * np.pi * np.outer(f, m) / GRID)
    s = np.sin(2 * np.pi * np.outer(f, m) / GRID)
    yt = np.zeros((128, 128))
    yt[:32, :64], yt[:32, 64:], yt[32:64, :64], yt[32:64, 64:] = c, s, -s, c
    x1 = np.concatenate([c.T, s.T], 1) / BAND
    x2 = np.concatenate([c, s], 1) / BAND
    y2 = np.zeros((128, 128))
    half = np.concatenate([np.concatenate([c.T, -s.T], 1), np.concatenate([s.T, c.T], 1)], 0)
    y2[:, :64], y2[:, 64:] = half, half
    g = np.arange(-31, 32)

    def interp(extent):
        d = np.arange(extent)[:, None] / extent - m[None, :] / GRID
        return np.cos(2 * np.pi * g[:, None, None] * d[None]).sum(0) / GRID

    ux = interp(DOMAIN)
    ux = sum(BLUR[i] * ux[MARGIN - 2 + i : MARGIN - 2 + i + TILE] for i in range(5))
    uy = interp(TILE)
    uy = sum(BLUR[i] * np.roll(uy, i - 2, axis=0) for i in range(5))
    uyt = np.concatenate([uy.T, uy.T], 0)
    uy2 = np.concatenate([uy, uy], 1)
    whole = [ph_x, ph_y, sh, yt, x1, x2, y2, ux, uyt]
    return [np.ascontiguousarray(t, dtype=np.float32) for t in whole] + [
        split(np.ascontiguousarray(t, dtype=np.float32)) for t in (by, lx, lx.T, ux.T, uy2)
    ]


def split(t):
    hi = t.astype(jnp.bfloat16)
    return np.stack([hi, (t - hi.astype(np.float32)).astype(jnp.bfloat16)])


def dot(x, y):
    return jnp.dot(x, y, precision=HIGHEST, preferred_element_type=jnp.float32)


def halves(x):
    hi = x.astype(jnp.bfloat16)
    return hi, (x - hi.astype(jnp.float32)).astype(jnp.bfloat16)


def dot3(x, y, dims=((1,), (0,))):
    def one(p, q):
        return lax.dot_general(p, q, (dims, ((), ())), preferred_element_type=jnp.float32)

    return one(x[0], y[0]) + (one(x[0], y[1]) + one(x[1], y[0]))


def build_tables(n, cap, mates, index_out, meta_out):
    direct, lines = cap // 2, n // 8
    row = jnp.concatenate([mates[...], mates[...]], axis=1)
    square = jnp.broadcast_to(row, (128, 128))
    across, down = square[0:CELLS], square.T[0:CELLS]
    lane = lax.broadcasted_iota(jnp.int32, (CELLS, 128), 1)
    cell = lax.broadcasted_iota(jnp.int32, (CELLS, 128), 0)
    own_r, pos_r, own_c, pos_c = across >> 6, across & 63, down >> 6, down & 63
    valid = lane < CELLS

    def over_cells(mask):
        return jnp.sum(jnp.where(mask, 1, 0), axis=0, keepdims=True)

    def over_lanes(mask):
        return jnp.sum(jnp.where(mask & valid, 1, 0), axis=1, keepdims=True)

    same = own_r == own_c
    rank_r = over_cells(same & (pos_c < pos_r))
    recv_r = over_cells(same & (cell < lane))
    rank_c = over_lanes(same & (pos_r < pos_c))
    spare_c = jnp.broadcast_to(rank_c, (CELLS, 128)) >= direct
    spare_r = jnp.broadcast_to(rank_r, (CELLS, 128)) >= direct
    ahead_r = over_cells(spare_c & (own_c < own_r))
    ahead_c = over_lanes(spare_r & (own_r < own_c))
    hit = own_c * cap + rank_c == lane
    own, pos, first = own_r[0:1], pos_r[0:1], lane[0:1] < CELLS
    kind = jnp.where(pos < SIDE, 0, jnp.where(pos >= CELLS - SIDE, 2, 1))
    recv = jnp.where(
        recv_r < direct, own * direct + recv_r,
        n * direct + jnp.minimum(ahead_r + recv_r - direct, EXTRA - 1),
    )
    index_out[0:1] = jnp.max(jnp.where(hit, cell, 0), axis=0, keepdims=True)
    index_out[1:2] = jnp.min(jnp.where(hit, pos_c, CELLS), axis=0, keepdims=True)
    index_out[2:3] = jnp.where(first, recv, own * 3 + kind)
    index_out[3:4] = jnp.where(
        first, pos,
        jnp.max(jnp.where(spare_c & (ahead_c + rank_c - direct == lane - CELLS), cell, 0), axis=0, keepdims=True),
    )
    index_out[4:8] = jnp.zeros((4, 128), jnp.int32)
    meta_out[...] = jnp.zeros(meta_out.shape, jnp.int32)
    for h in range(lines):
        dest = (lane + 128 * h) >> 4
        meta_out[h : h + 1] = over_cells(spare_c & (own_c == dest))
        meta_out[lines + h : lines + h + 1] = over_cells(spare_c & (own_c < dest))


def body(n, cap, n_in, wts, dose, tab, *refs):
    hbm, outs = refs[:n_in], refs[n_in : n_in + 3]
    vm = refs[n_in + 3 : 2 * n_in + 3]
    load_sem = refs[2 * n_in + 3]
    (
        mask, target, kraw, ph_x, ph_y, sh, yt, x1, x2, y2, ux, uyt, by, lx, lxt, uxt, uy2
    ) = vm
    main(n, cap, tab, wts, dose, hbm, vm, load_sem,
         mask, target, kraw, ph_x, ph_y, sh, yt, x1, x2, y2, ux, uyt, by, lx, lxt, uxt, uy2,
         *outs, *refs[2 * n_in + 4 :])


def main(
    n, cap, tab, wts, dose, hbm, vm, load_sem,
    mask, target, kraw, ph_x, ph_y, sh, yt, x1, x2, y2, ux, uyt, by, lx, lxt, uxt, uy2,
    grad_out, upd_out, flag_out, pc, ps,
    out_cells, in_cells, tiles, plane, vv, wide, part, shared, top, bot, spec_in, acc_all, acc2, acc2s, rhs, rhs2, stack,
    kr, ki, mates, ix_v, ix, tab_sem, mask_sem, out_ov, in_ov, out2, in2, meta_out, meta_in, route_v, route, flag_mine, flag_in,
    ov_send, ov_recv, meta_send, meta_recv, hop_send, hop_recv, flag_send, flag_recv,
    cell_send, cell_recv, spec_send, spec_recv, acc_send, acc_recv,
):
    me = lax.axis_index("tile")
    lane = lax.broadcasted_iota(jnp.int32, (32, 128), 1)
    low = lane < 64
    slabs = lax.axis_size("slab")
    slab = lax.axis_index("slab")
    direct = cap // 2
    first = n // 4
    relay = (me - first) // 2
    is_relay = (me >= first) & (me < first + 2 * RELAYS) & (lax.rem(me, 2) == 0)

    def swap(x):
        return jnp.where(lane % 64 < 32, pltpu.roll(x, 96, 1), pltpu.roll(x, 32, 1))

    def pair(x, y):
        rx, ry = pltpu.roll(x, 64, 1), pltpu.roll(y, 64, 1)
        return jnp.where(low, x, ry), jnp.where(low, rx, y)

    def to_tiles(src, start=0, stop=SIDE):
        @pl.loop(start, stop, unroll=2)
        def _(a):
            r = pl.multiple_of(a * 64, 64)
            for b in range(4):
                h0 = src[pl.ds(r, 32), 128 * b : 128 * b + 128]
                h1 = src[pl.ds(r + 32, 32), 128 * b : 128 * b + 128]
                x, y = pair(h0, h1)
                tiles[a * 8 + 2 * b] = x
                tiles[a * 8 + 2 * b + 1] = y

    def compact(x):
        return jnp.where(low[0:16], x[0:16], x[16:32])

    def expand(x):
        r = pltpu.roll(x, 64, 1)
        return jnp.concatenate([jnp.where(low[0:16], x, r), jnp.where(low[0:16], r, x)], axis=0)

    chips = n // 2
    core = lax.rem(me, 2)
    chip = me // 2
    half = chips // 2
    low_chip, high_chip = lax.rem(chip, half), chip // half
    mine = core * chips + 2 * low_chip
    across = 2 * (low_chip + half * (1 - high_chip)) + core

    def place(t):
        return lax.rem(t, 2) * chips + 2 * lax.rem(t // 2, half) + t // 2 // half

    def peer_of(k):
        return jnp.bitwise_xor(me, k)

    barrier = pltpu.get_barrier_semaphore()

    partner_load = pltpu.make_async_copy(tab, mates, tab_sem.at[1])
    partner_load.start()
    rows = TILE // 4
    mask_loads = [
        pltpu.make_async_copy(hbm[0].at[pl.ds(rows * c, rows)], mask.at[pl.ds(rows * c, rows)], mask_sem.at[c])
        for c in range(4)
    ]
    for load in mask_loads:
        load.start()

    @pl.loop(1, n)
    def _(k):
        pl.semaphore_signal(barrier, inc=1, device_id={"tile": peer_of(k)}, device_id_type=pl.DeviceIdType.MESH)

    for k in range(1, slabs):
        pl.semaphore_signal(
            barrier, inc=1, device_id={"slab": lax.rem(slab + k, slabs)}, device_id_type=pl.DeviceIdType.MESH
        )

    partner_load.wait()
    build_tables(n, cap, mates, ix_v, meta_out)
    index_load = pltpu.make_async_copy(ix_v, ix, tab_sem.at[0])
    index_load.start()

    for c in range(4):
        mask_loads[c].wait()
        to_tiles(mask, 2 * c, 2 * c + 2)

    in_cells[pl.ds(me * direct, direct)] = jnp.zeros((direct, 32, 128), jnp.float32)
    index_load.wait()

    @pl.loop(0, EXTRA, unroll=4)
    def _(o):
        x = tiles[ix[3, CELLS + o]]
        for q in range(RELAYS):
            out_ov[q, o] = x[8 * q : 8 * q + 8]

    pl.semaphore_wait(barrier, n + slabs - 2)

    def to_relay(q, source):
        where = {"device_id": {"tile": first + 2 * q}, "device_id_type": pl.DeviceIdType.MESH}
        return (
            pltpu.make_async_remote_copy(
                src_ref=meta_out, dst_ref=meta_in.at[source],
                send_sem=meta_send.at[q], recv_sem=meta_recv.at[source], **where,
            ),
            pltpu.make_async_remote_copy(
                src_ref=out_ov.at[q], dst_ref=in_ov.at[pl.ds(source * EXTRA, EXTRA)],
                send_sem=ov_send.at[q], recv_sem=ov_recv.at[source], **where,
            ),
        )

    for q in range(RELAYS):
        @pl.when(me != first + 2 * q)
        def _():
            for copy in to_relay(q, me):
                copy.start()
    loads = [pltpu.make_async_copy(hbm[i], vm[i], load_sem.at[i]) for i in range(1, len(hbm))]
    for load in loads:
        load.start()


    def cell_copy(k):
        to = peer_of(k)
        return pltpu.make_async_remote_copy(
            src_ref=out_cells.at[to], dst_ref=in_cells.at[pl.ds(me * direct, direct)],
            send_sem=cell_send.at[k], recv_sem=cell_recv.at[k],
            device_id={"tile": to}, device_id_type=pl.DeviceIdType.MESH,
        )

    cuts = [(n - 1) * c // 15 for c in (0,) + CUTS + (15,)]

    def offset_of(j):
        return jnp.where(lax.rem(j, 2) == 0, n // 2 + j // 4 + lax.rem(j // 2, 2) * (n // 4), n // 2 - 1 - j // 2)

    def pack(k):
        to = peer_of(k)
        for r in range(direct):
            out_cells[to, r] = tiles[ix[0, to * cap + r]]

    def start_cells(stage):
        @pl.loop(cuts[stage], cuts[stage + 1])
        def _(j):
            cell_copy(offset_of(j)).start()

    @pl.loop(cuts[0], cuts[1])
    def _(j):
        pack(offset_of(j))
        cell_copy(offset_of(j)).start()

    @pl.loop(cuts[1], n - 1)
    def _(j):
        pack(offset_of(j))

    for load in loads:
        load.wait()

    zero = jnp.zeros((32, 128), jnp.float32)
    lane_sign = jnp.where(lane % 64 < 32, -1.0, 1.0)

    @pl.loop(0, SIDE, unroll=2)
    def _(a):
        c, s = ph_x[0, a], ph_x[1, a]
        for b in range(SIDE):
            cb, sb = ph_y[0, b : b + 1, :], ph_y[1, b : b + 1, :]
            pc[a * 8 + b] = c * cb - s * sb
            ps[a * 8 + b] = (s * cb + c * sb) * lane_sign

    pc[CELLS] = zero
    ps[CELLS] = zero

    lxt_pair = lxt[0], lxt[1]
    for g in range(2):
        vv[g] = dot3(lxt_pair, halves(mask[256 * g : 256 * g + 256, :]))
    for g in range(2):
        for c in range(2):
            cols = slice(256 * c, 256 * c + 256)
            left = jnp.concatenate([vv[g, 0:256, cols], vv[g, 256:512, cols]], axis=1)
            plane[256 * g : 256 * g + 256, cols] = dot3(halves(left), (by[0], by[1]), ((1,), (1,)))
    to_tiles(plane)

    top[n] = zero
    bot[0] = zero

    @pl.loop(0, n, unroll=4)
    def _(t):
        sums = [zero] * 6
        for r in range(cap):
            s = t * cap + r
            x = tiles[ix[0, s]]
            p = ix[1, s]
            u, w = x * pc[p], x * ps[p]
            wt = jnp.where(p < 8, 1.0, 0.0)
            wb = jnp.where(p >= 56, 1.0, 0.0)
            sums = [
                sums[0] + u, sums[1] + w, sums[2] + wt * u, sums[3] + wt * w,
                sums[4] + wb * u, sums[5] + wb * w,
            ]
        wide[t] = sums[0] + swap(sums[1])
        top[t] = sums[2] + swap(sums[3])
        bot[t + 1] = sums[4] + swap(sums[5])

    def own_row(a, carry):
        u, w = carry
        for b in range(8):
            x = tiles[a * 8 + b]
            u, w = u + x * pc[a * 8 + b], w + x * ps[a * 8 + b]
        return u, w

    u0, w0 = own_row(0, (zero, zero))
    u7, w7 = own_row(7, (zero, zero))
    u, w = lax.fori_loop(1, 7, own_row, (u0 + u7, w0 + w7), unroll=2)
    wide[me] += u + swap(w)
    top[me] += u0 + swap(w0)
    bot[me + 1] += u7 + swap(w7)

    @pl.loop(0, n, unroll=8)
    def _(t):
        tp = jnp.where(low, top[t + 1], 0.0)
        bt = jnp.where(low, 0.0, bot[t])
        tp = tp + pltpu.roll(tp, 64, 1)
        bt = bt + pltpu.roll(bt, 64, 1)
        x = wide[t]
        x = x + pltpu.roll(x, 64, 1)
        both = (tp + bt) * sh[0] + pltpu.roll((bt - tp), 32, 1) * sh[1]
        part[place(t)] = compact(x + both)

    def spec_copy(k):
        to = jnp.bitwise_xor(chip, k)
        return pltpu.make_async_remote_copy(
            src_ref=part.at[place(2 * to + core)], dst_ref=spec_in.at[chip],
            send_sem=spec_send.at[k], recv_sem=spec_recv.at[k],
            device_id={"tile": 2 * to + core}, device_id_type=pl.DeviceIdType.MESH,
        )

    other = pl.ds((1 - core) * chips, chips)
    share = pltpu.make_async_remote_copy(
        src_ref=part.at[other], dst_ref=shared, send_sem=spec_send.at[0], recv_sem=spec_recv.at[0],
        device_id={"tile": jnp.bitwise_xor(me, 1)}, device_id_type=pl.DeviceIdType.MESH,
    )
    share.start()
    share.wait_recv()
    own_part = pl.ds(core * chips, chips)
    part[own_part] = part[own_part] + shared[...]

    @pl.loop(1, chips)
    def _(k):
        spec_copy(k).start()

    start_cells(1)

    def flag_copy(k):
        to = lax.rem(slab + k, slabs)
        return pltpu.make_async_remote_copy(
            src_ref=flag_mine, dst_ref=flag_in.at[k],
            send_sem=flag_send.at[k], recv_sem=flag_recv.at[k],
            device_id={"slab": to}, device_id_type=pl.DeviceIdType.MESH,
        )

    def hop_copy(k, source):
        to = peer_of(k)
        return pltpu.make_async_remote_copy(
            src_ref=out2.at[to], dst_ref=in2.at[source],
            send_sem=hop_send.at[k], recv_sem=hop_recv.at[source],
            device_id={"tile": to}, device_id_type=pl.DeviceIdType.MESH,
        )

    spec_in[chip] = part[place(me)]

    for k in range(KERNELS):
        rows = slice(32 * k, 32 * k + 32)
        re, im = kraw[64 * k : 64 * k + 32, :], kraw[64 * k + 32 : 64 * k + 64, :]
        kr[rows, :] = jnp.concatenate([re] * 4, axis=1)
        ki[rows, :] = jnp.concatenate([-im, im] * 2, axis=1)

    @pl.loop(1, chips)
    def _(k):
        spec_copy(k).wait_recv()

    start_cells(2)
    spec = expand(sum((spec_in[t] for t in range(1, chips)), spec_in[0]))

    spec_s = pltpu.roll(spec, 32, 1)
    for k in range(KERNELS):
        rows = slice(32 * k, 32 * k + 32)
        stack[rows, :] = spec * kr[rows, :] + spec_s * ki[rows, :]
    fields_y = dot(stack[...], yt[...])
    sign = jnp.where(low, -1.0, 1.0)
    for k in range(KERNELS):
        part_k = fields_y[32 * k : 32 * k + 32]
        rhs[0:32, 128 * k : 128 * k + 128] = part_k
        rhs[32:64, 128 * k : 128 * k + 128] = pltpu.roll(part_k, 64, 1) * sign
    fields = dot(x1[...], rhs[...])
    inten = jnp.zeros((64, 128), jnp.float32)
    for k in range(KERNELS):
        e = fields[:, 128 * k : 128 * k + 128]
        inten = inten + wts[k] * (e * e)
    blurred = dot(ux[...], dot(inten, uyt[...]))
    d = dose[0]
    resist = jax.nn.sigmoid(4.0 * (d * blurred - 1.0))
    slope = 2.0 * (resist - target[...]) * (4.0 * d) * resist * (1.0 - resist)
    grad_i = dot3((uxt[0], uxt[1]), halves(dot3(halves(slope), (uy2[0], uy2[1]))))
    lane2 = lax.broadcasted_iota(jnp.int32, (64, 128), 1)
    sign2 = jnp.where(lane2 < 64, 1.0, -1.0)
    for k in range(KERNELS):
        ge = (2.0 * wts[k]) * grad_i * fields[:, 128 * k : 128 * k + 128]
        rhs2[0:64, 128 * k : 128 * k + 128] = ge
        rhs2[64:128, 128 * k : 128 * k + 128] = pltpu.roll(ge, 64, 1) * sign2
    grad_y = dot(x2[...], rhs2[...])
    for k in range(KERNELS):
        stack[32 * k : 32 * k + 32, :] = grad_y[:, 128 * k : 128 * k + 128]
    grad_a = dot(stack[...], y2[...])
    acc = zero
    for k in range(KERNELS):
        rows = slice(32 * k, 32 * k + 32)
        ga = grad_a[rows]
        acc = acc + kr[rows, :] * ga - ki[rows, :] * pltpu.roll(ga, 32, 1)
    acc_all[place(me)] = compact(acc)

    def acc_copy(k):
        to = jnp.bitwise_xor(low_chip, k)
        return pltpu.make_async_remote_copy(
            src_ref=acc_all.at[pl.ds(mine, 2)], dst_ref=acc_all.at[pl.ds(mine, 2)],
            send_sem=acc_send.at[k], recv_sem=acc_recv.at[k],
            device_id={"tile": 2 * (to + half * high_chip) + core}, device_id_type=pl.DeviceIdType.MESH,
        )

    acc_cross = pltpu.make_async_remote_copy(
        src_ref=acc_all.at[place(me)], dst_ref=acc_all.at[place(me)],
        send_sem=acc_send.at[half], recv_sem=acc_recv.at[half],
        device_id={"tile": across}, device_id_type=pl.DeviceIdType.MESH,
    )
    acc_cross.start()
    start_cells(3)
    acc_cross.wait_recv()

    @pl.loop(1, half)
    def _(k):
        acc_copy(k).start()

    start_cells(4)

    @pl.when(is_relay)
    def _():
        meta_in[me] = meta_out[...]
        in_ov[pl.ds(me * EXTRA, EXTRA)] = out_ov[relay]

        @pl.loop(1, n)
        def _(k):
            for copy in to_relay(0, peer_of(k)):
                copy.wait_recv()

        lines = n // 8
        slot = lax.broadcasted_iota(jnp.int32, (lines, 128), 1) % 16
        start = jnp.zeros((lines, 128), jnp.int32)
        found = jnp.zeros((lines, 128), jnp.int32)
        most = jnp.zeros((lines, 128), jnp.int32)
        for i in range(n):
            count, offset = meta_in[i, 0:lines], meta_in[i, lines : 2 * lines]
            rel = slot - start
            found = jnp.where((rel >= 0) & (rel < count), i * EXTRA + offset + rel, found)
            start = start + count
            most = jnp.maximum(most, count + offset)
        route_v[...] = jnp.zeros((8, 128), jnp.int32)
        route_v[0:lines] = jnp.clip(found, 0, n * EXTRA - 1)
        over = jnp.broadcast_to(jnp.max(jnp.where(most > EXTRA, 1.0, 0.0)), (8, 128))
        route_copy = pltpu.make_async_copy(route_v, route, tab_sem.at[2])
        route_copy.start()
        flag_mine[...] = over

        @pl.when(me == first)
        def _():
            for k in range(1, slabs):
                flag_copy(k).start()

        route_copy.wait()

        @pl.loop(0, n)
        def _(d):
            for m in range(EXTRA):
                out2[d, m] = in_ov[route[d // 8, lax.rem(d, 8) * 16 + m]]

        flag_in[0] = over

        @pl.when(me == first)
        def _():
            for k in range(1, slabs):
                flag_copy(k).wait()
                flag_in[0] = jnp.maximum(flag_in[0], flag_in[k])

        @pl.loop(0, n)
        def _(d):
            out2[d, EXTRA] = flag_in[0]

        @pl.loop(1, n)
        def _(k):
            hop_copy(k, relay).start()

        in2[relay] = out2[me]

    @pl.loop(1, half)
    def _(k):
        acc_copy(k).wait_recv()

    give = pltpu.make_async_remote_copy(
        src_ref=acc_all.at[own_part], dst_ref=acc_all.at[own_part],
        send_sem=acc_send.at[0], recv_sem=acc_recv.at[0],
        device_id={"tile": jnp.bitwise_xor(me, 1)}, device_id_type=pl.DeviceIdType.MESH,
    )
    give.start()
    give.wait_recv()


    @pl.loop(0, n, unroll=8)
    def _(t):
        mid = expand(acc_all[place(t)])
        before = expand(acc_all[place(jnp.maximum(t - 1, 0))]) * jnp.where(t > 0, 1.0, 0.0)
        after = expand(acc_all[place(jnp.minimum(t + 1, n - 1))]) * jnp.where(t < n - 1, 1.0, 0.0)
        first = mid + before * sh[0] + pltpu.roll(before, 32, 1) * sh[1]
        last = mid + after * sh[0] - pltpu.roll(after, 32, 1) * sh[1]
        mid_s, first_s, last_s = (pltpu.roll(v, 32, 1) for v in (mid, first, last))
        acc2[t * 3] = jnp.where(low, first, mid)
        acc2[t * 3 + 1] = mid
        acc2[t * 3 + 2] = jnp.where(low, mid, last)
        acc2s[t * 3] = jnp.where(low, first_s, mid_s)
        acc2s[t * 3 + 1] = mid_s
        acc2s[t * 3 + 2] = jnp.where(low, mid_s, last_s)

    @pl.loop(0, SIDE, unroll=2)
    def _(a):
        r = pl.multiple_of(a * 64, 64)
        own = me * 3 + jnp.where(a == 0, 0, jnp.where(a == SIDE - 1, 2, 1))
        own_x, own_s = acc2[own], acc2s[own]
        for b in range(4):
            pieces = []
            for i in range(2):
                c = a * 8 + 2 * b + i
                g, p = ix[2, CELLS + c], ix[3, c]
                pieces.append(own_x * pc[c] + own_s * ps[c] + acc2[g] * pc[p] + acc2s[g] * ps[p])
            h0, h1 = pair(*pieces)
            plane[pl.ds(r, 32), 128 * b : 128 * b + 128] = h0
            plane[pl.ds(r + 32, 32), 128 * b : 128 * b + 128] = h1

    for c in range(2):
        for g in range(2):
            v = dot3(halves(plane[256 * g : 256 * g + 256, 256 * c : 256 * c + 256]), (by[0], by[1]))
            vv[g, 0:256, 256 * c : 256 * c + 256] = v[:, 0:256]
            vv[g, 256:512, 256 * c : 256 * c + 256] = v[:, 256:512]
    for g in range(2):
        grad_out[256 * g : 256 * g + 256, :] = dot3((lx[0], lx[1]), halves(vv[g]))

    @pl.loop(0, SIDE)
    def _(a):
        r = pl.multiple_of(a * 64, 64)
        for b in range(4):
            for h in range(2):
                where = (pl.ds(r + 32 * h, 32), slice(128 * b, 128 * b + 128))
                upd_out[where] = 0.5 * mask[where] - 0.1 * grad_out[where]

    @pl.loop(1, n)
    def _(k):
        cell_copy(k).wait_send()

    @pl.loop(1, chips)
    def _(k):
        spec_copy(k).wait_send()

    @pl.loop(1, half)
    def _(k):
        acc_copy(k).wait_send()

    acc_cross.wait_send()

    share.wait_send()
    give.wait_send()

    for q in range(RELAYS):
        @pl.when(me != first + 2 * q)
        def _():
            for copy in to_relay(q, me):
                copy.wait_send()

    @pl.when(is_relay)
    def _():
        @pl.loop(1, n)
        def _(k):
            hop_copy(k, relay).wait_send()

    @pl.loop(1, n)
    def _(k):
        cell_copy(k).wait_recv()

    for q in range(RELAYS):
        @pl.when(me != first + 2 * q)
        def _():
            hop_copy(1, q).wait_recv()

    flag_out[0] = in2[0, EXTRA][0, 0]
    for m in range(EXTRA):
        in_cells[n * direct + m] = jnp.concatenate([in2[q, m] for q in range(RELAYS)], axis=0)

    @pl.loop(0, SIDE, unroll=2)
    def _(a):
        r = pl.multiple_of(a * 64, 64)
        for b in range(4):
            c = a * 8 + 2 * b
            both = pair(in_cells[ix[2, c]],
                          in_cells[ix[2, c + 1]])
            for h in range(2):
                where = (pl.ds(r + 32 * h, 32), slice(128 * b, 128 * b + 128))
                upd_out[where] = upd_out[where] + 0.5 * both[h]


def full_body(n, cap, tab, mask_hbm, both_out, mask, ix, tiles, out_cells, in_cells, tab_sem, cell_send, cell_recv):
    me = lax.axis_index("tile")
    low = lax.broadcasted_iota(jnp.int32, (32, 128), 1) < 64

    def pair(x, y):
        rx, ry = pltpu.roll(x, 64, 1), pltpu.roll(y, 64, 1)
        return jnp.where(low, x, ry), jnp.where(low, rx, y)

    barrier = pltpu.get_barrier_semaphore()

    @pl.loop(1, n)
    def _(k):
        pl.semaphore_signal(
            barrier, inc=1, device_id={"tile": jnp.bitwise_xor(me, k)}, device_id_type=pl.DeviceIdType.MESH
        )

    index_load = pltpu.make_async_copy(tab.at[pl.ds(0, 8)], ix, tab_sem.at[0])
    index_load.start()
    mask_load = pltpu.make_async_copy(mask_hbm, mask, tab_sem.at[1])
    mask_load.start()
    mask_load.wait()

    @pl.loop(0, SIDE)
    def _(a):
        r = pl.multiple_of(a * 64, 64)
        for b in range(4):
            h0 = mask[pl.ds(r, 32), 128 * b : 128 * b + 128]
            h1 = mask[pl.ds(r + 32, 32), 128 * b : 128 * b + 128]
            tiles[a * 8 + 2 * b], tiles[a * 8 + 2 * b + 1] = pair(h0, h1)

    index_load.wait()

    @pl.loop(0, n)
    def _(to):
        for r in range(cap):
            out_cells[to, r] = tiles[ix[0, to * cap + r]]

    in_cells[pl.ds(me * cap, cap)] = out_cells[me]
    pl.semaphore_wait(barrier, n - 1)

    def cell_copy(k):
        to = jnp.bitwise_xor(me, k)
        return pltpu.make_async_remote_copy(
            src_ref=out_cells.at[to], dst_ref=in_cells.at[pl.ds(me * cap, cap)],
            send_sem=cell_send.at[k], recv_sem=cell_recv.at[k],
            device_id={"tile": to}, device_id_type=pl.DeviceIdType.MESH,
        )

    @pl.loop(1, n)
    def _(k):
        cell_copy(k).start()

    @pl.loop(1, n)
    def _(k):
        cell_copy(k).wait()

    @pl.loop(0, SIDE)
    def _(a):
        r = pl.multiple_of(a * 64, 64)
        for b in range(4):
            c = a * 8 + 2 * b
            halves_of = pair(in_cells[ix[1, c]], in_cells[ix[1, c + 1]])
            for h in range(2):
                where = (pl.ds(r + 32 * h, 32), slice(128 * b, 128 * b + 128))
                both_out[where] = mask[where] + halves_of[h]


def full_exchange(n, cap, partner, mask):
    owner = partner // CELLS
    pos = partner % CELLS
    ids = jnp.arange(CELLS, dtype=jnp.int32)
    same = owner[:, None] == owner[None, :]
    send_rank = jnp.sum((same & (pos[None, :] < pos[:, None])).astype(jnp.int32), axis=1)
    recv_rank = jnp.sum((same & (ids[None, :] < ids[:, None])).astype(jnp.int32), axis=1)
    send_slot = owner * cap + send_rank
    recv_slot = owner * cap + recv_rank
    hit = (jnp.arange(n * cap, dtype=jnp.int32)[:, None] == send_slot[None, :]).astype(jnp.int32)
    slot_cell = jnp.sum(hit * ids[None, :], axis=1)
    tab = jnp.concatenate([slot_cell, recv_slot, recv_slot, jnp.zeros((6 * 128,), jnp.int32)]).reshape(8, 128)
    f32 = jnp.float32
    dma = pltpu.SemaphoreType.DMA((n,))
    vmem = pl.BlockSpec(memory_space=pltpu.VMEM)
    return pl.pallas_call(
        functools.partial(full_body, n, cap),
        out_shape=jax.ShapeDtypeStruct((TILE, TILE), f32),
        in_specs=[pl.BlockSpec(memory_space=pl.ANY), pl.BlockSpec(memory_space=pltpu.HBM)],
        out_specs=vmem,
        scratch_shapes=[
            pltpu.VMEM((TILE, TILE), f32),
            pltpu.SMEM((8, 128), jnp.int32),
            pltpu.VMEM((CELLS, 32, 128), f32),
            pltpu.VMEM((n, cap, 32, 128), f32),
            pltpu.VMEM((n * cap, 32, 128), f32),
            pltpu.SemaphoreType.DMA((2,)),
            dma, dma,
        ],
        compiler_params=pltpu.CompilerParams(
            collective_id=1, has_side_effects=True, vmem_limit_bytes=32 * 1024 * 1024
        ),
    )(tab, mask)


def local(consts, mask, target, partner, kernels, socs_weights, dose):
    n = lax.axis_size("tile")
    cap, direct = 2 * CELLS // n, CELLS // n
    meta_lines = (2 * n // 8 + 7) // 8 * 8
    raw = kernels.reshape(2 * KERNELS * BAND, BAND)
    f32 = jnp.float32
    vmem = pl.BlockSpec(memory_space=pltpu.VMEM)
    hbm = pl.BlockSpec(memory_space=pltpu.HBM)
    arrays = [mask, target, raw, *consts]
    smem = pl.BlockSpec(memory_space=pltpu.SMEM)
    dma, few = pltpu.SemaphoreType.DMA((n,)), pltpu.SemaphoreType.DMA((RELAYS,))
    flags = pltpu.SemaphoreType.DMA((lax.axis_size("slab"),))
    twice, both, flag = pl.pallas_call(
        functools.partial(body, n, cap, len(arrays)),
        out_shape=(jax.ShapeDtypeStruct((TILE, TILE), f32),) * 2 + (jax.ShapeDtypeStruct((1,), f32),),
        in_specs=[smem] * 2 + [hbm] + [hbm] * len(arrays),
        out_specs=(vmem, vmem, smem),
        scratch_shapes=[pltpu.VMEM(x.shape, x.dtype) for x in arrays] + [
            pltpu.SemaphoreType.DMA((len(arrays),)),
            pltpu.VMEM((CELLS + 1, 32, 128), f32),
            pltpu.VMEM((CELLS + 1, 32, 128), f32),
            pltpu.VMEM((n, direct, 32, 128), f32),
            pltpu.VMEM((n * direct + EXTRA, 32, 128), f32),
            pltpu.VMEM((CELLS, 32, 128), f32),
            pltpu.VMEM((TILE, TILE), f32),
            pltpu.VMEM((2, 512, 512), f32),
            pltpu.VMEM((n, 32, 128), f32),
            pltpu.VMEM((n, 16, 128), f32),
            pltpu.VMEM((n // 2, 16, 128), f32),
            pltpu.VMEM((n + 1, 32, 128), f32),
            pltpu.VMEM((n + 1, 32, 128), f32),
            pltpu.VMEM((n, 16, 128), f32),
            pltpu.VMEM((n, 16, 128), f32),
            pltpu.VMEM((3 * n, 32, 128), f32),
            pltpu.VMEM((3 * n, 32, 128), f32),
            pltpu.VMEM((64, 768), f32),
            pltpu.VMEM((128, 768), f32),
            pltpu.VMEM((192, 128), f32),
            pltpu.VMEM((192, 128), f32),
            pltpu.VMEM((192, 128), f32),
            pltpu.VMEM((1, CELLS), jnp.int32),
            pltpu.VMEM((8, 128), jnp.int32),
            pltpu.SMEM((8, 128), jnp.int32),
            pltpu.SemaphoreType.DMA((3,)),
            pltpu.SemaphoreType.DMA((4,)),
            pltpu.VMEM((RELAYS, EXTRA, 8, 128), f32),
            pltpu.VMEM((n * EXTRA, 8, 128), f32),
            pltpu.VMEM((n, EXTRA + 1, 8, 128), f32),
            pltpu.VMEM((RELAYS, EXTRA + 1, 8, 128), f32),
            pltpu.VMEM((meta_lines, 128), jnp.int32),
            pltpu.VMEM((n, meta_lines, 128), jnp.int32),
            pltpu.VMEM((8, 128), jnp.int32),
            pltpu.SMEM((8, 128), jnp.int32),
            pltpu.VMEM((8, 128), f32),
            pltpu.VMEM((lax.axis_size("slab"), 8, 128), f32),
            few, dma, few, dma, dma, few, flags, flags,
            dma, dma, dma, dma, dma, dma,
        ],
        compiler_params=pltpu.CompilerParams(
            collective_id=0, has_side_effects=True, vmem_limit_bytes=VMEM_LIMIT
        ),
    )(socs_weights, dose, partner.reshape(1, CELLS), *arrays)
    def finish(p, m, g, u):
        return write_out(g, u)

    def redo(p, m, g, u):
        return write_out(g, 0.5 * full_exchange(n, cap, p, m) - 0.1 * g)

    return lax.cond(flag[0] > 0.5, redo, finish, partner, mask, twice, both)


def write_body(parts, g, u, g_out, u_out, sem):
    rows = TILE // parts
    copies = []
    for c in range(parts):
        where = pl.ds(rows * c, rows)
        for i, (src, dst) in enumerate(((g, g_out), (u, u_out))):
            copies.append(pltpu.make_async_copy(src.at[where], dst.at[where], sem.at[i, c]))
    for copy in copies:
        copy.start()
    for copy in copies:
        copy.wait()


def write_out(g, u):
    parts = 4
    vmem = pl.BlockSpec(memory_space=pltpu.VMEM)
    hbm = pl.BlockSpec(memory_space=pltpu.HBM)
    return tuple(pl.pallas_call(
        functools.partial(write_body, parts),
        out_shape=(jax.ShapeDtypeStruct((TILE, TILE), jnp.float32),) * 2,
        in_specs=[vmem, vmem],
        out_specs=(hbm, hbm),
        scratch_shapes=[pltpu.SemaphoreType.DMA((2, parts))],
        compiler_params=pltpu.CompilerParams(vmem_limit_bytes=4 * 1024 * 1024),
    )(g, u))


def solution(mesh):
    consts = tables()

    def run(mask, target, partner, kernels, socs_weights, dose):
        return local([jnp.asarray(t) for t in consts], mask, target, partner, kernels, socs_weights, dose)

    return jax.shard_map(
        run,
        mesh=mesh,
        in_specs=(
            P(("slab", "tile"), None),
            P(("slab", "tile"), None),
            P(("slab", "tile")),
            P(),
            P(),
            P(),
        ),
        out_specs=(P(("slab", "tile"), None), P(("slab", "tile"), None)),
        check_vma=False,
    )
```
